32 devices in a mesh: shard: 4 (over y, x), rep: 8 (over z, core).
Axes of the slice: x: 2, y: 2, z: 4, core: 2. Of those that a mesh axis runs over, the one named last changes fastest.
Arguments:
- tokens: bfloat16 [8, 1032, 1024], P('rep', 'shard'), may hold values from -6 to 6
- cotangent: bfloat16 [8, 1032, 1024], P('rep', 'shard'), may hold values from -6 to 6
- slot_live: int32 [8], P('rep'), may hold values from 0 to 1, as said below
- w_qkv: bfloat16 [1, 1024, 3072], P(None, 'shard'), as said below
- w_out: bfloat16 [1, 1024, 1024], P(None, 'shard'), may hold values from -0.75 to 0.75
- w_fc1: bfloat16 [1, 1024, 4096], P(None, 'shard'), may hold values from -0.1875 to 0.1875
- w_fc2: bfloat16 [1, 4096, 1024], P(None, 'shard'), may hold values from -0.09375 to 0.09375
- norm_gain: bfloat16 [1, 2, 1024], P(None, None, 'shard'), may hold values from 0.5 to 1.5
- norm_bias: bfloat16 [1, 2, 1024], P(None, None, 'shard'), may hold values from -1.5 to 1.5
- layer_scale: bfloat16 [1, 2, 1024], P(None, None, 'shard'), may hold values from 0.29882812 to 1.1953125
- qv_bias: bfloat16 [1, 2, 1024], P(None, None, 'shard'), may hold values from -1.5 to 1.5
- proj_bias: bfloat16 [1, 2, 1024], P(None, None, 'shard'), may hold values from -1.5 to 1.5
- fc1_bias: bfloat16 [1, 4096], P(None, 'shard'), may hold values from -1.5 to 1.5
Outputs:
- output: bfloat16 [8, 1032, 1024], P('rep', 'shard')
- input_grad: float32 [8, 1032, 1024], P('rep', 'shard')
- grad_w_qkv: float32 [1, 1024, 3072], P(None, 'shard')
- grad_w_out: float32 [1, 1024, 1024], P(None, 'shard')
- grad_w_fc1: float32 [1, 1024, 4096], P(None, 'shard')
- grad_w_fc2: float32 [1, 4096, 1024], P(None, 'shard')
- grad_norm_gain: float32 [1, 2, 1024], P(None, None, 'shard')
- grad_norm_bias: float32 [1, 2, 1024], P(None, None, 'shard')
- grad_layer_scale: float32 [1, 2, 1024], P(None, None, 'shard')
- grad_qv_bias: float32 [1, 2, 1024], P(None, None, 'shard')
- grad_proj_bias: float32 [1, 2, 1024], P(None, None, 'shard')
- grad_fc1_bias: float32 [1, 4096], P(None, 'shard')
The draws below stay inside these ranges and needn't reach their ends.
Inputs may be any that keep to these rules, and one draw needn't show every extreme that they name: `slot_live`: entries i * 1 to (i + 1) - 1 are the slots of replica group i; in every draw one group holds 1 images and another holds none. `w_qkv`: columns are the query, key and value projections in that order, heads of 64 columns in order within each.
All inputs are finite; a program needn't handle non-finite values.
Results may differ from the reference program's by a relative error of at most 0.0079.
Values may be sent and summed in bfloat16 or wider, within the bound.
A program may use at most 192 MiB of HBM per device.

```python
import math
import jax
import jax.numpy as jnp
from jax import lax

D = 1024
HEADS = 16
FF = 4096
LAYERS = 1
LEN = 1025
LPAD = 1032
SLOTS = 1
IMAGES = 8
N_REP = 8


def draw_slot_live(key, part):
    pick_key, full_key, empty_key = jax.random.split(key, 3)
    holding = (jax.random.randint(pick_key, (N_REP, SLOTS), 0, 3) > 0).astype(jnp.int32)
    full_group = jax.random.randint(full_key, (), 0, N_REP)
    empty_group = (full_group + 1 + jax.random.randint(empty_key, (), 0, N_REP - 1)) % N_REP
    groups = jnp.arange(N_REP)[:, None]
    holding = jnp.where(groups == full_group, 1, jnp.where(groups == empty_group, 0, holding))
    return holding.reshape(N_REP * SLOTS).astype(jnp.int32)


def draw_w_qkv(key, part):
    base_key = jax.random.fold_in(key, 0)
    standard = jax.random.normal(base_key, (LAYERS, D, 3 * D), jnp.float32) * D ** (-0.5)
    return standard.astype(jnp.bfloat16)


def shard_levels(stream_key, shape, cuts, smallest, largest):
    loudness, own = 1.0, jax.random.fold_in(stream_key, 6)
    for position, blocks in cuts:
        draws = jnp.exp(jax.random.uniform(jax.random.fold_in(own, position), (blocks,), jnp.float32, smallest / len(cuts), largest / len(cuts)))
        loudness = loudness * jnp.repeat(draws, shape[position] // blocks).reshape([-1 if axis == position else 1 for axis in range(len(shape))])
    return loudness


def gaussian(stream_key, extent, scale, reach, cuts=(), kind=jnp.bfloat16):
    array = jax.random.normal(stream_key, extent, jnp.float32) * scale
    if len(cuts) > 0:
        array = shard_levels(stream_key, extent, cuts, -0.22, 0.18) * array
    return jnp.clip(array, min=-reach, max=reach).astype(kind)


def setup_inputs(seed: int = 0) -> dict:
    key_list = jax.random.split(jax.random.key(seed), 14)
    tokens = gaussian(key_list[0], (IMAGES, LPAD, D), 1.0, 6.0, ((0, 8), (1, 4)))
    cotangent = gaussian(key_list[1], (IMAGES, LPAD, D), 1.0, 6.0, ((0, 8), (1, 4)))
    slot_live = draw_slot_live(jax.random.fold_in(key_list[13], 71), 0)
    w_qkv = draw_w_qkv(jax.random.fold_in(key_list[13], 71), 0)
    w_out = gaussian(key_list[4], (LAYERS, D, D), (D // 16) ** -0.5, 0.75, ((1, 4),))
    w_fc1 = gaussian(key_list[5], (LAYERS, D, FF), D ** -0.5, 0.1875, ((1, 4),))
    w_fc2 = gaussian(key_list[6], (LAYERS, FF, D), FF ** -0.5, 0.09375, ((1, 4),))
    norm_gain = jnp.clip(1.0 + 0.1 * jax.random.normal(key_list[7], (LAYERS, 2, D), jnp.float32), 0.5, 1.5).astype(jnp.bfloat16)
    norm_bias = gaussian(key_list[8], (LAYERS, 2, D), 0.3, 1.5, ((2, 4),))
    layer_scale = jnp.clip(jnp.exp(math.log(1.1953125) - 1.3862944 * jax.random.uniform(key_list[9], (LAYERS, 2, D), jnp.float32) ** shard_levels(key_list[9], (LAYERS, 2, D), ((2, 4),), -0.2, 0.2)), 0.29882812, 1.1953125).astype(jnp.bfloat16)
    qv_bias = gaussian(key_list[10], (LAYERS, 2, D), 0.3, 1.5, ((2, 4),))
    proj_bias = gaussian(key_list[11], (LAYERS, 2, D), 0.3, 1.5, ((2, 4),))
    fc1_bias = gaussian(key_list[12], (LAYERS, FF), 0.3, 1.5, ((1, 4),))
    return {"tokens": tokens, "cotangent": cotangent, "slot_live": slot_live, "w_qkv": w_qkv, "w_out": w_out, "w_fc1": w_fc1, "w_fc2": w_fc2, "norm_gain": norm_gain, "norm_bias": norm_bias, "layer_scale": layer_scale, "qv_bias": qv_bias, "proj_bias": proj_bias, "fc1_bias": fc1_bias}


EPSILON = 1e-06

def norm_forward(hidden, gain, offset):
    center = hidden - lax.optimization_barrier(jnp.mean(hidden, axis=-1, keepdims=True))
    inverse = lax.rsqrt(lax.optimization_barrier(jnp.mean(center * center, axis=-1, keepdims=True)) + EPSILON)
    normed = center * inverse
    return (normed * gain + offset, normed, inverse)

def norm_backward(incoming, normed, inverse, gain):
    scaled = incoming * gain
    return inverse * (scaled - lax.optimization_barrier(jnp.mean(scaled, axis=-1, keepdims=True)) - normed * lax.optimization_barrier(jnp.mean(scaled * normed, axis=-1, keepdims=True)))

def gelu_pair(values):
    cumulative = 0.5 * (1.0 + jax.scipy.special.erf(values * 0.7071067811865476))
    slope = cumulative + values * jnp.exp(-0.5 * values * values) * 0.3989422804014327
    return (values * cumulative, slope)

def plain_dot(left, right):
    return jnp.dot(left, right, preferred_element_type=jnp.float32)

def row_dot(left, right):
    return lax.dot_general(left, right, (((0,), (0,)), ((), ())), preferred_element_type=jnp.float32)

def back_dot(left, right):
    return lax.dot_general(left, right, (((1,), (1,)), ((), ())), preferred_element_type=jnp.float32)

def score_block(queries, keys, key_live):
    factor = 1.0 / math.sqrt(queries.shape[-1])
    scores = jnp.einsum('sqhe,skhe->shqk', queries.astype(jnp.float32), keys.astype(jnp.float32)) * factor
    return jnp.where(key_live[None, None, None, :], scores, -1e+30)

def attend_forward(queries, keys, values, key_live):
    scores = score_block(queries, keys, key_live)
    row_max = lax.optimization_barrier(jnp.max(scores, axis=-1, keepdims=True))
    logsum = row_max + jnp.log(lax.optimization_barrier(jnp.sum(jnp.exp(scores - row_max), axis=-1, keepdims=True)))
    probs = jnp.exp(scores - logsum).astype(jnp.bfloat16)
    mixed = jnp.einsum('shqk,skhe->sqhe', probs.astype(jnp.float32), values.astype(jnp.float32))
    return (mixed.astype(jnp.bfloat16), logsum)

def attend_backward(queries, keys, values, logsum, mixed_grad, key_live):
    factor = 1.0 / math.sqrt(queries.shape[-1])
    weights = jnp.exp(score_block(queries, keys, key_live) - logsum)
    probs = weights.astype(jnp.bfloat16)
    grad_in = mixed_grad.astype(jnp.float32)
    prob_grad = jnp.einsum('sqhe,skhe->shqk', grad_in, values.astype(jnp.float32))
    row_delta = lax.optimization_barrier(jnp.sum(weights * prob_grad, axis=-1, keepdims=True))
    score_grad = (weights * (prob_grad - row_delta) * factor).astype(jnp.bfloat16).astype(jnp.float32)
    query_grad = jnp.einsum('shqk,skhe->sqhe', score_grad, keys.astype(jnp.float32))
    key_grad = jnp.einsum('shqk,sqhe->skhe', score_grad, queries.astype(jnp.float32))
    value_grad = jnp.einsum('shqk,sqhe->skhe', probs.astype(jnp.float32), grad_in)
    return (query_grad, key_grad, value_grad)

def layer_forward(hidden, params, key_live):
    w_qkv, w_out, w_fc1, w_fc2, gains, offsets, scales, qv_bias, proj_bias, fc1_bias = params
    gains = gains.astype(jnp.float32)
    offsets = offsets.astype(jnp.float32)
    scales = scales.astype(jnp.float32)
    qv_bias = qv_bias.astype(jnp.float32)
    proj_bias = proj_bias.astype(jnp.float32)
    slot_count, seq_len, model_width = hidden.shape
    head_count = HEADS
    head_size = model_width // head_count
    first_norm, normed_one, inverse_one = norm_forward(hidden, gains[0], offsets[0])
    first_rows = first_norm.astype(jnp.bfloat16).reshape(-1, model_width)
    bias_row = jnp.concatenate([qv_bias[0], jnp.zeros_like(qv_bias[0]), qv_bias[1]])
    project = plain_dot(first_rows, w_qkv) + bias_row
    shape_heads = (slot_count, seq_len, head_count, head_size)
    queries = project[:, :model_width].astype(jnp.bfloat16).reshape(shape_heads)
    keys = project[:, model_width:2 * model_width].astype(jnp.bfloat16).reshape(shape_heads)
    values = project[:, 2 * model_width:].astype(jnp.bfloat16).reshape(shape_heads)
    mixed, logsum = attend_forward(queries, keys, values, key_live)
    mixed_rows = mixed.reshape(-1, model_width)
    attn_out = plain_dot(mixed_rows, w_out) + proj_bias[0]
    middle = hidden + scales[0] * attn_out.reshape(hidden.shape)
    second_norm, normed_two, inverse_two = norm_forward(middle, gains[1], offsets[1])
    second_rows = second_norm.astype(jnp.bfloat16).reshape(-1, model_width)
    pre_act = plain_dot(second_rows, w_fc1) + fc1_bias.astype(jnp.float32)
    act_value, act_slope = gelu_pair(pre_act)
    act_rows = act_value.astype(jnp.bfloat16)
    branch = plain_dot(act_rows, w_fc2) + proj_bias[1]
    result = middle + scales[1] * branch.reshape(hidden.shape)
    stored = (normed_one, inverse_one, first_rows, queries, keys, values, mixed_rows, logsum, attn_out, normed_two, inverse_two, second_rows, act_slope, act_rows, branch)
    return (result, stored)

def layer_backward(incoming, params, stored, key_live):
    w_qkv, w_out, w_fc1, w_fc2, gains, offsets, scales, qv_bias, proj_bias, fc1_bias = params
    gains = gains.astype(jnp.float32)
    scales = scales.astype(jnp.float32)
    normed_one, inverse_one, first_rows, queries, keys, values, mixed_rows, logsum, attn_out, normed_two, inverse_two, second_rows, act_slope, act_rows, branch = stored
    model_width = incoming.shape[-1]
    upstream = incoming.reshape(-1, model_width)
    fc2_grad = upstream * scales[1]
    fc2_in = fc2_grad.astype(jnp.bfloat16)
    grad_fc2 = row_dot(act_rows, fc2_in)
    proj_two = lax.optimization_barrier(jnp.sum(fc2_grad, axis=0))
    scale_two = lax.optimization_barrier(jnp.sum(upstream * branch, axis=0))
    pre_grad = back_dot(fc2_in, w_fc2) * act_slope
    pre_in = pre_grad.astype(jnp.bfloat16)
    grad_fc1 = row_dot(second_rows, pre_in)
    grad_fc1_bias = lax.optimization_barrier(jnp.sum(pre_grad, axis=0))
    second_grad = back_dot(pre_in, w_fc1)
    normed_two_rows = normed_two.reshape(-1, model_width)
    gain_two = lax.optimization_barrier(jnp.sum(second_grad * normed_two_rows, axis=0))
    offset_two = lax.optimization_barrier(jnp.sum(second_grad, axis=0))
    middle_grad = upstream + norm_backward(second_grad, normed_two_rows, inverse_two.reshape(-1, 1), gains[1])
    attn_grad = middle_grad * scales[0]
    attn_in = attn_grad.astype(jnp.bfloat16)
    grad_out = row_dot(mixed_rows, attn_in)
    proj_one = lax.optimization_barrier(jnp.sum(attn_grad, axis=0))
    scale_one = lax.optimization_barrier(jnp.sum(middle_grad * attn_out, axis=0))
    mixed_grad = back_dot(attn_in, w_out).astype(jnp.bfloat16).reshape(queries.shape)
    query_grad, key_grad, value_grad = attend_backward(queries, keys, values, logsum, mixed_grad, key_live)
    query_rows = query_grad.reshape(-1, model_width)
    key_rows = key_grad.reshape(-1, model_width)
    value_rows = value_grad.reshape(-1, model_width)
    grad_qv = jnp.stack([lax.optimization_barrier(jnp.sum(query_rows, axis=0)), lax.optimization_barrier(jnp.sum(value_rows, axis=0))])
    joined = jnp.concatenate([query_rows, key_rows, value_rows], axis=1).astype(jnp.bfloat16)
    grad_qkv = row_dot(first_rows, joined)
    first_grad = back_dot(joined, w_qkv)
    normed_one_rows = normed_one.reshape(-1, model_width)
    gain_one = lax.optimization_barrier(jnp.sum(first_grad * normed_one_rows, axis=0))
    offset_one = lax.optimization_barrier(jnp.sum(first_grad, axis=0))
    outgoing = middle_grad + norm_backward(first_grad, normed_one_rows, inverse_one.reshape(-1, 1), gains[0])
    terms = (grad_qkv, grad_out, grad_fc1, grad_fc2, jnp.stack([gain_one, gain_two]), jnp.stack([offset_one, offset_two]), jnp.stack([scale_one, scale_two]), grad_qv, jnp.stack([proj_one, proj_two]), grad_fc1_bias)
    return (outgoing.reshape(incoming.shape), terms)

def reference(tokens, cotangent, slot_live, w_qkv, w_out, w_fc1, w_fc2, norm_gain, norm_bias, layer_scale, qv_bias, proj_bias, fc1_bias):
    layers = w_qkv.shape[0]
    arrays = (w_qkv, w_out, w_fc1, w_fc2, norm_gain, norm_bias, layer_scale, qv_bias, proj_bias, fc1_bias)
    key_live = jnp.arange(LPAD, dtype=jnp.int32) < LEN
    token_groups = tokens.reshape(N_REP, SLOTS, LPAD, D)
    cotan_groups = cotangent.reshape(N_REP, SLOTS, LPAD, D)
    live_groups = slot_live.reshape(N_REP, SLOTS)

    def one_group(totals, pieces):
        group_tokens, group_cotan, group_live = pieces
        hidden = group_tokens.astype(jnp.float32)
        stores = []
        for depth in range(layers):
            params = tuple((member[depth] for member in arrays))
            hidden, stored = layer_forward(hidden, params, key_live)
            stores.append(stored)
        out_block = hidden.astype(jnp.bfloat16)
        valid = ((group_live[:, None] > 0) & key_live[None, :]).astype(jnp.float32)
        upstream = group_cotan.astype(jnp.float32) * valid[:, :, None]
        layer_terms = [None] * layers
        for depth in reversed(range(layers)):
            params = tuple((member[depth] for member in arrays))
            upstream, terms = layer_backward(upstream, params, stores[depth], key_live)
            layer_terms[depth] = terms
        stacked = tuple((jnp.stack([layer_terms[depth][number] for depth in range(layers)]) for number in range(10)))
        totals = tuple((total + extra for total, extra in zip(totals, stacked)))
        return (totals, (out_block, upstream))
    zeros = (jnp.zeros((layers, D, 3 * D), jnp.float32), jnp.zeros((layers, D, D), jnp.float32), jnp.zeros((layers, D, FF), jnp.float32), jnp.zeros((layers, FF, D), jnp.float32), jnp.zeros((layers, 2, D), jnp.float32), jnp.zeros((layers, 2, D), jnp.float32), jnp.zeros((layers, 2, D), jnp.float32), jnp.zeros((layers, 2, D), jnp.float32), jnp.zeros((layers, 2, D), jnp.float32), jnp.zeros((layers, FF), jnp.float32))
    totals, (outputs, grads_in) = lax.scan(one_group, zeros, (token_groups, cotan_groups, live_groups))
    return (outputs.reshape(IMAGES, LPAD, D), grads_in.reshape(IMAGES, LPAD, D), totals[0], totals[1], totals[2], totals[3], totals[4], totals[5], totals[6], totals[7], totals[8], totals[9])
```

```python
import functools
import math

import jax
import jax.numpy as jnp
from jax import lax
from jax.experimental import pallas as pl
from jax.experimental.pallas import tpu as pltpu
from jax.sharding import PartitionSpec as P

HEADS = 16
LEN = 1025
EPSILON = 1e-06
F32 = jnp.float32
BF16 = jnp.bfloat16
MESH = pl.DeviceIdType.MESH
VMEM = pl.BlockSpec(memory_space=pltpu.VMEM)


def norm_parts(hidden):
    center = hidden - jnp.mean(hidden, axis=-1, keepdims=True)
    inverse = lax.rsqrt(jnp.mean(center * center, axis=-1, keepdims=True) + EPSILON)
    return (center * inverse, inverse)


def norm_backward(incoming, normed, inverse, gain):
    scaled = incoming * gain
    return inverse * (
        scaled
        - jnp.mean(scaled, axis=-1, keepdims=True)
        - normed * jnp.mean(scaled * normed, axis=-1, keepdims=True)
    )


def gelu_pair(values):
    cumulative = 0.5 * (1.0 + lax.erf(values * 0.7071067811865476))
    slope = cumulative + values * jnp.exp(-0.5 * values * values) * 0.3989422804014327
    return (values * cumulative, slope)


def plain_dot(left, right):
    return jnp.dot(left, right, preferred_element_type=F32)


def row_dot(left, right):
    return lax.dot_general(left, right, (((0,), (0,)), ((), ())), preferred_element_type=F32)


def back_dot(left, right):
    return lax.dot_general(left, right, (((1,), (1,)), ((), ())), preferred_element_type=F32)


def head_parts(size, width):
    lane = lax.broadcasted_iota(jnp.int32, (1, width), 1)
    return [
        ((lane >= size * number) & (lane < size * (number + 1))) for number in range(width // size)
    ]


def column_sum(values):
    return jnp.sum(values, axis=0, keepdims=True)


def partner(me, step, count):
    other, bit = me, 1
    while bit < count:
        other = other + ((step // bit) % 2) * (1 - 2 * ((me // bit) % 2)) * bit
        bit *= 2
    return other


def spot(index, rows):
    return pl.ds(pl.multiple_of(index * rows, math.gcd(rows, 1024)), rows)


def greet(me, count, others=()):
    barrier = pltpu.get_barrier_semaphore()
    for step in range(1, count):
        pl.semaphore_signal(
            barrier, 1, device_id={"shard": partner(me, step, count)}, device_id_type=MESH
        )
    for other in others:
        pl.semaphore_signal(barrier, 1, device_id={"rep": other}, device_id_type=MESH)
    pl.semaphore_wait(barrier, count - 1 + len(others))


def post(source, target, sems, kind, step, where):
    return pltpu.make_async_remote_copy(
        source,
        target,
        sems[0].at[kind, step],
        sems[1].at[kind, step],
        device_id=where,
        device_id_type=MESH,
    )


def score(queries, keys, live):
    return jnp.where(live, back_dot(queries, keys), -1e30)


def attend_rows(size, here, live, project, mixed, stat):
    owned = mixed.shape[1]
    width = min(max(128, size), owned)
    factor = 1.0 / math.sqrt(size)
    for pair in range(owned // width):
        columns = slice(pair * width, (pair + 1) * width)
        queries = project[here, columns]
        keys = project[:, owned + pair * width : owned + (pair + 1) * width]
        values = project[:, 2 * owned + pair * width : 2 * owned + (pair + 1) * width]
        out = jnp.zeros(queries.shape, F32)
        for number, part in enumerate(head_parts(size, width)):
            own = (jnp.where(part, queries, 0) * factor).astype(BF16)
            scores = score(own, keys, live)
            top = jnp.max(scores, axis=-1, keepdims=True)
            power = jnp.exp(scores - top)
            total = jnp.sum(power, axis=-1, keepdims=True)
            product = plain_dot(power.astype(BF16), values) * (1.0 / total)
            out = jnp.where(part, product, out)
            place = pair * (width // size) + number
            stat[here, place : place + 1] = top + jnp.log(total)
        mixed[here, columns] = out.astype(BF16)


def attend_rows_back(size, here, live, project, mixed, stat, grad, joined, dk, dv, between):
    owned = mixed.shape[1]
    width = min(max(128, size), owned)
    factor = 1.0 / math.sqrt(size)
    for pair in range(owned // width):
        columns = slice(pair * width, (pair + 1) * width)
        queries = project[here, columns]
        keys = project[:, owned + pair * width : owned + (pair + 1) * width]
        values = project[:, 2 * owned + pair * width : 2 * owned + (pair + 1) * width]
        grads = grad[:, columns]
        overlap = grads.astype(F32) * mixed[here, columns].astype(F32)
        turned_q = jnp.transpose(queries.astype(F32) * factor).astype(BF16)
        turned_g = jnp.transpose(grads.astype(F32)).astype(BF16)
        dq = jnp.zeros(queries.shape, F32)
        for number, part in enumerate(head_parts(size, width)):
            place = pair * (width // size) + number
            own_q = (jnp.where(part, queries, 0) * factor).astype(BF16)
            own_g = jnp.where(part, grads, 0).astype(BF16)
            weights = jnp.exp(score(own_q, keys, live) - stat[here, place : place + 1])
            delta = jnp.sum(jnp.where(part, overlap, 0), axis=-1, keepdims=True)
            slope = (weights * (back_dot(own_g, values) - delta)).astype(BF16)
            span = slice(place * size, (place + 1) * size)
            inner = slice(number * size, (number + 1) * size)
            dk[span, :] += plain_dot(turned_q[inner], slope)
            dv[span, :] += plain_dot(turned_g[inner], weights.astype(BF16))
            dq = jnp.where(part, plain_dot(slope, keys), dq)
        joined[here, columns] = (dq * factor).astype(BF16)
        between(pair)


class Gather:
    def __init__(self, array, rows, me, count, sems, kind):
        self.array, self.rows, self.me, self.count = array, rows, me, count
        self.sems, self.kind, self.square = sems, kind, count == 4
        self.steps = (1, 2) if self.square else tuple(range(1, count))
        self.half = array.shape[1] // 2

    def direct(self, owner, step):
        block = self.array.at[spot(owner, self.rows)]
        where = {"shard": partner(self.me, step, self.count)}
        return post(block, block, self.sems, self.kind, step, where)

    def relay(self, owner, step):
        columns = pl.ds((step - 1) * self.half, self.half)
        block = self.array.at[spot(owner, self.rows), columns]
        where = {"shard": partner(self.me, 3 - step, self.count)}
        return post(block, block, self.sems, self.kind + 1, step, where)

    def start(self):
        for step in self.steps:
            self.direct(self.me, step).start()

    def arrive(self, step):
        if not self.square:

            @pl.when(step > 0)
            def _():
                self.direct(partner(self.me, step, self.count), step).wait_recv()

            return

        @pl.when(step == 1)
        def _():
            for near in (1, 2):
                owner = partner(self.me, near, 4)
                self.direct(owner, near).wait_recv()
                self.relay(owner, near).start()

        @pl.when(step == 3)
        def _():
            for near in (1, 2):
                self.relay(partner(self.me, 3, 4), near).wait_recv()

    def finish(self):
        for step in self.steps:
            self.direct(self.me, step).wait_send()
            if self.square:
                self.relay(partner(self.me, step, 4), step).wait_send()


class Scatter:
    def __init__(self, part, landed, via, me, count, sems, kind):
        self.part, self.landed, self.via, self.me, self.count = part, landed, via, me, count
        self.sems, self.kind, self.square = sems, kind, count == 4
        self.steps = (1, 2) if self.square else tuple(range(1, count))
        self.half = part.shape[2] // 2

    def direct(self, step, side=0):
        source, target = self.part.at[step - 1], self.landed.at[step - 1]
        if self.square:
            columns = pl.ds(side * self.half, self.half)
            source, target = source.at[:, columns], target.at[:, columns]
        where = {"shard": partner(self.me, step, self.count)}
        return post(source, target, self.sems, self.kind + 2 * side, step, where)

    def early(self, near):
        return post(
            self.part.at[2, :, pl.ds((near - 1) * self.half, self.half)],
            self.via.at[near - 1],
            self.sems,
            self.kind + 1,
            near,
            {"shard": partner(self.me, near, 4)},
        )

    def send(self, step, value, ready=True):
        if not self.square:
            self.part[step - 1] = value.astype(BF16)
            self.direct(step).start()
            return
        self.part[step - 1] = value.astype(BF16)

        @pl.when(step == 3)
        def _():
            for near in (1, 2):
                self.early(near).start()

        for near in (1, 2):

            @pl.when(step == near)
            def _():
                self.direct(near, near - 1).start()
                if ready:
                    side = 2 - near
                    self.combine(near, value[:, side * self.half : (side + 1) * self.half])

    def combine(self, near, value=None):
        side = 2 - near
        columns = slice(side * self.half, (side + 1) * self.half)
        if value is None:
            value = self.part[near - 1, :, columns].astype(F32)
        self.early(3 - near).wait_recv()
        self.part[near - 1, :, columns] = (value + self.via[side].astype(F32)).astype(BF16)
        self.direct(near, side).start()

    def total(self, value):
        for step in self.steps:
            for side in range(2 if self.square else 1):
                self.direct(step, side).wait_recv()
            value += self.landed[step - 1].astype(F32)
        return value

    def finish(self):
        for step in self.steps:
            for side in range(2 if self.square else 1):
                self.direct(step, side).wait_send()
            if self.square:
                self.early(step).wait_send()


def passing(count, rows, model):
    slots = 2 if count == 4 else count - 1
    return [
        ((count - 1, rows, model), BF16),
        ((slots, rows, model), BF16),
        ((2, rows, model // 2), BF16),
    ]


class Chain:
    def __init__(self, rep, chips, parts, own, sems, kind, scratch, total):
        self.parts, self.own, self.sems, self.kind = parts, own, sems, kind
        self.up, self.cross, self.held = scratch
        self.total = total
        core, chip = rep % 2, rep // 2
        side = chip // (chips // 2)
        self.core, self.last = core, chips // 2 - 1
        self.depth = side * (chips - 1 - chip) + (1 - side) * chip
        ahead = 1 - 2 * side
        self.inner = {"rep": (chip + ahead) * 2 + core}
        self.outer = {"rep": (chip - ahead) * 2 + core}
        self.mate = {"rep": rep + 1 - 2 * core}

    def copy(self, which, part):
        where = (self.inner, self.inner, self.outer, self.mate)[which]
        final = self.total(self.core, part)
        source = self.held.at[part] if which < 2 else final
        target = (self.up.at[part], self.cross.at[part], final, final)[which]
        return post(source, target, self.sems, self.kind + which, part, where)

    def reduce(self, part):
        depth, last = self.depth, self.last
        value = self.own(part)

        @pl.when(depth == 0)
        def _():
            self.held[part] = value.astype(BF16)

        if last > 0:

            @pl.when(depth > 0)
            def _():
                self.copy(0, part).wait_recv()
                self.held[part] = (value + self.up[part].astype(F32)).astype(BF16)

            @pl.when(depth < last)
            def _():
                self.copy(0, part).start()

        @pl.when(depth == last)
        def _():
            self.copy(1, part).start()

    def result(self, part):
        depth, last = self.depth, self.last

        @pl.when(depth == last)
        def _():
            self.copy(1, part).wait_recv()
            both = self.held[part].astype(F32) + self.cross[part].astype(F32)
            self.total(self.core, part)[...] = both.astype(BF16)

        if last > 0:

            @pl.when(depth < last)
            def _():
                self.copy(2, part).wait_recv()

            @pl.when(depth > 0)
            def _():
                self.copy(2, part).start()

        self.copy(3, part).start()

    def within(self, part, act):
        @pl.when((part >= 0) & (part < self.parts))
        def _():
            act(part)

    def step(self, turn):
        self.within(turn - self.depth, self.reduce)
        self.within(turn - (2 * self.last + 1 - self.depth), self.result)

    def turns(self):
        return self.parts + 2 * self.last + 1

    def finish(self):
        def closing(part, carry):
            if self.last > 0:

                @pl.when(self.depth < self.last)
                def _():
                    self.copy(0, part).wait_send()

                @pl.when(self.depth > 0)
                def _():
                    self.copy(2, part).wait_send()

            @pl.when(self.depth == self.last)
            def _():
                self.copy(1, part).wait_send()

            final = self.total(1 - self.core, part)
            self.copy(3, part).wait_send()
            post(final, final, self.sems, self.kind + 3, part, self.mate).wait_recv()
            return carry

        lax.fori_loop(0, self.parts, closing, 0)


def run(chains):
    depth, lag = chains[0].depth, 2

    def loop(count, act):
        def body(part, carry):
            act(part)
            return carry

        lax.fori_loop(0, count, body, 0)

    @pl.when(depth == 0)
    def _():
        for chain in chains:
            loop(chain.parts, chain.reduce)
        for chain in chains:
            loop(chain.parts, chain.result)

    if chains[0].last > 0:

        @pl.when(depth > 0)
        def _():
            for chain in chains:

                def both(part):
                    chain.within(part, chain.reduce)
                    chain.within(part - lag, chain.result)

                loop(chain.parts + lag, both)


def live_keys(local_len, rows, total):
    place = lax.broadcasted_iota(jnp.int32, (1, total), 1)
    inner = place % rows
    return (inner < local_len) & ((place // rows) * local_len + inner < LEN)


def first_kernel(
    count,
    size,
    local_len,
    tok_ref,
    up_ref,
    pk_ref,
    wqkv_ref,
    wo_ref,
    w1_ref,
    bias_ref,
    first_all,
    fc2_all,
    wq,
    w1c,
    project,
    mixed,
    stat,
    attn,
    pk_all,
    part,
    landed,
    via,
    send_sem,
    recv_sem,
):
    sems = (send_sem, recv_sem)
    me, rep = lax.axis_index("shard"), lax.axis_index("rep")
    core = rep % 2
    mate = rep + 1 - 2 * core
    rows, model = tok_ref.shape
    owned = pk_ref.shape[1]
    units = w1c.shape[1]
    half = owned // 2
    greet(me, count, (mate,))

    own_cols = pl.ds(pl.multiple_of(me * owned, 128), owned)
    own_rows = pl.ds(pl.multiple_of(me * owned, 16), owned)
    mine = spot(me, rows)
    ours = pl.ds(pl.multiple_of(core * half, 16), half)
    pk_all[:, own_cols] = pk_ref[...]
    PK, FIRST, FC2, W1, WQ, FQ, F1, SUM = 0, 1, 3, 5, 6, 9, 10, 11
    gather_first = Gather(first_all, rows, me, count, sems, FIRST)
    gather_fc2 = Gather(fc2_all, rows, me, count, sems, FC2)
    scatter = Scatter(part, landed, via, me, count, sems, SUM)
    sent = []

    def block(source):
        return pl.ds(pl.multiple_of(source * owned + core * half, 16), half)

    def push(source, target, kind, step):
        copy = post(source, target, sems, kind, step, {"shard": partner(me, step, count)})
        copy.start()
        sent.append(copy)

    def hand(target, kind, step):
        copy = post(target, target, sems, kind, step, {"rep": mate})
        copy.start()
        sent.append(copy)
        return copy

    for step in range(1, count):
        push(pk_ref, pk_all.at[:, own_cols], PK, step)
    for step in range(1, count):
        other = partner(me, step, count)
        for third in range(3):
            push(
                wqkv_ref.at[ours, pl.ds(pl.multiple_of(third * model + other * owned, 128), owned)],
                wq.at[block(me), third * owned : (third + 1) * owned],
                WQ + third,
                step,
            )
    hidden = tok_ref[...].astype(F32)
    normed, _ = norm_parts(hidden)
    for step in range(1, count):
        other = pl.ds(pl.multiple_of(partner(me, step, count) * owned, 128), owned)
        post(pk_ref, pk_all.at[:, other], sems, PK, step, {"rep": mate}).wait_recv()
    first_all[mine, :] = (normed * pk_all[0:1] + pk_all[2:3]).astype(BF16)
    gather_first.start()
    for third in range(3):
        columns = pl.ds(pl.multiple_of(third * model + me * owned, 128), owned)
        wq[own_rows, third * owned : (third + 1) * owned] = wqkv_ref[:, columns]
    w1c[own_rows, :] = w1_ref[:, pl.ds(pl.multiple_of(me * units, 128), units)]
    fc2_all[mine, :] = (up_ref[...].astype(F32) * pk_all[5:6]).astype(BF16)

    handed = []
    for step in range(1, count):
        other = partner(me, step, count)
        for third in range(3):
            columns = slice(third * owned, (third + 1) * owned)
            post(
                wq.at[block(other), columns],
                wq.at[block(other), columns],
                sems,
                WQ + third,
                step,
                {"rep": mate},
            ).wait_recv()
        handed.append(hand(wq.at[block(other)], FQ, step))
    for step in range(1, count):
        push(
            w1_ref.at[ours, pl.ds(pl.multiple_of(partner(me, step, count) * units, 128), units)],
            w1c.at[block(me)],
            W1,
            step,
        )
    for copy in handed:
        copy.wait_recv()
    gather_fc2.start()

    def projecting(step, carry):
        there = spot(partner(me, step, count), rows)

        gather_first.arrive(step)
        project[there, :] = (plain_dot(first_all[there, :], wq[...]) + bias_ref[...]).astype(BF16)
        return carry

    lax.fori_loop(0, count, projecting, 0)
    live = live_keys(local_len, rows, project.shape[0])

    def attending(turn, carry):
        step = count - 1 - turn
        there = spot(partner(me, step, count), rows)

        @pl.when(turn == count - 2)
        def _():
            gather_fc2.arrive(1)

        attend_rows(size, there, live, project, mixed, stat)
        result = plain_dot(mixed[there, :], wo_ref[...])

        @pl.when(step > 0)
        def _():
            scatter.send(step, result)

        @pl.when(step == 0)
        def _():
            attn[...] = result

        return carry

    lax.fori_loop(0, count, attending, 0)
    for step in range(1, count):
        other = block(partner(me, step, count))
        post(w1c.at[other], w1c.at[other], sems, W1, step, {"rep": mate}).wait_recv()
        hand(w1c.at[other], F1, step).wait_recv()
        if step > 1:
            gather_fc2.arrive(step)
    attn[...] = scatter.total(attn[...] + pk_all[6:7])
    for done in (gather_first, gather_fc2, scatter):
        done.finish()
    for copy in sent:
        copy.wait_send()


def feed_kernel(
    count,
    tok_ref,
    up_ref,
    attn_ref,
    pk_ref,
    fc2_all,
    w1c,
    w2_ref,
    bias_ref,
    middle_out,
    middle_grad,
    branch,
    pair_w1,
    pair_w2,
    grad_bias,
    sums,
    grad_w1,
    grad_w2,
    other_w1,
    other_w2,
    second_all,
    pre_in,
    act,
    part,
    landed,
    via,
    own,
    send_sem,
    recv_sem,
):
    sems = (send_sem, recv_sem)
    me = lax.axis_index("shard")
    rows, model = tok_ref.shape
    units = w1c.shape[1]
    tile = min(256, units)
    mine = spot(me, rows)
    SECOND, SUM, PAIR = 0, 2, 5
    gather = Gather(second_all, rows, me, count, sems, SECOND)
    scatter = Scatter(part, landed, via, me, count, sems, SUM)
    rep = lax.axis_index("rep")
    core = rep % 2
    mate = rep + 1 - 2 * core
    owned = model // count
    half = owned // 2
    greet(me, count, (mate,))

    middle = tok_ref[...].astype(F32) + pk_ref[4:5] * attn_ref[...]
    middle_out[...] = middle
    normed, _ = norm_parts(middle)
    second_all[mine, :] = (normed * pk_ref[1:2] + pk_ref[3:4]).astype(BF16)
    gather.start()
    grad_bias[...] = jnp.zeros_like(grad_bias)

    def feeding(step, carry):
        there = spot(partner(me, step, count), rows)

        gather.arrive(step)

        def tiles(number, inner):
            columns = pl.ds(pl.multiple_of(number * tile, 128), tile)
            pre = plain_dot(second_all[there, :], w1c[:, columns]) + bias_ref[:, columns]
            value, slope = gelu_pair(pre)
            act[there, columns] = value.astype(BF16)
            back = back_dot(
                fc2_all[there, :], w2_ref[pl.ds(pl.multiple_of(number * tile, 16), tile), :]
            )
            back = back * slope
            grad_bias[:, columns] += column_sum(back)
            pre_in[there, columns] = back.astype(BF16)
            return inner

        lax.fori_loop(0, units // tile, tiles, 0)
        result = back_dot(pre_in[there, :], w1c[...])

        @pl.when(step > 0)
        def _():
            scatter.send(step, result, False)

        @pl.when(step == 0)
        def _():
            own[...] = result

        return carry

    lax.fori_loop(0, count, feeding, 0)

    def branching(step, carry):
        there = spot(partner(me, step, count), rows)
        branch[step] = plain_dot(act[there, :], w2_ref[...]).astype(BF16)
        return carry

    lax.fori_loop(0, count, branching, 0)
    if count == 4:
        for near in (1, 2):
            scatter.combine(near)

    def weighing_two(number, carry):
        columns = pl.ds(pl.multiple_of(number * tile, 128), tile)
        here = pl.ds(pl.multiple_of(lax.rem(number, halves) * tile, 16), tile)
        grad_w2[number // halves, here, :] = row_dot(act[:, columns], fc2_all[...]).astype(BF16)
        return carry

    halves = units // tile // 2
    lax.fori_loop(0, units // tile, weighing_two, 0)
    copies = [post(grad_w2.at[1 - core], other_w2, sems, PAIR, 0, {"rep": mate})]
    copies[0].start()

    def weighing_one(number, carry):
        columns = pl.ds(pl.multiple_of(number * owned, 128), owned)
        product = row_dot(second_all[:, columns], pre_in[...]).astype(BF16)
        grad_w1[0, number] = product[:half]
        grad_w1[1, number] = product[half:]
        return carry

    lax.fori_loop(0, count, weighing_one, 0)
    copies.append(post(grad_w1.at[1 - core], other_w1, sems, PAIR, 1, {"rep": mate}))
    copies[1].start()
    for copy in copies:
        copy.wait()
    pair_w2[...] = (grad_w2[core].astype(F32) + other_w2[...].astype(F32)).astype(BF16)
    pair_w1[...] = (grad_w1[core].astype(F32) + other_w1[...].astype(F32)).astype(BF16)

    result = scatter.total(own[...])
    normed, inverse = norm_parts(middle_out[...])
    sums[0:1, :] = column_sum(result * normed)
    sums[1:2, :] = column_sum(result)
    middle_grad[...] = up_ref[...].astype(F32) + norm_backward(
        result, normed, inverse, pk_ref[1:2]
    )
    gather.finish()
    scatter.finish()


def last_kernel(
    count,
    size,
    local_len,
    tok_ref,
    up_ref,
    attn_ref,
    pk_ref,
    middle_ref,
    middle_grad,
    branch,
    sums_in,
    first_all,
    project,
    mixed,
    stat,
    wo_ref,
    wq,
    pair_w1,
    pair_w2,
    bias_rows,
    output,
    outgoing,
    total_w1,
    total_w2,
    total_wq,
    total_wo,
    flat,
    attn_all,
    joined,
    dk,
    dv,
    part,
    landed,
    via,
    part_two,
    landed_two,
    via_two,
    own,
    swapped_w1,
    up_w1,
    cross_w1,
    held_w1,
    up_w2,
    cross_w2,
    held_w2,
    swapped_wq,
    up_wq,
    cross_wq,
    held_wq,
    up_wo,
    cross_wo,
    held_wo,
    grad_wq,
    grad_wo,
    other_wq,
    other_wo,
    sums,
    sums_by,
    flat_by,
    send_sem,
    recv_sem,
):
    sems = (send_sem, recv_sem)
    me = lax.axis_index("shard")
    rows, model = tok_ref.shape
    total, owned = mixed.shape
    mine = spot(me, rows)
    GRAD, BRANCH, SUM, SWAP1, SWAPQ, PAIR, SMALL, FLAT = 0, 2, 5, 8, 9, 10, 11, 12
    gather = Gather(attn_all, rows, me, count, sems, GRAD)
    scatter = Scatter(part, landed, via, me, count, sems, SUM)
    scatter_two = Scatter(part_two, landed_two, via_two, me, count, sems, BRANCH)
    rep, reps = lax.axis_index("rep"), lax.axis_size("rep")
    core = rep % 2
    mate = rep + 1 - 2 * core
    half = owned // 2
    pairs = max(1, owned // max(128, size))
    greet(me, count, [lax.rem(rep + other, reps) for other in range(1, reps)])

    def summed_w2(number):
        return pair_w2[number].astype(F32)

    def summed_w1(number):
        step = partner(me, number, count)

        @pl.when(step > 0)
        def _():
            post(
                swapped_w1.at[number], swapped_w1.at[number], sems, SWAP1, step, {"shard": me}
            ).wait_recv()

        return swapped_w1[number].astype(F32)

    def summed_wq(number):
        source, third = number // 3, lax.rem(number, 3)
        step = partner(me, source, count)

        @pl.when((step > 0) & (third == 0))
        def _():
            post(
                swapped_wq.at[source], swapped_wq.at[source], sems, SWAPQ, step, {"shard": me}
            ).wait_recv()

        columns = pl.ds(pl.multiple_of(third * owned, 128), owned)
        return swapped_wq[source, :, columns].astype(F32)

    def summed_wo(number):
        return grad_wo[core, number].astype(F32) + other_wo[number].astype(F32)

    def place_w1(part, number):
        rows_here = pl.ds(pl.multiple_of(part * half, 16), half)
        return total_w1.at[rows_here, pl.ds(pl.multiple_of(number * units, 128), units)]

    def place_w2(part, number):
        return total_w2.at[spot(part * count + number, pair_w2.shape[1])]

    def place_wq(part, number):
        column = lax.rem(number, 3) * model + (number // 3) * owned
        rows_here = pl.ds(pl.multiple_of(part * half, 16), half)
        return total_wq.at[rows_here, pl.ds(pl.multiple_of(column, 128), owned)]

    def place_wo(part, number):
        return total_wo.at[spot(part * count + number, half // count)]

    units = pair_w1.shape[2]
    line = functools.partial(Chain, rep, reps // 2)
    chain_w2 = line(count, summed_w2, sems, 13, (up_w2, cross_w2, held_w2), place_w2)
    chain_w1 = line(count, summed_w1, sems, 17, (up_w1, cross_w1, held_w1), place_w1)
    chain_wo = line(count, summed_wo, sems, 21, (up_wo, cross_wo, held_wo), place_wo)
    chain_wq = line(3 * count, summed_wq, sems, 25, (up_wq, cross_wq, held_wq), place_wq)

    def feed_turn(turn):
        chain_w2.step(turn)
        chain_w1.step(turn - count)

    attn_grad = middle_grad[...] * pk_ref[4:5]
    attn_all[mine, :] = attn_grad.astype(BF16)
    gather.start()
    sent = []
    for step in range(1, count):
        other = partner(me, step, count)
        copy = post(
            pair_w1.at[other], swapped_w1.at[me], sems, SWAP1, step, {"shard": other}
        )
        copy.start()
        sent.append(copy)
    swapped_w1[me] = pair_w1[me]
    for step in range(count - 1, 0, -1):
        scatter_two.send(step, branch[step].astype(F32), False)
    sums[1:2, :] = sums_in[0:1, :]
    sums[3:4, :] = sums_in[1:2, :]
    sums[4:5, :] = column_sum(middle_grad[...] * attn_ref[...])
    sums[6:7, :] = column_sum(attn_grad)
    sums[7:8, :] = column_sum(up_ref[...].astype(F32) * pk_ref[5:6])
    dk[...] = jnp.zeros_like(dk)
    dv[...] = jnp.zeros_like(dv)
    live = live_keys(local_len, rows, total)

    def attending(step, carry):
        there = spot(partner(me, step, count), rows)

        gather.arrive(step)
        if count == 4:

            @pl.when(step == 2)
            def _():
                for near in (1, 2):
                    scatter_two.combine(near)

        grad = back_dot(attn_all[there, :], wo_ref[...]).astype(BF16)
        attend_rows_back(
            size,
            there,
            live,
            project,
            mixed,
            stat,
            grad,
            joined,
            dk,
            dv,
            lambda pair: feed_turn(step * pairs + pair),
        )
        return carry

    lax.fori_loop(0, count, attending, 0)
    turned = jnp.transpose(dv[...])
    joined[:, owned : 2 * owned] = jnp.transpose(dk[...]).astype(BF16)
    joined[:, 2 * owned :] = turned.astype(BF16)
    flat[8:9, :] = column_sum(joined[:, 0:owned].astype(F32))
    flat[9:10, :] = column_sum(turned)

    product = row_dot(mixed[...], attn_all[...]).astype(BF16)
    grad_wo[0] = product[:half].reshape(grad_wo.shape[1:])
    grad_wo[1] = product[half:].reshape(grad_wo.shape[1:])
    pair_wo = post(grad_wo.at[1 - core], other_wo, sems, PAIR, 0, {"rep": mate})
    pair_wo.start()

    def weighing(number, carry):
        columns = pl.ds(pl.multiple_of(number * owned, 128), owned)
        product = row_dot(first_all[:, columns], joined[...]).astype(BF16)
        grad_wq[0, number] = product[:half]
        grad_wq[1, number] = product[half:]
        return carry

    lax.fori_loop(0, count, weighing, 0)
    pair_wq = post(grad_wq.at[1 - core], other_wq, sems, PAIR, 1, {"rep": mate})
    pair_wq.start()
    feed_turns = 2 * count + chain_w1.turns() - chain_w1.parts
    start = count * pairs

    def turning(turn, carry):
        feed_turn(turn)
        return carry

    pair_wo.wait()
    pair_wq.wait()
    grad_wq[core] = (grad_wq[core].astype(F32) + other_wq[...].astype(F32)).astype(BF16)
    for step in range(1, count):
        other = partner(me, step, count)
        copy = post(
            grad_wq.at[core, other], swapped_wq.at[me], sems, SWAPQ, step, {"shard": other}
        )
        copy.start()
        sent.append(copy)
    swapped_wq[me] = grad_wq[core, me]
    def returning(turn, carry):
        step = count - 1 - turn
        there = spot(partner(me, step, count), rows)
        result = back_dot(joined[there, :], wq[...])

        @pl.when(step > 0)
        def _():
            scatter.send(step, result)

        @pl.when(step == 0)
        def _():
            own[...] = result

        return carry

    lax.fori_loop(0, count, returning, 0)
    lax.fori_loop(start, feed_turns, turning, 0)
    result = branch[0].astype(F32) + pk_ref[7:8]
    result = scatter_two.total(result)
    output[...] = (middle_ref[...] + pk_ref[5:6] * result).astype(BF16)
    sums[5:6, :] = column_sum(up_ref[...].astype(F32) * result)

    run((chain_wo, chain_wq))
    result = scatter.total(own[...])
    normed, inverse = norm_parts(tok_ref[...].astype(F32))
    sums[0:1, :] = column_sum(result * normed)
    sums[2:3, :] = column_sum(result)
    outgoing[...] = middle_grad[...] + norm_backward(result, normed, inverse, pk_ref[0:1])
    own_cols = pl.ds(pl.multiple_of(me * owned, 128), owned)
    for step in range(1, count):
        other = partner(me, step, count)
        copy = post(
            sums.at[:, pl.ds(pl.multiple_of(other * owned, 128), owned)],
            sums_by.at[me],
            sems,
            SMALL,
            step,
            {"shard": other},
        )
        copy.start()
        sent.append(copy)
    sums_by[me] = sums[:, own_cols]

    for step in range(1, count):
        other = partner(me, step, count)
        post(sums_by.at[other], sums_by.at[other], sems, SMALL, step, {"shard": me}).wait_recv()
    flat[0:8, :] = functools.reduce(lambda left, right: left + right, [sums_by[i] for i in range(count)])
    flat[10:, :] = bias_rows[...]
    flat_by[rep] = flat[...]
    for step in range(1, reps):
        copy = post(
            flat, flat_by.at[rep], sems, FLAT, step, {"rep": lax.rem(rep + step, reps)}
        )
        copy.start()
        sent.append(copy)
    for copy in sent:
        copy.wait_send()
    for step in range(1, reps):
        source = lax.rem(rep + reps - step, reps)
        post(flat_by.at[source], flat_by.at[source], sems, FLAT, step, {"shard": me}).wait_recv()
    flat[...] = functools.reduce(lambda left, right: left + right, [flat_by[i] for i in range(reps)])
    for done in (gather, scatter, scatter_two, chain_w2, chain_w1, chain_wo, chain_wq):
        done.finish()


def call(body, number, name, operands, outs, scratch, kinds, flops):
    return pl.pallas_call(
        body,
        in_specs=[VMEM] * len(operands),
        out_specs=[VMEM] * len(outs),
        out_shape=[jax.ShapeDtypeStruct(*out) for out in outs],
        scratch_shapes=[pltpu.VMEM(*item) for item in scratch]
        + [pltpu.SemaphoreType.DMA(kinds), pltpu.SemaphoreType.DMA(kinds)],
        compiler_params=pltpu.CompilerParams(
            collective_id=number, has_side_effects=True, vmem_limit_bytes=60 * 1024 * 1024
        ),
        cost_estimate=pl.CostEstimate(flops=flops, bytes_accessed=2**24, transcendentals=2**22),
        name=name,
    )(*operands)


def local(
    tokens,
    cotangent,
    slot_live,
    w_qkv,
    w_out,
    w_fc1,
    w_fc2,
    norm_gain,
    norm_bias,
    layer_scale,
    qv_bias,
    proj_bias,
    fc1_bias,
):
    count = lax.axis_size("shard")
    me = lax.axis_index("shard")
    _, local_len, model = tokens.shape
    owned = model // count
    units = w_fc2.shape[1]
    hidden_units = w_fc1.shape[2]
    size = model // HEADS
    rows = -(-local_len // 16) * 16
    extra = rows - local_len
    total = rows * count

    tok = jnp.pad(tokens[0], ((0, extra), (0, 0)))
    place = jnp.arange(rows, dtype=jnp.int32)
    valid = (slot_live[0] > 0) & (place < local_len) & (me * local_len + place < LEN)
    up = jnp.where(valid[:, None], jnp.pad(cotangent[0], ((0, extra), (0, 0))), 0).astype(BF16)
    packed = jnp.concatenate([norm_gain[0], norm_bias[0], layer_scale[0], proj_bias[0]], axis=0)
    packed = packed.astype(F32)
    qv = qv_bias[0].astype(F32)
    bias_row = jnp.concatenate([qv[0], jnp.zeros_like(qv[0]), qv[1]])[None]

    big = (total, model)
    small = (rows, model)
    first_all, fc2_all, wq, w1c, project, mixed, stat, attn, pk_all = call(
        functools.partial(first_kernel, count, size, local_len),
        0,
        "attend_forward",
        (tok, up, packed, w_qkv[0], w_out[0], w_fc1[0], bias_row),
        (
            (big, BF16),
            (big, BF16),
            ((model, 3 * owned), BF16),
            ((model, units), BF16),
            ((total, 3 * owned), BF16),
            ((total, owned), BF16),
            ((total, 128), F32),
            (small, F32),
            ((8, model), F32),
        ),
        passing(count, *small),
        (14, count),
        10**10,
    )
    half = owned // 2
    wide_one = (count, half, units)
    wide_two = (count, units // 2 // count, model)
    wide_q = (count, half, 3 * owned)
    wide_o = (count, half // count, model)
    middle, middle_grad, branch, pair_w1, pair_w2, grad_b1, sums = call(
        functools.partial(feed_kernel, count),
        1,
        "feed",
        (tok, up, attn, pk_all, fc2_all, w1c, w_fc2[0], fc1_bias.astype(F32)),
        (
            (small, F32),
            (small, F32),
            ((count, *small), BF16),
            (wide_one, BF16),
            ((units // 2, model), BF16),
            ((1, units), F32),
            ((8, model), F32),
        ),
        (
            ((2, *wide_one), BF16),
            ((2, units // 2, model), BF16),
            (wide_one, BF16),
            ((units // 2, model), BF16),
            (big, BF16),
            ((total, units), BF16),
            ((total, units), BF16),
            *passing(count, *small),
            (small, F32),
        ),
        (6, count),
        10**10,
    )
    reps = lax.axis_size("rep")
    extra_rows = units // owned
    flat_rows = -(-(10 + extra_rows) // 8) * 8
    bias_rows = jnp.pad(
        grad_b1.reshape(extra_rows, owned), ((0, flat_rows - 10 - extra_rows), (0, 0))
    )
    output, outgoing, total_w1, total_w2, total_wq, total_wo, flat = call(
        functools.partial(last_kernel, count, size, local_len),
        2,
        "attend_backward",
        (
            tok,
            up,
            attn,
            pk_all,
            middle,
            middle_grad,
            branch,
            sums,
            first_all,
            project,
            mixed,
            stat,
            w_out[0],
            wq,
            pair_w1,
            pair_w2.reshape(wide_two),
            bias_rows,
        ),
        (
            (small, BF16),
            (small, F32),
            ((owned, hidden_units), BF16),
            ((units, model), BF16),
            ((owned, 3 * model), BF16),
            ((owned, model), BF16),
            ((flat_rows, owned), F32),
        ),
        (
            (big, BF16),
            ((total, 3 * owned), BF16),
            ((owned, total), F32),
            ((owned, total), F32),
            *passing(count, *small),
            *passing(count, *small),
            (small, F32),
            *([(wide_one, BF16)] * 4),
            *([(wide_two, BF16)] * 3),
            (wide_q, BF16),
            *([((3 * count, half, owned), BF16)] * 3),
            *([(wide_o, BF16)] * 3),
            ((2, *wide_q), BF16),
            ((2, *wide_o), BF16),
            (wide_q, BF16),
            (wide_o, BF16),
            ((8, model), F32),
            ((count, 8, owned), F32),
            ((reps, flat_rows, owned), F32),
        ),
        (29, max(3 * count, reps)),
        10**10,
    )
    return (
        output[:local_len][None],
        outgoing[:local_len][None],
        total_wq.astype(F32)[None],
        total_wo.astype(F32)[None],
        total_w1.astype(F32)[None],
        total_w2.astype(F32)[None],
        flat[0:2][None],
        flat[2:4][None],
        flat[4:6][None],
        flat[8:10][None],
        flat[6:8][None],
        flat[10 : 10 + extra_rows].reshape(1, -1),
    )


def solution(mesh):
    rows = P("rep", "shard", None)
    matrix = P(None, "shard", None)
    vector = P(None, None, "shard")
    return jax.shard_map(
        local,
        mesh=mesh,
        in_specs=(rows, rows, P("rep"), *([matrix] * 4), *([vector] * 5), P(None, "shard")),
        out_specs=(rows, rows, *([matrix] * 4), *([vector] * 5), P(None, "shard")),
        check_vma=False,
    )
```

```python
import functools
import math

import jax
import jax.numpy as jnp
from jax import lax
from jax.experimental import pallas as pl
from jax.experimental.pallas import tpu as pltpu
from jax.sharding import PartitionSpec as P

HEADS = 16
LEN = 1025
EPSILON = 1e-06
F32 = jnp.float32
BF16 = jnp.bfloat16
MESH = pl.DeviceIdType.MESH
HOP = 2
VMEM = pl.BlockSpec(memory_space=pltpu.VMEM)


def norm_parts(hidden):
    center = hidden - jnp.mean(hidden, axis=-1, keepdims=True)
    inverse = lax.rsqrt(jnp.mean(center * center, axis=-1, keepdims=True) + EPSILON)
    return (center * inverse, inverse)


def norm_backward(incoming, normed, inverse, gain):
    scaled = incoming * gain
    return inverse * (
        scaled
        - jnp.mean(scaled, axis=-1, keepdims=True)
        - normed * jnp.mean(scaled * normed, axis=-1, keepdims=True)
    )


def gelu_pair(values):
    cumulative = 0.5 * (1.0 + lax.erf(values * 0.7071067811865476))
    slope = cumulative + values * jnp.exp(-0.5 * values * values) * 0.3989422804014327
    return (values * cumulative, slope)


def plain_dot(left, right):
    return jnp.dot(left, right, preferred_element_type=F32)


def row_dot(left, right):
    return lax.dot_general(left, right, (((0,), (0,)), ((), ())), preferred_element_type=F32)


def back_dot(left, right):
    return lax.dot_general(left, right, (((1,), (1,)), ((), ())), preferred_element_type=F32)


def head_parts(size, width):
    lane = lax.broadcasted_iota(jnp.int32, (1, width), 1)
    return [
        ((lane >= size * number) & (lane < size * (number + 1))) for number in range(width // size)
    ]


def column_sum(values):
    return jnp.sum(values, axis=0, keepdims=True)


def partner(me, step, count):
    other, bit = me, 1
    while bit < count:
        other = other + ((step // bit) % 2) * (1 - 2 * ((me // bit) % 2)) * bit
        bit *= 2
    return other


def spot(index, rows):
    return pl.ds(pl.multiple_of(index * rows, math.gcd(rows, 1024)), rows)


def greet(me, count, others=()):
    barrier = pltpu.get_barrier_semaphore()
    for step in range(1, count):
        pl.semaphore_signal(
            barrier, 1, device_id={"shard": partner(me, step, count)}, device_id_type=MESH
        )
    for other in others:
        pl.semaphore_signal(barrier, 1, device_id={"rep": other}, device_id_type=MESH)
    pl.semaphore_wait(barrier, count - 1 + len(others))


def post(source, target, sems, kind, step, where):
    return pltpu.make_async_remote_copy(
        source,
        target,
        sems[0].at[kind, step],
        sems[1].at[kind, step],
        device_id=where,
        device_id_type=MESH,
    )


def score(queries, keys, live):
    return jnp.where(live, back_dot(queries, keys), -1e30)


def attend_rows(size, here, live, project, mixed, stat):
    owned = mixed.shape[1]
    width = min(max(128, size), owned)
    factor = 1.0 / math.sqrt(size)
    for pair in range(owned // width):
        columns = slice(pair * width, (pair + 1) * width)
        queries = project[here, columns]
        keys = project[:, owned + pair * width : owned + (pair + 1) * width]
        values = project[:, 2 * owned + pair * width : 2 * owned + (pair + 1) * width]
        out = jnp.zeros(queries.shape, F32)
        for number, part in enumerate(head_parts(size, width)):
            own = (jnp.where(part, queries, 0) * factor).astype(BF16)
            scores = score(own, keys, live)
            top = jnp.max(scores, axis=-1, keepdims=True)
            power = jnp.exp(scores - top)
            total = jnp.sum(power, axis=-1, keepdims=True)
            product = plain_dot(power.astype(BF16), values) * (1.0 / total)
            out = jnp.where(part, product, out)
            place = pair * (width // size) + number
            stat[here, place : place + 1] = top + jnp.log(total)
        mixed[here, columns] = out.astype(BF16)


def attend_rows_back(size, here, live, project, mixed, stat, grad, joined, dk, dv, between):
    owned = mixed.shape[1]
    width = min(max(128, size), owned)
    factor = 1.0 / math.sqrt(size)
    for pair in range(owned // width):
        columns = slice(pair * width, (pair + 1) * width)
        queries = project[here, columns]
        keys = project[:, owned + pair * width : owned + (pair + 1) * width]
        values = project[:, 2 * owned + pair * width : 2 * owned + (pair + 1) * width]
        grads = grad[:, columns]
        overlap = grads.astype(F32) * mixed[here, columns].astype(F32)
        turned_q = jnp.transpose(queries.astype(F32) * factor).astype(BF16)
        turned_g = jnp.transpose(grads.astype(F32)).astype(BF16)
        dq = jnp.zeros(queries.shape, F32)
        for number, part in enumerate(head_parts(size, width)):
            place = pair * (width // size) + number
            own_q = (jnp.where(part, queries, 0) * factor).astype(BF16)
            own_g = jnp.where(part, grads, 0).astype(BF16)
            weights = jnp.exp(score(own_q, keys, live) - stat[here, place : place + 1])
            delta = jnp.sum(jnp.where(part, overlap, 0), axis=-1, keepdims=True)
            slope = (weights * (back_dot(own_g, values) - delta)).astype(BF16)
            span = slice(place * size, (place + 1) * size)
            inner = slice(number * size, (number + 1) * size)
            dk[span, :] += plain_dot(turned_q[inner], slope)
            dv[span, :] += plain_dot(turned_g[inner], weights.astype(BF16))
            dq = jnp.where(part, plain_dot(slope, keys), dq)
            between(place)
        joined[here, columns] = (dq * factor).astype(BF16)


class Gather:
    def __init__(self, array, rows, me, count, sems, kind):
        self.array, self.rows, self.me, self.count = array, rows, me, count
        self.sems, self.kind, self.square = sems, kind, count == 4
        self.steps = (1, 2) if self.square else tuple(range(1, count))
        self.half = array.shape[1] // 2

    def direct(self, owner, step):
        block = self.array.at[spot(owner, self.rows)]
        where = {"shard": partner(self.me, step, self.count)}
        return post(block, block, self.sems, self.kind, step, where)

    def relay(self, owner, step):
        columns = pl.ds((step - 1) * self.half, self.half)
        block = self.array.at[spot(owner, self.rows), columns]
        where = {"shard": partner(self.me, 3 - step, self.count)}
        return post(block, block, self.sems, self.kind + 1, step, where)

    def start(self):
        for step in self.steps:
            self.direct(self.me, step).start()

    def arrive(self, step):
        if not self.square:

            @pl.when(step > 0)
            def _():
                self.direct(partner(self.me, step, self.count), step).wait_recv()

            return

        @pl.when(step == 1)
        def _():
            for near in (1, 2):
                owner = partner(self.me, near, 4)
                self.direct(owner, near).wait_recv()
                self.relay(owner, near).start()

        @pl.when(step == 3)
        def _():
            for near in (1, 2):
                self.relay(partner(self.me, 3, 4), near).wait_recv()

    def finish(self):
        for step in self.steps:
            self.direct(self.me, step).wait_send()
            if self.square:
                self.relay(partner(self.me, step, 4), step).wait_send()


class Scatter:
    def __init__(self, part, landed, via, me, count, sems, kind):
        self.part, self.landed, self.via, self.me, self.count = part, landed, via, me, count
        self.sems, self.kind, self.square = sems, kind, count == 4
        self.steps = (1, 2) if self.square else tuple(range(1, count))
        self.half = part.shape[2] // 2

    def direct(self, step, side=0):
        source, target = self.part.at[step - 1], self.landed.at[step - 1]
        if self.square:
            columns = pl.ds(side * self.half, self.half)
            source, target = source.at[:, columns], target.at[:, columns]
        where = {"shard": partner(self.me, step, self.count)}
        return post(source, target, self.sems, self.kind + 2 * side, step, where)

    def early(self, near):
        return post(
            self.part.at[2, :, pl.ds((near - 1) * self.half, self.half)],
            self.via.at[near - 1],
            self.sems,
            self.kind + 1,
            near,
            {"shard": partner(self.me, near, 4)},
        )

    def send(self, step, value, ready=True):
        if not self.square:
            self.part[step - 1] = value.astype(BF16)
            self.direct(step).start()
            return
        self.part[step - 1] = value.astype(BF16)

        @pl.when(step == 3)
        def _():
            for near in (1, 2):
                self.early(near).start()

        for near in (1, 2):

            @pl.when(step == near)
            def _():
                self.direct(near, near - 1).start()
                if ready:
                    side = 2 - near
                    self.combine(near, value[:, side * self.half : (side + 1) * self.half])

    def combine(self, near, value=None):
        side = 2 - near
        columns = slice(side * self.half, (side + 1) * self.half)
        if value is None:
            value = self.part[near - 1, :, columns].astype(F32)
        self.early(3 - near).wait_recv()
        self.part[near - 1, :, columns] = (value + self.via[side].astype(F32)).astype(BF16)
        self.direct(near, side).start()

    def total(self, value):
        for step in self.steps:
            for side in range(2 if self.square else 1):
                self.direct(step, side).wait_recv()
            value += self.landed[step - 1].astype(F32)
        return value

    def finish(self):
        for step in self.steps:
            for side in range(2 if self.square else 1):
                self.direct(step, side).wait_send()
            if self.square:
                self.early(step).wait_send()


def passing(count, rows, model):
    slots = 2 if count == 4 else count - 1
    return [
        ((count - 1, rows, model), BF16),
        ((slots, rows, model), BF16),
        ((2, rows, model // 2), BF16),
    ]


class Chain:
    def __init__(self, rep, chips, parts, own, sems, kind, scratch, total):
        self.parts, self.own, self.sems, self.kind = parts, own, sems, kind
        self.up, self.cross, self.held = scratch
        self.total = total
        core, chip = rep % 2, rep // 2
        side = chip // (chips // 2)
        self.core, self.last = core, chips // 2 - 1
        self.depth = side * (chips - 1 - chip) + (1 - side) * chip
        ahead = 1 - 2 * side
        self.inner = {"rep": (chip + ahead) * 2 + core}
        self.outer = {"rep": (chip - ahead) * 2 + core}
        self.mate = {"rep": rep + 1 - 2 * core}

    def copy(self, which, part):
        where = (self.inner, self.inner, self.outer, self.mate)[which]
        final = self.total(self.core, part)
        source = self.held.at[part] if which < 2 else final
        target = (self.up.at[part], self.cross.at[part], final, final)[which]
        return post(source, target, self.sems, self.kind + which, part, where)

    def reduce(self, part):
        depth, last = self.depth, self.last
        value = self.own(part)

        @pl.when(depth == 0)
        def _():
            self.held[part] = value.astype(BF16)

        if last > 0:

            @pl.when(depth > 0)
            def _():
                self.copy(0, part).wait_recv()
                self.held[part] = (value + self.up[part].astype(F32)).astype(BF16)

            @pl.when(depth < last)
            def _():
                self.copy(0, part).start()

        @pl.when(depth == last)
        def _():
            self.copy(1, part).start()

    def result(self, part):
        depth, last = self.depth, self.last

        @pl.when(depth == last)
        def _():
            self.copy(1, part).wait_recv()
            both = self.held[part].astype(F32) + self.cross[part].astype(F32)
            self.total(self.core, part)[...] = both.astype(BF16)

        if last > 0:

            @pl.when(depth < last)
            def _():
                self.copy(2, part).wait_recv()

            @pl.when(depth > 0)
            def _():
                self.copy(2, part).start()

        self.copy(3, part).start()

    def within(self, part, act):
        @pl.when((part >= 0) & (part < self.parts))
        def _():
            act(part)

    def step(self, turn):
        self.within(turn - HOP * self.depth, self.reduce)
        self.within(turn - HOP * (2 * self.last + 1 - self.depth), self.result)

    def turns(self):
        return self.parts + HOP * (2 * self.last + 1)

    def finish(self):
        def closing(part, carry):
            if self.last > 0:

                @pl.when(self.depth < self.last)
                def _():
                    self.copy(0, part).wait_send()

                @pl.when(self.depth > 0)
                def _():
                    self.copy(2, part).wait_send()

            @pl.when(self.depth == self.last)
            def _():
                self.copy(1, part).wait_send()

            final = self.total(1 - self.core, part)
            self.copy(3, part).wait_send()
            post(final, final, self.sems, self.kind + 3, part, self.mate).wait_recv()
            return carry

        lax.fori_loop(0, self.parts, closing, 0)


def loop(count, act):
    def body(part, carry):
        act(part)
        return carry

    lax.fori_loop(0, count, body, 0)


def lead(chain):
    @pl.when(chain.depth == 0)
    def _():
        loop(chain.parts, chain.reduce)


def follow(chain, lag=2):
    @pl.when(chain.depth == 0)
    def _():
        loop(chain.parts, chain.result)

    if chain.last > 0:

        @pl.when(chain.depth > 0)
        def _():
            def both(part):
                chain.within(part, chain.reduce)
                chain.within(part - lag, chain.result)

            loop(chain.parts + lag, both)


def live_keys(local_len, rows, total):
    place = lax.broadcasted_iota(jnp.int32, (1, total), 1)
    inner = place % rows
    return (inner < local_len) & ((place // rows) * local_len + inner < LEN)


def early_kernel(
    count,
    size,
    local_len,
    tok_ref,
    up_ref,
    pk_ref,
    wqkv_ref,
    wo_ref,
    w1_ref,
    bias_ref,
    w2_ref,
    fc1_bias,
    first_all,
    wq,
    project,
    mixed,
    stat,
    attn,
    pk_all,
    middle_out,
    middle_grad,
    branch,
    pair_w1,
    pair_w2,
    grad_bias,
    sums,
    fc2_all,
    w1c,
    part,
    landed,
    via,
    grad_w1,
    grad_w2,
    other_w1,
    other_w2,
    second_all,
    pre_in,
    act,
    part_two,
    landed_two,
    via_two,
    own,
    send_sem,
    recv_sem,
):
    sems = (send_sem, recv_sem)
    me, rep = lax.axis_index("shard"), lax.axis_index("rep")
    core = rep % 2
    mate = rep + 1 - 2 * core
    rows, model = tok_ref.shape
    owned = pk_ref.shape[1]
    units = w1c.shape[1]
    half = owned // 2
    greet(me, count, (mate,))

    own_cols = pl.ds(pl.multiple_of(me * owned, 128), owned)
    own_rows = pl.ds(pl.multiple_of(me * owned, 16), owned)
    mine = spot(me, rows)
    ours = pl.ds(pl.multiple_of(core * half, 16), half)
    pk_all[:, own_cols] = pk_ref[...]
    PK, FIRST, FC2, W1, WQ, FQ, F1, SUM = 0, 1, 3, 5, 6, 9, 10, 11
    gather_first = Gather(first_all, rows, me, count, sems, FIRST)
    gather_fc2 = Gather(fc2_all, rows, me, count, sems, FC2)
    scatter = Scatter(part, landed, via, me, count, sems, SUM)
    sent = []

    def block(source):
        return pl.ds(pl.multiple_of(source * owned + core * half, 16), half)

    def push(source, target, kind, step):
        copy = post(source, target, sems, kind, step, {"shard": partner(me, step, count)})
        copy.start()
        sent.append(copy)

    def hand(target, kind, step):
        copy = post(target, target, sems, kind, step, {"rep": mate})
        copy.start()
        sent.append(copy)
        return copy

    for step in range(1, count):
        push(pk_ref, pk_all.at[:, own_cols], PK, step)
    for step in range(1, count):
        other = partner(me, step, count)
        for third in range(3):
            push(
                wqkv_ref.at[ours, pl.ds(pl.multiple_of(third * model + other * owned, 128), owned)],
                wq.at[block(me), third * owned : (third + 1) * owned],
                WQ + third,
                step,
            )
    hidden = tok_ref[...].astype(F32)
    normed, _ = norm_parts(hidden)
    for step in range(1, count):
        other = pl.ds(pl.multiple_of(partner(me, step, count) * owned, 128), owned)
        post(pk_ref, pk_all.at[:, other], sems, PK, step, {"rep": mate}).wait_recv()
    first_all[mine, :] = (normed * pk_all[0:1] + pk_all[2:3]).astype(BF16)
    gather_first.start()
    for third in range(3):
        columns = pl.ds(pl.multiple_of(third * model + me * owned, 128), owned)
        wq[own_rows, third * owned : (third + 1) * owned] = wqkv_ref[:, columns]
    w1c[own_rows, :] = w1_ref[:, pl.ds(pl.multiple_of(me * units, 128), units)]
    fc2_all[mine, :] = (up_ref[...].astype(F32) * pk_all[5:6]).astype(BF16)

    handed = []
    for step in range(1, count):
        other = partner(me, step, count)
        for third in range(3):
            columns = slice(third * owned, (third + 1) * owned)
            post(
                wq.at[block(other), columns],
                wq.at[block(other), columns],
                sems,
                WQ + third,
                step,
                {"rep": mate},
            ).wait_recv()
        handed.append(hand(wq.at[block(other)], FQ, step))
    for copy in handed:
        copy.wait_recv()

    def shifting(step):
        other = partner(me, step, count)
        columns = pl.ds(pl.multiple_of(other * units, 128), units)
        where = {"shard": other}
        return post(w1_ref.at[ours, columns], w1c.at[block(me)], sems, W1, step, where)

    def projecting(step, carry):
        there = spot(partner(me, step, count), rows)

        gather_first.arrive(step)

        @pl.when(step == min(1, count - 1))
        def _():
            for other in range(1, count):
                shifting(other).start()

        project[there, :] = (plain_dot(first_all[there, :], wq[...]) + bias_ref[...]).astype(BF16)
        return carry

    lax.fori_loop(0, count, projecting, 0)
    gather_fc2.start()
    live = live_keys(local_len, rows, project.shape[0])

    def attending(turn, carry):
        step = count - 1 - turn
        there = spot(partner(me, step, count), rows)

        if count == 4:

            @pl.when(turn == count - 2)
            def _():
                gather_fc2.arrive(1)

        attend_rows(size, there, live, project, mixed, stat)
        result = plain_dot(mixed[there, :], wo_ref[...])

        @pl.when(step > 0)
        def _():
            scatter.send(step, result)

        @pl.when(step == 0)
        def _():
            attn[...] = result

        return carry

    lax.fori_loop(0, count, attending, 0)
    for step in range(1, count):
        other = block(partner(me, step, count))
        post(w1c.at[other], w1c.at[other], sems, W1, step, {"rep": mate}).wait_recv()
        handed.append(hand(w1c.at[other], F1, step))
    attn[...] = scatter.total(attn[...] + pk_all[6:7])
    tile = min(256, units)
    SECOND, SUM, PAIR = 14, 16, 19
    gather = Gather(second_all, rows, me, count, sems, SECOND)
    scatter_two = Scatter(part_two, landed_two, via_two, me, count, sems, SUM)
    middle = tok_ref[...].astype(F32) + pk_all[4:5] * attn[...]
    middle_out[...] = middle
    normed, _ = norm_parts(middle)
    second_all[mine, :] = (normed * pk_all[1:2] + pk_all[3:4]).astype(BF16)
    gather.start()
    grad_bias[...] = jnp.zeros_like(grad_bias)
    for copy in handed[count - 1 :]:
        copy.wait_recv()

    def feeding(step, carry):
        there = spot(partner(me, step, count), rows)

        gather.arrive(step)
        if count == 4:

            @pl.when(step > 1)
            def _():
                gather_fc2.arrive(step)

        else:
            gather_fc2.arrive(step)

        def tiles(number, inner):
            columns = pl.ds(pl.multiple_of(number * tile, 128), tile)
            pre = plain_dot(second_all[there, :], w1c[:, columns]) + fc1_bias[:, columns]
            value, slope = gelu_pair(pre)
            act[there, columns] = value.astype(BF16)
            back = back_dot(
                fc2_all[there, :], w2_ref[pl.ds(pl.multiple_of(number * tile, 16), tile), :]
            )
            back = back * slope
            grad_bias[:, columns] += column_sum(back)
            pre_in[there, columns] = back.astype(BF16)
            return inner

        lax.fori_loop(0, units // tile, tiles, 0)
        result = back_dot(pre_in[there, :], w1c[...])

        @pl.when(step > 0)
        def _():
            scatter_two.send(step, result, False)

        @pl.when(step == 0)
        def _():
            own[...] = result

        return carry

    lax.fori_loop(0, count, feeding, 0)

    def branching(step, carry):
        there = spot(partner(me, step, count), rows)
        branch[step] = plain_dot(act[there, :], w2_ref[...]).astype(BF16)
        return carry

    lax.fori_loop(0, count, branching, 0)
    if count == 4:
        for near in (1, 2):
            scatter_two.combine(near)

    def weighing_two(number, carry):
        columns = pl.ds(pl.multiple_of(number * tile, 128), tile)
        here = pl.ds(pl.multiple_of(lax.rem(number, halves) * tile, 16), tile)
        grad_w2[number // halves, here, :] = row_dot(act[:, columns], fc2_all[...]).astype(BF16)
        return carry

    halves = units // tile // 2
    lax.fori_loop(0, units // tile, weighing_two, 0)
    copies = [post(grad_w2.at[1 - core], other_w2, sems, PAIR, 0, {"rep": mate})]
    copies[0].start()

    def weighing_one(number, carry):
        columns = pl.ds(pl.multiple_of(number * owned, 128), owned)
        product = row_dot(second_all[:, columns], pre_in[...]).astype(BF16)
        grad_w1[0, number] = product[:half]
        grad_w1[1, number] = product[half:]
        return carry

    lax.fori_loop(0, count, weighing_one, 0)
    copies.append(post(grad_w1.at[1 - core], other_w1, sems, PAIR, 1, {"rep": mate}))
    copies[1].start()
    for copy in copies:
        copy.wait()
    pair_w2[...] = (grad_w2[core].astype(F32) + other_w2[...].astype(F32)).astype(BF16)
    pair_w1[...] = (grad_w1[core].astype(F32) + other_w1[...].astype(F32)).astype(BF16)

    result = scatter_two.total(own[...])
    normed, inverse = norm_parts(middle_out[...])
    sums[0:1, :] = column_sum(result * normed)
    sums[1:2, :] = column_sum(result)
    middle_grad[...] = up_ref[...].astype(F32) + norm_backward(
        result, normed, inverse, pk_all[1:2]
    )
    for done in (gather_first, gather_fc2, gather, scatter, scatter_two):
        done.finish()
    for step in range(1, count):
        shifting(step).wait_send()
    for copy in sent:
        copy.wait_send()


def last_kernel(
    count,
    size,
    local_len,
    tok_ref,
    up_ref,
    attn_ref,
    pk_ref,
    middle_ref,
    middle_grad,
    branch,
    sums_in,
    first_all,
    project,
    mixed,
    stat,
    wo_ref,
    wq,
    pair_w1,
    pair_w2,
    bias_rows,
    output,
    outgoing,
    total_w1,
    total_w2,
    total_wq,
    total_wo,
    flat,
    attn_all,
    joined,
    dk,
    dv,
    part,
    landed,
    via,
    part_two,
    landed_two,
    via_two,
    own,
    swapped_w1,
    up_w1,
    cross_w1,
    held_w1,
    up_w2,
    cross_w2,
    held_w2,
    swapped_wq,
    up_wq,
    cross_wq,
    held_wq,
    up_wo,
    cross_wo,
    held_wo,
    grad_wq,
    grad_wo,
    other_wq,
    other_wo,
    sums,
    sums_by,
    flat_by,
    send_sem,
    recv_sem,
):
    sems = (send_sem, recv_sem)
    me = lax.axis_index("shard")
    rows, model = tok_ref.shape
    total, owned = mixed.shape
    mine = spot(me, rows)
    GRAD, BRANCH, SUM, SWAP1, SWAPQ, PAIR, SMALL, FLAT = 0, 2, 5, 8, 9, 10, 11, 12
    gather = Gather(attn_all, rows, me, count, sems, GRAD)
    scatter = Scatter(part, landed, via, me, count, sems, SUM)
    scatter_two = Scatter(part_two, landed_two, via_two, me, count, sems, BRANCH)
    rep, reps = lax.axis_index("rep"), lax.axis_size("rep")
    core = rep % 2
    mate = rep + 1 - 2 * core
    half = owned // 2
    heads = owned // size
    greet(me, count, [lax.rem(rep + other, reps) for other in range(1, reps)])

    def summed_w2(number):
        return pair_w2[number].astype(F32)

    def summed_w1(part):
        number = part // 2
        step = partner(me, number, count)

        @pl.when((step > 0) & (lax.rem(part, 2) == 0))
        def _():
            post(
                swapped_w1.at[number], swapped_w1.at[number], sems, SWAP1, step, {"shard": me}
            ).wait_recv()

        return swapped_w1[number, spot(lax.rem(part, 2), half // 2)].astype(F32)

    def summed_wq(number):
        source, third = number // 3, lax.rem(number, 3)
        step = partner(me, source, count)

        @pl.when((step > 0) & (third == 0))
        def _():
            post(
                swapped_wq.at[source], swapped_wq.at[source], sems, SWAPQ, step, {"shard": me}
            ).wait_recv()

        columns = pl.ds(pl.multiple_of(third * owned, 128), owned)
        return swapped_wq[source, :, columns].astype(F32)

    def summed_wo(number):
        return grad_wo[core, number].astype(F32) + other_wo[number].astype(F32)

    def place_w1(part, number):
        rows_here = spot(part * 2 + lax.rem(number, 2), half // 2)
        return total_w1.at[rows_here, pl.ds(pl.multiple_of((number // 2) * units, 128), units)]

    def place_w2(part, number):
        return total_w2.at[spot(part * 2 * count + number, pair_w2.shape[1])]

    def place_wq(part, number):
        column = lax.rem(number, 3) * model + (number // 3) * owned
        rows_here = pl.ds(pl.multiple_of(part * half, 16), half)
        return total_wq.at[rows_here, pl.ds(pl.multiple_of(column, 128), owned)]

    def place_wo(part, number):
        return total_wo.at[spot(part * count + number, half // count)]

    units = pair_w1.shape[2]
    line = functools.partial(Chain, rep, reps // 2)
    chain_w2 = line(2 * count, summed_w2, sems, 13, (up_w2, cross_w2, held_w2), place_w2)
    chain_w1 = line(2 * count, summed_w1, sems, 17, (up_w1, cross_w1, held_w1), place_w1)
    chain_wo = line(count, summed_wo, sems, 21, (up_wo, cross_wo, held_wo), place_wo)
    chain_wq = line(3 * count, summed_wq, sems, 25, (up_wq, cross_wq, held_wq), place_wq)

    def feed_turn(turn):
        chain_w2.step(turn)

    attn_grad = middle_grad[...] * pk_ref[4:5]
    attn_all[mine, :] = attn_grad.astype(BF16)
    gather.start()
    sent = []
    def swapping(step):
        other = partner(me, step, count)
        return post(pair_w1.at[other], swapped_w1.at[me], sems, SWAP1, step, {"shard": other})

    swapped_w1[me] = pair_w1[me]
    sums[1:2, :] = sums_in[0:1, :]
    sums[3:4, :] = sums_in[1:2, :]
    sums[4:5, :] = column_sum(middle_grad[...] * attn_ref[...])
    sums[6:7, :] = column_sum(attn_grad)
    sums[7:8, :] = column_sum(up_ref[...].astype(F32) * pk_ref[5:6])
    dk[...] = jnp.zeros_like(dk)
    dv[...] = jnp.zeros_like(dv)
    live = live_keys(local_len, rows, total)

    def attending(step, carry):
        there = spot(partner(me, step, count), rows)

        gather.arrive(step)

        @pl.when(step == min(1, count - 1))
        def _():
            for other in range(1, count):
                swapping(other).start()

        @pl.when(step == min(2, count - 1))
        def _():
            for other in range(count - 1, 0, -1):
                scatter_two.send(other, branch[other].astype(F32), False)

        grad = back_dot(attn_all[there, :], wo_ref[...]).astype(BF16)
        attend_rows_back(
            size,
            there,
            live,
            project,
            mixed,
            stat,
            grad,
            joined,
            dk,
            dv,
            lambda head: feed_turn(step * heads + head),
        )
        return carry

    lax.fori_loop(0, count, attending, 0)
    lead(chain_w1)
    turned = jnp.transpose(dv[...])
    joined[:, owned : 2 * owned] = jnp.transpose(dk[...]).astype(BF16)
    joined[:, 2 * owned :] = turned.astype(BF16)
    flat[8:9, :] = column_sum(joined[:, 0:owned].astype(F32))
    flat[9:10, :] = column_sum(turned)

    product = row_dot(mixed[...], attn_all[...]).astype(BF16)
    grad_wo[0] = product[:half].reshape(grad_wo.shape[1:])
    grad_wo[1] = product[half:].reshape(grad_wo.shape[1:])
    pair_wo = post(grad_wo.at[1 - core], other_wo, sems, PAIR, 0, {"rep": mate})
    pair_wo.start()

    def weighing(number, carry):
        columns = pl.ds(pl.multiple_of(number * owned, 128), owned)
        product = row_dot(first_all[:, columns], joined[...]).astype(BF16)
        grad_wq[0, number] = product[:half]
        grad_wq[1, number] = product[half:]
        return carry

    lax.fori_loop(0, count, weighing, 0)
    pair_wq = post(grad_wq.at[1 - core], other_wq, sems, PAIR, 1, {"rep": mate})
    pair_wq.start()
    def returning(turn, carry):
        step = count - 1 - turn
        there = spot(partner(me, step, count), rows)
        result = back_dot(joined[there, :], wq[...])

        @pl.when(step > 0)
        def _():
            scatter.send(step, result, False)

        @pl.when(step == 0)
        def _():
            own[...] = result

        return carry

    lax.fori_loop(0, count, returning, 0)
    pair_wo.wait()
    pair_wq.wait()
    grad_wq[core] = (grad_wq[core].astype(F32) + other_wq[...].astype(F32)).astype(BF16)
    for step in range(1, count):
        other = partner(me, step, count)
        copy = post(
            grad_wq.at[core, other], swapped_wq.at[me], sems, SWAPQ, step, {"shard": other}
        )
        copy.start()
        sent.append(copy)
    swapped_wq[me] = grad_wq[core, me]
    lax.fori_loop(count * heads, chain_w2.turns(), lambda turn, carry: (feed_turn(turn), carry)[1], 0)
    lead(chain_wo)
    follow(chain_w1)
    if count == 4:
        for near in (1, 2):
            scatter.combine(near)
            scatter_two.combine(near)
    lead(chain_wq)
    follow(chain_wo)
    for step in range(1, count):
        swapping(step).wait_send()
    result = scatter.total(own[...])
    normed, inverse = norm_parts(tok_ref[...].astype(F32))
    sums[0:1, :] = column_sum(result * normed)
    sums[2:3, :] = column_sum(result)
    outgoing[...] = middle_grad[...] + norm_backward(result, normed, inverse, pk_ref[0:1])
    result = branch[0].astype(F32) + pk_ref[7:8]
    result = scatter_two.total(result)
    output[...] = (middle_ref[...] + pk_ref[5:6] * result).astype(BF16)
    sums[5:6, :] = column_sum(up_ref[...].astype(F32) * result)

    own_cols = pl.ds(pl.multiple_of(me * owned, 128), owned)
    for step in range(1, count):
        other = partner(me, step, count)
        copy = post(
            sums.at[:, pl.ds(pl.multiple_of(other * owned, 128), owned)],
            sums_by.at[me],
            sems,
            SMALL,
            step,
            {"shard": other},
        )
        copy.start()
        sent.append(copy)
    sums_by[me] = sums[:, own_cols]

    follow(chain_wq)
    for step in range(1, count):
        other = partner(me, step, count)
        post(sums_by.at[other], sums_by.at[other], sems, SMALL, step, {"shard": me}).wait_recv()
    flat[0:8, :] = functools.reduce(lambda left, right: left + right, [sums_by[i] for i in range(count)])
    flat[10:, :] = bias_rows[...]
    flat_by[rep] = flat[...]
    for step in range(1, reps):
        copy = post(
            flat, flat_by.at[rep], sems, FLAT, step, {"rep": lax.rem(rep + step, reps)}
        )
        copy.start()
        sent.append(copy)
    for copy in sent:
        copy.wait_send()
    for step in range(1, reps):
        source = lax.rem(rep + reps - step, reps)
        post(flat_by.at[source], flat_by.at[source], sems, FLAT, step, {"shard": me}).wait_recv()
    flat[...] = functools.reduce(lambda left, right: left + right, [flat_by[i] for i in range(reps)])
    for done in (gather, scatter, scatter_two, chain_w2, chain_w1, chain_wo, chain_wq):
        done.finish()


def call(body, number, name, operands, outs, scratch, kinds, flops):
    return pl.pallas_call(
        body,
        in_specs=[VMEM] * len(operands),
        out_specs=[VMEM] * len(outs),
        out_shape=[jax.ShapeDtypeStruct(*out) for out in outs],
        scratch_shapes=[pltpu.VMEM(*item) for item in scratch]
        + [pltpu.SemaphoreType.DMA(kinds), pltpu.SemaphoreType.DMA(kinds)],
        compiler_params=pltpu.CompilerParams(
            collective_id=number, has_side_effects=True, vmem_limit_bytes=60 * 1024 * 1024
        ),
        cost_estimate=pl.CostEstimate(flops=flops, bytes_accessed=2**24, transcendentals=2**22),
        name=name,
    )(*operands)


def local(
    tokens,
    cotangent,
    slot_live,
    w_qkv,
    w_out,
    w_fc1,
    w_fc2,
    norm_gain,
    norm_bias,
    layer_scale,
    qv_bias,
    proj_bias,
    fc1_bias,
):
    count = lax.axis_size("shard")
    me = lax.axis_index("shard")
    _, local_len, model = tokens.shape
    owned = model // count
    units = w_fc2.shape[1]
    hidden_units = w_fc1.shape[2]
    size = model // HEADS
    rows = -(-local_len // 16) * 16
    extra = rows - local_len
    total = rows * count

    tok = jnp.pad(tokens[0], ((0, extra), (0, 0)))
    place = jnp.arange(rows, dtype=jnp.int32)
    valid = (slot_live[0] > 0) & (place < local_len) & (me * local_len + place < LEN)
    up = jnp.where(valid[:, None], jnp.pad(cotangent[0], ((0, extra), (0, 0))), 0).astype(BF16)
    packed = jnp.concatenate([norm_gain[0], norm_bias[0], layer_scale[0], proj_bias[0]], axis=0)
    packed = packed.astype(F32)
    qv = qv_bias[0].astype(F32)
    bias_row = jnp.concatenate([qv[0], jnp.zeros_like(qv[0]), qv[1]])[None]

    big = (total, model)
    small = (rows, model)
    half = owned // 2
    wide_one = (count, half, units)
    wide_two = (2 * count, units // 4 // count, model)
    wide_half = (2 * count, half // 2, units)
    wide_q = (count, half, 3 * owned)
    wide_o = (count, half // count, model)
    (
        first_all,
        wq,
        project,
        mixed,
        stat,
        attn,
        pk_all,
        middle,
        middle_grad,
        branch,
        pair_w1,
        pair_w2,
        grad_b1,
        sums,
    ) = call(
        functools.partial(early_kernel, count, size, local_len),
        0,
        "forward_and_feed",
        (
            tok,
            up,
            packed,
            w_qkv[0],
            w_out[0],
            w_fc1[0],
            bias_row,
            w_fc2[0],
            fc1_bias.astype(F32),
        ),
        (
            (big, BF16),
            ((model, 3 * owned), BF16),
            ((total, 3 * owned), BF16),
            ((total, owned), BF16),
            ((total, 128), F32),
            (small, F32),
            ((8, model), F32),
            (small, F32),
            (small, F32),
            ((count, *small), BF16),
            (wide_one, BF16),
            ((units // 2, model), BF16),
            ((1, units), F32),
            ((8, model), F32),
        ),
        (
            (big, BF16),
            ((model, units), BF16),
            *passing(count, *small),
            ((2, *wide_one), BF16),
            ((2, units // 2, model), BF16),
            (wide_one, BF16),
            ((units // 2, model), BF16),
            (big, BF16),
            ((total, units), BF16),
            ((total, units), BF16),
            *passing(count, *small),
            (small, F32),
        ),
        (20, count),
        2 * 10**10,
    )
    reps = lax.axis_size("rep")
    extra_rows = units // owned
    flat_rows = -(-(10 + extra_rows) // 8) * 8
    bias_rows = jnp.pad(
        grad_b1.reshape(extra_rows, owned), ((0, flat_rows - 10 - extra_rows), (0, 0))
    )
    output, outgoing, total_w1, total_w2, total_wq, total_wo, flat = call(
        functools.partial(last_kernel, count, size, local_len),
        2,
        "attend_backward",
        (
            tok,
            up,
            attn,
            pk_all,
            middle,
            middle_grad,
            branch,
            sums,
            first_all,
            project,
            mixed,
            stat,
            w_out[0],
            wq,
            pair_w1,
            pair_w2.reshape(wide_two),
            bias_rows,
        ),
        (
            (small, BF16),
            (small, F32),
            ((owned, hidden_units), BF16),
            ((units, model), BF16),
            ((owned, 3 * model), BF16),
            ((owned, model), BF16),
            ((flat_rows, owned), F32),
        ),
        (
            (big, BF16),
            ((total, 3 * owned), BF16),
            ((owned, total), F32),
            ((owned, total), F32),
            *passing(count, *small),
            *passing(count, *small),
            (small, F32),
            (wide_one, BF16),
            *([(wide_half, BF16)] * 3),
            *([(wide_two, BF16)] * 3),
            (wide_q, BF16),
            *([((3 * count, half, owned), BF16)] * 3),
            *([(wide_o, BF16)] * 3),
            ((2, *wide_q), BF16),
            ((2, *wide_o), BF16),
            (wide_q, BF16),
            (wide_o, BF16),
            ((8, model), F32),
            ((count, 8, owned), F32),
            ((reps, flat_rows, owned), F32),
        ),
        (29, max(3 * count, reps)),
        10**10,
    )
    return (
        output[:local_len][None],
        outgoing[:local_len][None],
        total_wq.astype(F32)[None],
        total_wo.astype(F32)[None],
        total_w1.astype(F32)[None],
        total_w2.astype(F32)[None],
        flat[0:2][None],
        flat[2:4][None],
        flat[4:6][None],
        flat[8:10][None],
        flat[6:8][None],
        flat[10 : 10 + extra_rows].reshape(1, -1),
    )


def solution(mesh):
    rows = P("rep", "shard", None)
    matrix = P(None, "shard", None)
    vector = P(None, None, "shard")
    return jax.shard_map(
        local,
        mesh=mesh,
        in_specs=(rows, rows, P("rep"), *([matrix] * 4), *([vector] * 5), P(None, "shard")),
        out_specs=(rows, rows, *([matrix] * 4), *([vector] * 5), P(None, "shard")),
        check_vma=False,
    )
```

```python
import functools
import math

import jax
import jax.numpy as jnp
from jax import lax
from jax.experimental import pallas as pl
from jax.experimental.pallas import tpu as pltpu
from jax.sharding import PartitionSpec as P

HEADS = 16
LEN = 1025
EPSILON = 1e-06
F32 = jnp.float32
BF16 = jnp.bfloat16
MESH = pl.DeviceIdType.MESH
HOP = 2
VMEM = pl.BlockSpec(memory_space=pltpu.VMEM)


def norm_parts(hidden):
    center = hidden - jnp.mean(hidden, axis=-1, keepdims=True)
    inverse = lax.rsqrt(jnp.mean(center * center, axis=-1, keepdims=True) + EPSILON)
    return (center * inverse, inverse)


def norm_backward(incoming, normed, inverse, gain):
    scaled = incoming * gain
    return inverse * (
        scaled
        - jnp.mean(scaled, axis=-1, keepdims=True)
        - normed * jnp.mean(scaled * normed, axis=-1, keepdims=True)
    )


def gelu_pair(values):
    cumulative = 0.5 * (1.0 + lax.erf(values * 0.7071067811865476))
    slope = cumulative + values * jnp.exp(-0.5 * values * values) * 0.3989422804014327
    return (values * cumulative, slope)


def plain_dot(left, right):
    return jnp.dot(left, right, preferred_element_type=F32)


def row_dot(left, right):
    return lax.dot_general(left, right, (((0,), (0,)), ((), ())), preferred_element_type=F32)


def back_dot(left, right):
    return lax.dot_general(left, right, (((1,), (1,)), ((), ())), preferred_element_type=F32)


def head_parts(size, width):
    lane = lax.broadcasted_iota(jnp.int32, (1, width), 1)
    return [
        ((lane >= size * number) & (lane < size * (number + 1))) for number in range(width // size)
    ]


def column_sum(values):
    return jnp.sum(values, axis=0, keepdims=True)


def partner(me, step, count):
    other, bit = me, 1
    while bit < count:
        other = other + ((step // bit) % 2) * (1 - 2 * ((me // bit) % 2)) * bit
        bit *= 2
    return other


def spot(index, rows):
    return pl.ds(pl.multiple_of(index * rows, math.gcd(rows, 1024)), rows)


def greet(me, count, others=()):
    barrier = pltpu.get_barrier_semaphore()
    for step in range(1, count):
        pl.semaphore_signal(
            barrier, 1, device_id={"shard": partner(me, step, count)}, device_id_type=MESH
        )
    for other in others:
        pl.semaphore_signal(barrier, 1, device_id={"rep": other}, device_id_type=MESH)
    pl.semaphore_wait(barrier, count - 1 + len(others))


def post(source, target, sems, kind, step, where):
    return pltpu.make_async_remote_copy(
        source,
        target,
        sems[0].at[kind, step],
        sems[1].at[kind, step],
        device_id=where,
        device_id_type=MESH,
    )


def score(queries, keys, live):
    return jnp.where(live, back_dot(queries, keys), -1e30)


def attend_rows(size, here, live, project, mixed, stat):
    owned = mixed.shape[1]
    width = min(max(128, size), owned)
    factor = 1.0 / math.sqrt(size)
    for pair in range(owned // width):
        columns = slice(pair * width, (pair + 1) * width)
        queries = project[here, columns]
        keys = project[:, owned + pair * width : owned + (pair + 1) * width]
        values = project[:, 2 * owned + pair * width : 2 * owned + (pair + 1) * width]
        out = jnp.zeros(queries.shape, F32)
        for number, part in enumerate(head_parts(size, width)):
            own = (jnp.where(part, queries, 0) * factor).astype(BF16)
            scores = score(own, keys, live)
            top = jnp.max(scores, axis=-1, keepdims=True)
            power = jnp.exp(scores - top)
            total = jnp.sum(power, axis=-1, keepdims=True)
            product = plain_dot(power.astype(BF16), values) * (1.0 / total)
            out = jnp.where(part, product, out)
            place = pair * (width // size) + number
            stat[here, place : place + 1] = top + jnp.log(total)
        mixed[here, columns] = out.astype(BF16)


def attend_rows_back(size, here, live, project, mixed, stat, grad, joined, dk, dv, between):
    owned = mixed.shape[1]
    width = min(max(128, size), owned)
    factor = 1.0 / math.sqrt(size)
    for pair in range(owned // width):
        columns = slice(pair * width, (pair + 1) * width)
        queries = project[here, columns]
        keys = project[:, owned + pair * width : owned + (pair + 1) * width]
        values = project[:, 2 * owned + pair * width : 2 * owned + (pair + 1) * width]
        grads = grad[:, columns]
        overlap = grads.astype(F32) * mixed[here, columns].astype(F32)
        turned_q = jnp.transpose(queries.astype(F32) * factor).astype(BF16)
        turned_g = jnp.transpose(grads.astype(F32)).astype(BF16)
        dq = jnp.zeros(queries.shape, F32)
        for number, part in enumerate(head_parts(size, width)):
            place = pair * (width // size) + number
            own_q = (jnp.where(part, queries, 0) * factor).astype(BF16)
            own_g = jnp.where(part, grads, 0).astype(BF16)
            weights = jnp.exp(score(own_q, keys, live) - stat[here, place : place + 1])
            delta = jnp.sum(jnp.where(part, overlap, 0), axis=-1, keepdims=True)
            slope = (weights * (back_dot(own_g, values) - delta)).astype(BF16)
            span = slice(place * size, (place + 1) * size)
            inner = slice(number * size, (number + 1) * size)
            dk[span, :] += plain_dot(turned_q[inner], slope)
            dv[span, :] += plain_dot(turned_g[inner], weights.astype(BF16))
            dq = jnp.where(part, plain_dot(slope, keys), dq)
            between(place)
        joined[here, columns] = (dq * factor).astype(BF16)


class Gather:
    def __init__(self, array, rows, me, count, sems, kind):
        self.array, self.rows, self.me, self.count = array, rows, me, count
        self.sems, self.kind, self.square = sems, kind, count == 4
        self.steps = (1, 2) if self.square else tuple(range(1, count))
        self.half = array.shape[1] // 2

    def direct(self, owner, step):
        block = self.array.at[spot(owner, self.rows)]
        where = {"shard": partner(self.me, step, self.count)}
        return post(block, block, self.sems, self.kind, step, where)

    def relay(self, owner, step):
        columns = pl.ds((step - 1) * self.half, self.half)
        block = self.array.at[spot(owner, self.rows), columns]
        where = {"shard": partner(self.me, 3 - step, self.count)}
        return post(block, block, self.sems, self.kind + 1, step, where)

    def start(self):
        for step in self.steps:
            self.direct(self.me, step).start()

    def arrive(self, step):
        if not self.square:

            @pl.when(step > 0)
            def _():
                self.direct(partner(self.me, step, self.count), step).wait_recv()

            return

        @pl.when(step == 1)
        def _():
            for near in (1, 2):
                owner = partner(self.me, near, 4)
                self.direct(owner, near).wait_recv()
                self.relay(owner, near).start()

        @pl.when(step == 3)
        def _():
            for near in (1, 2):
                self.relay(partner(self.me, 3, 4), near).wait_recv()

    def finish(self):
        for step in self.steps:
            self.direct(self.me, step).wait_send()
            if self.square:
                self.relay(partner(self.me, step, 4), step).wait_send()


class Scatter:
    def __init__(self, part, landed, via, me, count, sems, kind):
        self.part, self.landed, self.via, self.me, self.count = part, landed, via, me, count
        self.sems, self.kind, self.square = sems, kind, count == 4
        self.steps = (1, 2) if self.square else tuple(range(1, count))
        self.half = part.shape[2] // 2

    def direct(self, step, side=0):
        source, target = self.part.at[step - 1], self.landed.at[step - 1]
        if self.square:
            columns = pl.ds(side * self.half, self.half)
            source, target = source.at[:, columns], target.at[:, columns]
        where = {"shard": partner(self.me, step, self.count)}
        return post(source, target, self.sems, self.kind + 2 * side, step, where)

    def early(self, near):
        return post(
            self.part.at[2, :, pl.ds((near - 1) * self.half, self.half)],
            self.via.at[near - 1],
            self.sems,
            self.kind + 1,
            near,
            {"shard": partner(self.me, near, 4)},
        )

    def send(self, step, value, ready=True):
        if not self.square:
            self.part[step - 1] = value.astype(BF16)
            self.direct(step).start()
            return
        self.part[step - 1] = value.astype(BF16)

        @pl.when(step == 3)
        def _():
            for near in (1, 2):
                self.early(near).start()

        for near in (1, 2):

            @pl.when(step == near)
            def _():
                self.direct(near, near - 1).start()
                if ready:
                    side = 2 - near
                    self.combine(near, value[:, side * self.half : (side + 1) * self.half])

    def combine(self, near, value=None):
        side = 2 - near
        columns = slice(side * self.half, (side + 1) * self.half)
        if value is None:
            value = self.part[near - 1, :, columns].astype(F32)
        self.early(3 - near).wait_recv()
        self.part[near - 1, :, columns] = (value + self.via[side].astype(F32)).astype(BF16)
        self.direct(near, side).start()

    def total(self, value):
        for step in self.steps:
            for side in range(2 if self.square else 1):
                self.direct(step, side).wait_recv()
            value += self.landed[step - 1].astype(F32)
        return value

    def finish(self):
        for step in self.steps:
            for side in range(2 if self.square else 1):
                self.direct(step, side).wait_send()
            if self.square:
                self.early(step).wait_send()


def passing(count, rows, model):
    slots = 2 if count == 4 else count - 1
    return [
        ((count - 1, rows, model), BF16),
        ((slots, rows, model), BF16),
        ((2, rows, model // 2), BF16),
    ]


class Chain:
    def __init__(self, rep, chips, parts, own, sems, kind, scratch, total):
        self.parts, self.own, self.sems, self.kind = parts, own, sems, kind
        self.up, self.cross, self.held = scratch
        self.total = total
        core, chip = rep % 2, rep // 2
        side = chip // (chips // 2)
        self.core, self.last = core, chips // 2 - 1
        self.depth = side * (chips - 1 - chip) + (1 - side) * chip
        ahead = 1 - 2 * side
        self.inner = {"rep": (chip + ahead) * 2 + core}
        self.outer = {"rep": (chip - ahead) * 2 + core}
        self.mate = {"rep": rep + 1 - 2 * core}

    def copy(self, which, part):
        where = (self.inner, self.inner, self.outer, self.mate)[which]
        final = self.total(self.core, part)
        source = self.held.at[part] if which < 2 else final
        target = (self.up.at[part], self.cross.at[part], final, final)[which]
        return post(source, target, self.sems, self.kind + which, part, where)

    def reduce(self, part):
        depth, last = self.depth, self.last
        value = self.own(part)

        @pl.when(depth == 0)
        def _():
            self.held[part] = value.astype(BF16)

        if last > 0:

            @pl.when(depth > 0)
            def _():
                self.copy(0, part).wait_recv()
                self.held[part] = (value + self.up[part].astype(F32)).astype(BF16)

            @pl.when(depth < last)
            def _():
                self.copy(0, part).start()

        @pl.when(depth == last)
        def _():
            self.copy(1, part).start()

    def result(self, part):
        depth, last = self.depth, self.last

        @pl.when(depth == last)
        def _():
            self.copy(1, part).wait_recv()
            both = self.held[part].astype(F32) + self.cross[part].astype(F32)
            self.total(self.core, part)[...] = both.astype(BF16)

        if last > 0:

            @pl.when(depth < last)
            def _():
                self.copy(2, part).wait_recv()

            @pl.when(depth > 0)
            def _():
                self.copy(2, part).start()

        self.copy(3, part).start()

    def within(self, part, act):
        @pl.when((part >= 0) & (part < self.parts))
        def _():
            act(part)

    def step(self, turn):
        self.within(turn - HOP * self.depth, self.reduce)
        self.within(turn - HOP * (2 * self.last + 1 - self.depth), self.result)

    def turns(self):
        return self.parts + HOP * (2 * self.last + 1)

    def finish(self):
        def closing(part, carry):
            if self.last > 0:

                @pl.when(self.depth < self.last)
                def _():
                    self.copy(0, part).wait_send()

                @pl.when(self.depth > 0)
                def _():
                    self.copy(2, part).wait_send()

            @pl.when(self.depth == self.last)
            def _():
                self.copy(1, part).wait_send()

            final = self.total(1 - self.core, part)
            self.copy(3, part).wait_send()
            post(final, final, self.sems, self.kind + 3, part, self.mate).wait_recv()
            return carry

        lax.fori_loop(0, self.parts, closing, 0)


def loop(count, act):
    def body(part, carry):
        act(part)
        return carry

    lax.fori_loop(0, count, body, 0)


def lead(chain):
    @pl.when(chain.depth == 0)
    def _():
        loop(chain.parts, chain.reduce)


def follow(chain, lag=2):
    @pl.when(chain.depth == 0)
    def _():
        loop(chain.parts, chain.result)

    if chain.last > 0:

        @pl.when(chain.depth > 0)
        def _():
            def both(part):
                chain.within(part, chain.reduce)
                chain.within(part - lag, chain.result)

            loop(chain.parts + lag, both)


def live_keys(local_len, rows, total):
    place = lax.broadcasted_iota(jnp.int32, (1, total), 1)
    inner = place % rows
    return (inner < local_len) & ((place // rows) * local_len + inner < LEN)


def early_kernel(
    count,
    size,
    local_len,
    raw_ref,
    raw_up,
    live_ref,
    pk_ref,
    wqkv_ref,
    wo_ref,
    w1_ref,
    bias_ref,
    w2_ref,
    fc1_bias,
    tok_ref,
    up_ref,
    first_all,
    wq,
    project,
    mixed,
    stat,
    attn,
    pk_all,
    middle_out,
    middle_grad,
    branch,
    pair_w1,
    pair_w2,
    grad_bias,
    sums,
    fc2_all,
    w1c,
    part,
    landed,
    via,
    grad_w1,
    grad_w2,
    other_w1,
    other_w2,
    second_all,
    pre_in,
    act,
    part_two,
    landed_two,
    via_two,
    own,
    send_sem,
    recv_sem,
):
    sems = (send_sem, recv_sem)
    me, rep = lax.axis_index("shard"), lax.axis_index("rep")
    core = rep % 2
    mate = rep + 1 - 2 * core
    rows, model = tok_ref.shape
    owned = pk_ref.shape[1]
    units = w1c.shape[1]
    half = owned // 2
    greet(me, count, (mate,))

    own_cols = pl.ds(pl.multiple_of(me * owned, 128), owned)
    own_rows = pl.ds(pl.multiple_of(me * owned, 16), owned)
    mine = spot(me, rows)
    ours = pl.ds(pl.multiple_of(core * half, 16), half)
    pk_all[:, own_cols] = pk_ref[...]
    PK, FIRST, FC2, W1, WQ, FQ, F1, SUM = 0, 1, 3, 5, 6, 9, 10, 11
    gather_first = Gather(first_all, rows, me, count, sems, FIRST)
    gather_fc2 = Gather(fc2_all, rows, me, count, sems, FC2)
    scatter = Scatter(part, landed, via, me, count, sems, SUM)
    sent = []

    def block(source):
        return pl.ds(pl.multiple_of(source * owned + core * half, 16), half)

    def push(source, target, kind, step):
        copy = post(source, target, sems, kind, step, {"shard": partner(me, step, count)})
        copy.start()
        sent.append(copy)

    def hand(target, kind, step):
        copy = post(target, target, sems, kind, step, {"rep": mate})
        copy.start()
        sent.append(copy)
        return copy

    for step in range(1, count):
        push(pk_ref, pk_all.at[:, own_cols], PK, step)
    for step in range(1, count):
        other = partner(me, step, count)
        for third in range(3):
            push(
                wqkv_ref.at[ours, pl.ds(pl.multiple_of(third * model + other * owned, 128), owned)],
                wq.at[block(me), third * owned : (third + 1) * owned],
                WQ + third,
                step,
            )
    own[...] = jnp.zeros_like(own)
    own[0:local_len, :] = raw_ref[...].astype(F32)
    tok_ref[...] = own[...].astype(BF16)
    hidden = tok_ref[...].astype(F32)
    normed, _ = norm_parts(hidden)
    for step in range(1, count):
        other = pl.ds(pl.multiple_of(partner(me, step, count) * owned, 128), owned)
        post(pk_ref, pk_all.at[:, other], sems, PK, step, {"rep": mate}).wait_recv()
    first_all[mine, :] = (normed * pk_all[0:1] + pk_all[2:3]).astype(BF16)
    gather_first.start()
    for third in range(3):
        columns = pl.ds(pl.multiple_of(third * model + me * owned, 128), owned)
        wq[own_rows, third * owned : (third + 1) * owned] = wqkv_ref[:, columns]
    w1c[own_rows, :] = w1_ref[:, pl.ds(pl.multiple_of(me * units, 128), units)]
    own[0:local_len, :] = raw_up[...].astype(F32)
    place = lax.broadcasted_iota(jnp.int32, (rows, 1), 0)
    valid = (place < local_len) & (me * local_len + place < LEN) & (live_ref[0:1, 0:1] > 0.5)
    up_ref[...] = jnp.where(valid, own[...], 0.0).astype(BF16)
    fc2_all[mine, :] = (up_ref[...].astype(F32) * pk_all[5:6]).astype(BF16)

    handed = []
    for step in range(1, count):
        other = partner(me, step, count)
        for third in range(3):
            columns = slice(third * owned, (third + 1) * owned)
            post(
                wq.at[block(other), columns],
                wq.at[block(other), columns],
                sems,
                WQ + third,
                step,
                {"rep": mate},
            ).wait_recv()
        handed.append(hand(wq.at[block(other)], FQ, step))
    for copy in handed:
        copy.wait_recv()

    def shifting(step):
        other = partner(me, step, count)
        columns = pl.ds(pl.multiple_of(other * units, 128), units)
        where = {"shard": other}
        return post(w1_ref.at[ours, columns], w1c.at[block(me)], sems, W1, step, where)

    def projecting(step, carry):
        there = spot(partner(me, step, count), rows)

        gather_first.arrive(step)

        @pl.when(step == min(1, count - 1))
        def _():
            for other in range(1, count):
                shifting(other).start()

        project[there, :] = (plain_dot(first_all[there, :], wq[...]) + bias_ref[...]).astype(BF16)
        return carry

    lax.fori_loop(0, count, projecting, 0)
    gather_fc2.start()
    live = live_keys(local_len, rows, project.shape[0])

    def attending(turn, carry):
        step = count - 1 - turn
        there = spot(partner(me, step, count), rows)

        if count == 4:

            @pl.when(turn == count - 2)
            def _():
                gather_fc2.arrive(1)

        attend_rows(size, there, live, project, mixed, stat)
        result = plain_dot(mixed[there, :], wo_ref[...])

        @pl.when(step > 0)
        def _():
            scatter.send(step, result)

        @pl.when(step == 0)
        def _():
            attn[...] = result

        return carry

    lax.fori_loop(0, count, attending, 0)
    for step in range(1, count):
        other = block(partner(me, step, count))
        post(w1c.at[other], w1c.at[other], sems, W1, step, {"rep": mate}).wait_recv()
        handed.append(hand(w1c.at[other], F1, step))
    attn[...] = scatter.total(attn[...] + pk_all[6:7])
    tile = min(256, units)
    SECOND, SUM, PAIR = 14, 16, 19
    gather = Gather(second_all, rows, me, count, sems, SECOND)
    scatter_two = Scatter(part_two, landed_two, via_two, me, count, sems, SUM)
    middle = tok_ref[...].astype(F32) + pk_all[4:5] * attn[...]
    middle_out[...] = middle
    normed, _ = norm_parts(middle)
    second_all[mine, :] = (normed * pk_all[1:2] + pk_all[3:4]).astype(BF16)
    gather.start()
    grad_bias[...] = jnp.zeros_like(grad_bias)
    for copy in handed[count - 1 :]:
        copy.wait_recv()

    def feeding(step, carry):
        there = spot(partner(me, step, count), rows)

        gather.arrive(step)
        if count == 4:

            @pl.when(step > 1)
            def _():
                gather_fc2.arrive(step)

        else:
            gather_fc2.arrive(step)

        def tiles(number, inner):
            columns = pl.ds(pl.multiple_of(number * tile, 128), tile)
            pre = plain_dot(second_all[there, :], w1c[:, columns]) + fc1_bias[:, columns]
            value, slope = gelu_pair(pre)
            act[there, columns] = value.astype(BF16)
            back = back_dot(
                fc2_all[there, :], w2_ref[pl.ds(pl.multiple_of(number * tile, 16), tile), :]
            )
            back = back * slope
            grad_bias[:, columns] += column_sum(back)
            pre_in[there, columns] = back.astype(BF16)
            return inner

        lax.fori_loop(0, units // tile, tiles, 0)
        result = back_dot(pre_in[there, :], w1c[...])

        @pl.when(step > 0)
        def _():
            scatter_two.send(step, result, False)

        @pl.when(step == 0)
        def _():
            own[...] = result

        return carry

    lax.fori_loop(0, count, feeding, 0)

    def branching(step, carry):
        there = spot(partner(me, step, count), rows)
        branch[step] = plain_dot(act[there, :], w2_ref[...]).astype(BF16)
        return carry

    lax.fori_loop(0, count, branching, 0)
    if count == 4:
        for near in (1, 2):
            scatter_two.combine(near)

    def weighing_two(number, carry):
        columns = pl.ds(pl.multiple_of(number * tile, 128), tile)
        here = pl.ds(pl.multiple_of(lax.rem(number, halves) * tile, 16), tile)
        grad_w2[number // halves, here, :] = row_dot(act[:, columns], fc2_all[...]).astype(BF16)
        return carry

    halves = units // tile // 2
    lax.fori_loop(0, units // tile, weighing_two, 0)
    copies = [post(grad_w2.at[1 - core], other_w2, sems, PAIR, 0, {"rep": mate})]
    copies[0].start()

    def weighing_one(number, carry):
        columns = pl.ds(pl.multiple_of(number * owned, 128), owned)
        product = row_dot(second_all[:, columns], pre_in[...]).astype(BF16)
        grad_w1[0, number] = product[:half]
        grad_w1[1, number] = product[half:]
        return carry

    lax.fori_loop(0, count, weighing_one, 0)
    copies.append(post(grad_w1.at[1 - core], other_w1, sems, PAIR, 1, {"rep": mate}))
    copies[1].start()
    for copy in copies:
        copy.wait()
    pair_w2[...] = (grad_w2[core].astype(F32) + other_w2[...].astype(F32)).astype(BF16)
    pair_w1[...] = (grad_w1[core].astype(F32) + other_w1[...].astype(F32)).astype(BF16)

    result = scatter_two.total(own[...])
    normed, inverse = norm_parts(middle_out[...])
    sums[0:1, :] = column_sum(result * normed)
    sums[1:2, :] = column_sum(result)
    middle_grad[...] = up_ref[...].astype(F32) + norm_backward(
        result, normed, inverse, pk_all[1:2]
    )
    for done in (gather_first, gather_fc2, gather, scatter, scatter_two):
        done.finish()
    for step in range(1, count):
        shifting(step).wait_send()
    for copy in sent:
        copy.wait_send()


def last_kernel(
    count,
    size,
    local_len,
    tok_ref,
    up_ref,
    attn_ref,
    pk_ref,
    middle_ref,
    middle_grad,
    branch,
    sums_in,
    first_all,
    project,
    mixed,
    stat,
    wo_ref,
    wq,
    pair_w1,
    pair_w2,
    bias_rows,
    output,
    outgoing,
    total_w1,
    total_w2,
    total_wq,
    total_wo,
    flat,
    attn_all,
    joined,
    dk,
    dv,
    part,
    landed,
    via,
    part_two,
    landed_two,
    via_two,
    own,
    swapped_w1,
    up_w1,
    cross_w1,
    held_w1,
    up_w2,
    cross_w2,
    held_w2,
    swapped_wq,
    up_wq,
    cross_wq,
    held_wq,
    up_wo,
    cross_wo,
    held_wo,
    grad_wq,
    grad_wo,
    other_wq,
    other_wo,
    sums,
    sums_by,
    flat_by,
    send_sem,
    recv_sem,
):
    sems = (send_sem, recv_sem)
    me = lax.axis_index("shard")
    rows, model = tok_ref.shape
    total, owned = mixed.shape
    mine = spot(me, rows)
    GRAD, BRANCH, SUM, SWAP1, SWAPQ, PAIR, SMALL, FLAT = 0, 2, 5, 8, 9, 10, 11, 12
    gather = Gather(attn_all, rows, me, count, sems, GRAD)
    scatter = Scatter(part, landed, via, me, count, sems, SUM)
    scatter_two = Scatter(part_two, landed_two, via_two, me, count, sems, BRANCH)
    rep, reps = lax.axis_index("rep"), lax.axis_size("rep")
    core = rep % 2
    mate = rep + 1 - 2 * core
    half = owned // 2
    heads = owned // size
    greet(me, count, [lax.rem(rep + other, reps) for other in range(1, reps)])

    def summed_w2(number):
        return pair_w2[number].astype(F32)

    def summed_w1(part):
        number = part // 2
        step = partner(me, number, count)

        @pl.when((step > 0) & (lax.rem(part, 2) == 0))
        def _():
            post(
                swapped_w1.at[number], swapped_w1.at[number], sems, SWAP1, step, {"shard": me}
            ).wait_recv()

        return swapped_w1[number, spot(lax.rem(part, 2), half // 2)].astype(F32)

    def summed_wq(number):
        source, third = number // 3, lax.rem(number, 3)
        step = partner(me, source, count)

        @pl.when((step > 0) & (third == 0))
        def _():
            post(
                swapped_wq.at[source], swapped_wq.at[source], sems, SWAPQ, step, {"shard": me}
            ).wait_recv()

        columns = pl.ds(pl.multiple_of(third * owned, 128), owned)
        return swapped_wq[source, :, columns].astype(F32)

    def summed_wo(number):
        return grad_wo[core, number].astype(F32) + other_wo[number].astype(F32)

    def place_w1(part, number):
        rows_here = spot(part * 2 + lax.rem(number, 2), half // 2)
        return total_w1.at[rows_here, pl.ds(pl.multiple_of((number // 2) * units, 128), units)]

    def place_w2(part, number):
        return total_w2.at[spot(part * 2 * count + number, pair_w2.shape[1])]

    def place_wq(part, number):
        column = lax.rem(number, 3) * model + (number // 3) * owned
        rows_here = pl.ds(pl.multiple_of(part * half, 16), half)
        return total_wq.at[rows_here, pl.ds(pl.multiple_of(column, 128), owned)]

    def place_wo(part, number):
        return total_wo.at[spot(part * count + number, half // count)]

    units = pair_w1.shape[2]
    line = functools.partial(Chain, rep, reps // 2)
    chain_w2 = line(2 * count, summed_w2, sems, 13, (up_w2, cross_w2, held_w2), place_w2)
    chain_w1 = line(2 * count, summed_w1, sems, 17, (up_w1, cross_w1, held_w1), place_w1)
    chain_wo = line(count, summed_wo, sems, 21, (up_wo, cross_wo, held_wo), place_wo)
    chain_wq = line(3 * count, summed_wq, sems, 25, (up_wq, cross_wq, held_wq), place_wq)

    def feed_turn(turn):
        chain_w2.step(turn)

    attn_grad = middle_grad[...] * pk_ref[4:5]
    attn_all[mine, :] = attn_grad.astype(BF16)
    gather.start()
    sent = []
    def swapping(step):
        other = partner(me, step, count)
        return post(pair_w1.at[other], swapped_w1.at[me], sems, SWAP1, step, {"shard": other})

    swapped_w1[me] = pair_w1[me]
    sums[1:2, :] = sums_in[0:1, :]
    sums[3:4, :] = sums_in[1:2, :]
    sums[4:5, :] = column_sum(middle_grad[...] * attn_ref[...])
    sums[6:7, :] = column_sum(attn_grad)
    sums[7:8, :] = column_sum(up_ref[...].astype(F32) * pk_ref[5:6])
    dk[...] = jnp.zeros_like(dk)
    dv[...] = jnp.zeros_like(dv)
    live = live_keys(local_len, rows, total)

    def attending(step, carry):
        there = spot(partner(me, step, count), rows)

        gather.arrive(step)

        @pl.when(step == min(1, count - 1))
        def _():
            for other in range(1, count):
                swapping(other).start()

        @pl.when(step == min(2, count - 1))
        def _():
            for other in range(count - 1, 0, -1):
                scatter_two.send(other, branch[other].astype(F32), False)

        grad = back_dot(attn_all[there, :], wo_ref[...]).astype(BF16)
        attend_rows_back(
            size,
            there,
            live,
            project,
            mixed,
            stat,
            grad,
            joined,
            dk,
            dv,
            lambda head: feed_turn(step * heads + head),
        )
        return carry

    lax.fori_loop(0, count, attending, 0)
    lead(chain_w1)
    turned = jnp.transpose(dv[...])
    joined[:, owned : 2 * owned] = jnp.transpose(dk[...]).astype(BF16)
    joined[:, 2 * owned :] = turned.astype(BF16)
    flat[8:9, :] = column_sum(joined[:, 0:owned].astype(F32))
    flat[9:10, :] = column_sum(turned)

    product = row_dot(mixed[...], attn_all[...]).astype(BF16)
    grad_wo[0] = product[:half].reshape(grad_wo.shape[1:])
    grad_wo[1] = product[half:].reshape(grad_wo.shape[1:])
    pair_wo = post(grad_wo.at[1 - core], other_wo, sems, PAIR, 0, {"rep": mate})
    pair_wo.start()

    def weighing(number, carry):
        columns = pl.ds(pl.multiple_of(number * owned, 128), owned)
        product = row_dot(first_all[:, columns], joined[...]).astype(BF16)
        grad_wq[0, number] = product[:half]
        grad_wq[1, number] = product[half:]
        return carry

    lax.fori_loop(0, count, weighing, 0)
    pair_wq = post(grad_wq.at[1 - core], other_wq, sems, PAIR, 1, {"rep": mate})
    pair_wq.start()
    def returning(turn, carry):
        step = count - 1 - turn
        there = spot(partner(me, step, count), rows)
        result = back_dot(joined[there, :], wq[...])

        @pl.when(step > 0)
        def _():
            scatter.send(step, result, False)

        @pl.when(step == 0)
        def _():
            own[...] = result

        return carry

    lax.fori_loop(0, count, returning, 0)
    pair_wo.wait()
    pair_wq.wait()
    grad_wq[core] = (grad_wq[core].astype(F32) + other_wq[...].astype(F32)).astype(BF16)
    for step in range(1, count):
        other = partner(me, step, count)
        copy = post(
            grad_wq.at[core, other], swapped_wq.at[me], sems, SWAPQ, step, {"shard": other}
        )
        copy.start()
        sent.append(copy)
    swapped_wq[me] = grad_wq[core, me]
    lax.fori_loop(count * heads, chain_w2.turns(), lambda turn, carry: (feed_turn(turn), carry)[1], 0)
    lead(chain_wo)
    follow(chain_w1)
    if count == 4:
        for near in (1, 2):
            scatter.combine(near)
            scatter_two.combine(near)
    lead(chain_wq)
    follow(chain_wo)
    for step in range(1, count):
        swapping(step).wait_send()
    result = scatter.total(own[...])
    normed, inverse = norm_parts(tok_ref[...].astype(F32))
    sums[0:1, :] = column_sum(result * normed)
    sums[2:3, :] = column_sum(result)
    own[...] = middle_grad[...] + norm_backward(result, normed, inverse, pk_ref[0:1])
    outgoing[...] = own[0:local_len, :]
    result = branch[0].astype(F32) + pk_ref[7:8]
    result = scatter_two.total(result)
    output[...] = (middle_ref[...] + pk_ref[5:6] * result).astype(BF16)
    sums[5:6, :] = column_sum(up_ref[...].astype(F32) * result)

    own_cols = pl.ds(pl.multiple_of(me * owned, 128), owned)
    for step in range(1, count):
        other = partner(me, step, count)
        copy = post(
            sums.at[:, pl.ds(pl.multiple_of(other * owned, 128), owned)],
            sums_by.at[me],
            sems,
            SMALL,
            step,
            {"shard": other},
        )
        copy.start()
        sent.append(copy)
    sums_by[me] = sums[:, own_cols]

    follow(chain_wq)
    for step in range(1, count):
        other = partner(me, step, count)
        post(sums_by.at[other], sums_by.at[other], sems, SMALL, step, {"shard": me}).wait_recv()
    flat[0:8, :] = functools.reduce(lambda left, right: left + right, [sums_by[i] for i in range(count)])
    flat[10:, :] = jnp.zeros((flat.shape[0] - 10, owned), F32)
    for number in range(bias_rows.shape[1] // owned):
        flat[10 + number : 11 + number, :] = bias_rows[:, number * owned : (number + 1) * owned]
    flat_by[rep] = flat[...]
    for step in range(1, reps):
        copy = post(
            flat, flat_by.at[rep], sems, FLAT, step, {"rep": lax.rem(rep + step, reps)}
        )
        copy.start()
        sent.append(copy)
    for copy in sent:
        copy.wait_send()
    for step in range(1, reps):
        source = lax.rem(rep + reps - step, reps)
        post(flat_by.at[source], flat_by.at[source], sems, FLAT, step, {"shard": me}).wait_recv()
    flat[...] = functools.reduce(lambda left, right: left + right, [flat_by[i] for i in range(reps)])
    for done in (gather, scatter, scatter_two, chain_w2, chain_w1, chain_wo, chain_wq):
        done.finish()


def call(body, number, name, operands, outs, scratch, kinds, flops):
    return pl.pallas_call(
        body,
        in_specs=[VMEM] * len(operands),
        out_specs=[VMEM] * len(outs),
        out_shape=[jax.ShapeDtypeStruct(*out) for out in outs],
        scratch_shapes=[pltpu.VMEM(*item) for item in scratch]
        + [pltpu.SemaphoreType.DMA(kinds), pltpu.SemaphoreType.DMA(kinds)],
        compiler_params=pltpu.CompilerParams(
            collective_id=number, has_side_effects=True, vmem_limit_bytes=60 * 1024 * 1024
        ),
        cost_estimate=pl.CostEstimate(flops=flops, bytes_accessed=2**24, transcendentals=2**22),
        name=name,
    )(*operands)


def local(
    tokens,
    cotangent,
    slot_live,
    w_qkv,
    w_out,
    w_fc1,
    w_fc2,
    norm_gain,
    norm_bias,
    layer_scale,
    qv_bias,
    proj_bias,
    fc1_bias,
):
    count = lax.axis_size("shard")
    me = lax.axis_index("shard")
    _, local_len, model = tokens.shape
    owned = model // count
    units = w_fc2.shape[1]
    hidden_units = w_fc1.shape[2]
    size = model // HEADS
    rows = -(-local_len // 16) * 16
    extra = rows - local_len
    total = rows * count

    alive = jnp.broadcast_to((slot_live > 0).astype(F32)[:, None], (1, 128))
    packed = jnp.concatenate([norm_gain[0], norm_bias[0], layer_scale[0], proj_bias[0]], axis=0)
    packed = packed.astype(F32)
    qv = qv_bias[0].astype(F32)
    bias_row = jnp.concatenate([qv[0], jnp.zeros_like(qv[0]), qv[1]])[None]

    big = (total, model)
    small = (rows, model)
    half = owned // 2
    wide_one = (count, half, units)
    wide_two = (2 * count, units // 4 // count, model)
    wide_half = (2 * count, half // 2, units)
    wide_q = (count, half, 3 * owned)
    wide_o = (count, half // count, model)
    (
        tok,
        up,
        first_all,
        wq,
        project,
        mixed,
        stat,
        attn,
        pk_all,
        middle,
        middle_grad,
        branch,
        pair_w1,
        pair_w2,
        grad_b1,
        sums,
    ) = call(
        functools.partial(early_kernel, count, size, local_len),
        0,
        "forward_and_feed",
        (
            tokens[0],
            cotangent[0],
            alive,
            packed,
            w_qkv[0],
            w_out[0],
            w_fc1[0],
            bias_row,
            w_fc2[0],
            fc1_bias.astype(F32),
        ),
        (
            (small, BF16),
            (small, BF16),
            (big, BF16),
            ((model, 3 * owned), BF16),
            ((total, 3 * owned), BF16),
            ((total, owned), BF16),
            ((total, 128), F32),
            (small, F32),
            ((8, model), F32),
            (small, F32),
            (small, F32),
            ((count, *small), BF16),
            (wide_one, BF16),
            ((units // 2, model), BF16),
            ((1, units), F32),
            ((8, model), F32),
        ),
        (
            (big, BF16),
            ((model, units), BF16),
            *passing(count, *small),
            ((2, *wide_one), BF16),
            ((2, units // 2, model), BF16),
            (wide_one, BF16),
            ((units // 2, model), BF16),
            (big, BF16),
            ((total, units), BF16),
            ((total, units), BF16),
            *passing(count, *small),
            (small, F32),
        ),
        (20, count),
        2 * 10**10,
    )
    reps = lax.axis_size("rep")
    extra_rows = units // owned
    flat_rows = -(-(10 + extra_rows) // 8) * 8
    output, outgoing, total_w1, total_w2, total_wq, total_wo, flat = call(
        functools.partial(last_kernel, count, size, local_len),
        2,
        "attend_backward",
        (
            tok,
            up,
            attn,
            pk_all,
            middle,
            middle_grad,
            branch,
            sums,
            first_all,
            project,
            mixed,
            stat,
            w_out[0],
            wq,
            pair_w1,
            pair_w2.reshape(wide_two),
            grad_b1,
        ),
        (
            (small, BF16),
            ((local_len, model), F32),
            ((owned, hidden_units), BF16),
            ((units, model), BF16),
            ((owned, 3 * model), BF16),
            ((owned, model), BF16),
            ((flat_rows, owned), F32),
        ),
        (
            (big, BF16),
            ((total, 3 * owned), BF16),
            ((owned, total), F32),
            ((owned, total), F32),
            *passing(count, *small),
            *passing(count, *small),
            (small, F32),
            (wide_one, BF16),
            *([(wide_half, BF16)] * 3),
            *([(wide_two, BF16)] * 3),
            (wide_q, BF16),
            *([((3 * count, half, owned), BF16)] * 3),
            *([(wide_o, BF16)] * 3),
            ((2, *wide_q), BF16),
            ((2, *wide_o), BF16),
            (wide_q, BF16),
            (wide_o, BF16),
            ((8, model), F32),
            ((count, 8, owned), F32),
            ((reps, flat_rows, owned), F32),
        ),
        (29, max(3 * count, reps)),
        10**10,
    )
    return (
        output[:local_len][None],
        outgoing[None],
        total_wq.astype(F32)[None],
        total_wo.astype(F32)[None],
        total_w1.astype(F32)[None],
        total_w2.astype(F32)[None],
        flat[0:2][None],
        flat[2:4][None],
        flat[4:6][None],
        flat[8:10][None],
        flat[6:8][None],
        flat[10 : 10 + extra_rows].reshape(1, -1),
    )


def solution(mesh):
    rows = P("rep", "shard", None)
    matrix = P(None, "shard", None)
    vector = P(None, None, "shard")
    return jax.shard_map(
        local,
        mesh=mesh,
        in_specs=(rows, rows, P("rep"), *([matrix] * 4), *([vector] * 5), P(None, "shard")),
        out_specs=(rows, rows, *([matrix] * 4), *([vector] * 5), P(None, "shard")),
        check_vma=False,
    )
```

```python
import functools
import math

import jax
import jax.numpy as jnp
from jax import lax
from jax.experimental import pallas as pl
from jax.experimental.pallas import tpu as pltpu
from jax.sharding import PartitionSpec as P

HEADS = 16
LEN = 1025
EPSILON = 1e-06
F32 = jnp.float32
BF16 = jnp.bfloat16
MESH = pl.DeviceIdType.MESH
HOP = 2
VMEM = pl.BlockSpec(memory_space=pltpu.VMEM)


def norm_parts(hidden):
    center = hidden - jnp.mean(hidden, axis=-1, keepdims=True)
    inverse = lax.rsqrt(jnp.mean(center * center, axis=-1, keepdims=True) + EPSILON)
    return (center * inverse, inverse)


def norm_backward(incoming, normed, inverse, gain):
    scaled = incoming * gain
    return inverse * (
        scaled
        - jnp.mean(scaled, axis=-1, keepdims=True)
        - normed * jnp.mean(scaled * normed, axis=-1, keepdims=True)
    )


def gelu_pair(values):
    cumulative = 0.5 * (1.0 + lax.erf(values * 0.7071067811865476))
    slope = cumulative + values * jnp.exp(-0.5 * values * values) * 0.3989422804014327
    return (values * cumulative, slope)


def plain_dot(left, right):
    return jnp.dot(left, right, preferred_element_type=F32)


def row_dot(left, right):
    return lax.dot_general(left, right, (((0,), (0,)), ((), ())), preferred_element_type=F32)


def back_dot(left, right):
    return lax.dot_general(left, right, (((1,), (1,)), ((), ())), preferred_element_type=F32)


def head_parts(size, width):
    lane = lax.broadcasted_iota(jnp.int32, (1, width), 1)
    return [
        ((lane >= size * number) & (lane < size * (number + 1))) for number in range(width // size)
    ]


def column_sum(values):
    return jnp.sum(values, axis=0, keepdims=True)


def partner(me, step, count):
    other, bit = me, 1
    while bit < count:
        other = other + ((step // bit) % 2) * (1 - 2 * ((me // bit) % 2)) * bit
        bit *= 2
    return other


def spot(index, rows):
    return pl.ds(pl.multiple_of(index * rows, math.gcd(rows, 1024)), rows)


def greet(me, count, others=()):
    barrier = pltpu.get_barrier_semaphore()
    for step in range(1, count):
        pl.semaphore_signal(
            barrier, 1, device_id={"shard": partner(me, step, count)}, device_id_type=MESH
        )
    for other in others:
        pl.semaphore_signal(barrier, 1, device_id={"rep": other}, device_id_type=MESH)
    pl.semaphore_wait(barrier, count - 1 + len(others))


def post(source, target, sems, kind, step, where):
    return pltpu.make_async_remote_copy(
        source,
        target,
        sems[0].at[kind, step],
        sems[1].at[kind, step],
        device_id=where,
        device_id_type=MESH,
    )


def score(queries, keys, live):
    return jnp.where(live, back_dot(queries, keys), -1e30)


def attend_rows(size, here, live, project, mixed, stat):
    owned = mixed.shape[1]
    width = min(max(128, size), owned)
    factor = 1.0 / math.sqrt(size)
    for pair in range(owned // width):
        columns = slice(pair * width, (pair + 1) * width)
        queries = project[here, columns]
        keys = project[:, owned + pair * width : owned + (pair + 1) * width]
        values = project[:, 2 * owned + pair * width : 2 * owned + (pair + 1) * width]
        out = jnp.zeros(queries.shape, F32)
        for number, part in enumerate(head_parts(size, width)):
            own = (jnp.where(part, queries, 0) * factor).astype(BF16)
            scores = score(own, keys, live)
            top = jnp.max(scores, axis=-1, keepdims=True)
            power = jnp.exp(scores - top)
            total = jnp.sum(power, axis=-1, keepdims=True)
            product = plain_dot(power.astype(BF16), values) * (1.0 / total)
            out = jnp.where(part, product, out)
            place = pair * (width // size) + number
            stat[here, place : place + 1] = top + jnp.log(total)
        mixed[here, columns] = out.astype(BF16)


def attend_rows_back(size, here, live, project, mixed, stat, grad, joined, dk, dv, between):
    owned = mixed.shape[1]
    width = min(max(128, size), owned)
    factor = 1.0 / math.sqrt(size)
    for pair in range(owned // width):
        columns = slice(pair * width, (pair + 1) * width)
        queries = project[here, columns]
        keys = project[:, owned + pair * width : owned + (pair + 1) * width]
        values = project[:, 2 * owned + pair * width : 2 * owned + (pair + 1) * width]
        grads = grad[:, columns]
        overlap = grads.astype(F32) * mixed[here, columns].astype(F32)
        turned_q = jnp.transpose(queries.astype(F32) * factor).astype(BF16)
        turned_g = jnp.transpose(grads.astype(F32)).astype(BF16)
        dq = jnp.zeros(queries.shape, F32)
        for number, part in enumerate(head_parts(size, width)):
            place = pair * (width // size) + number
            own_q = (jnp.where(part, queries, 0) * factor).astype(BF16)
            own_g = jnp.where(part, grads, 0).astype(BF16)
            weights = jnp.exp(score(own_q, keys, live) - stat[here, place : place + 1])
            delta = jnp.sum(jnp.where(part, overlap, 0), axis=-1, keepdims=True)
            slope = (weights * (back_dot(own_g, values) - delta)).astype(BF16)
            span = slice(place * size, (place + 1) * size)
            inner = slice(number * size, (number + 1) * size)
            dk[span, :] += plain_dot(turned_q[inner], slope)
            dv[span, :] += plain_dot(turned_g[inner], weights.astype(BF16))
            dq = jnp.where(part, plain_dot(slope, keys), dq)
            between(place)
        joined[here, columns] = (dq * factor).astype(BF16)


class Gather:
    def __init__(self, array, rows, me, count, sems, kind):
        self.array, self.rows, self.me, self.count = array, rows, me, count
        self.sems, self.kind, self.square = sems, kind, count == 4
        self.steps = (1, 2) if self.square else tuple(range(1, count))
        self.half = array.shape[1] // 2

    def direct(self, owner, step):
        block = self.array.at[spot(owner, self.rows)]
        where = {"shard": partner(self.me, step, self.count)}
        return post(block, block, self.sems, self.kind, step, where)

    def relay(self, owner, step):
        columns = pl.ds((step - 1) * self.half, self.half)
        block = self.array.at[spot(owner, self.rows), columns]
        where = {"shard": partner(self.me, 3 - step, self.count)}
        return post(block, block, self.sems, self.kind + 1, step, where)

    def start(self):
        for step in self.steps:
            self.direct(self.me, step).start()

    def arrive(self, step):
        if not self.square:

            @pl.when(step > 0)
            def _():
                self.direct(partner(self.me, step, self.count), step).wait_recv()

            return

        @pl.when(step == 1)
        def _():
            for near in (1, 2):
                owner = partner(self.me, near, 4)
                self.direct(owner, near).wait_recv()
                self.relay(owner, near).start()

        @pl.when(step == 3)
        def _():
            for near in (1, 2):
                self.relay(partner(self.me, 3, 4), near).wait_recv()

    def finish(self):
        for step in self.steps:
            self.direct(self.me, step).wait_send()
            if self.square:
                self.relay(partner(self.me, step, 4), step).wait_send()


class Scatter:
    def __init__(self, part, landed, via, me, count, sems, kind):
        self.part, self.landed, self.via, self.me, self.count = part, landed, via, me, count
        self.sems, self.kind, self.square = sems, kind, count == 4
        self.steps = (1, 2) if self.square else tuple(range(1, count))
        self.half = part.shape[2] // 2

    def direct(self, step, side=0):
        source, target = self.part.at[step - 1], self.landed.at[step - 1]
        if self.square:
            columns = pl.ds(side * self.half, self.half)
            source, target = source.at[:, columns], target.at[:, columns]
        where = {"shard": partner(self.me, step, self.count)}
        return post(source, target, self.sems, self.kind + 2 * side, step, where)

    def early(self, near):
        return post(
            self.part.at[2, :, pl.ds((near - 1) * self.half, self.half)],
            self.via.at[near - 1],
            self.sems,
            self.kind + 1,
            near,
            {"shard": partner(self.me, near, 4)},
        )

    def send(self, step, value, ready=True):
        if not self.square:
            self.part[step - 1] = value.astype(BF16)
            self.direct(step).start()
            return
        self.part[step - 1] = value.astype(BF16)

        @pl.when(step == 3)
        def _():
            for near in (1, 2):
                self.early(near).start()

        for near in (1, 2):

            @pl.when(step == near)
            def _():
                self.direct(near, near - 1).start()
                if ready:
                    side = 2 - near
                    self.combine(near, value[:, side * self.half : (side + 1) * self.half])

    def combine(self, near, value=None):
        side = 2 - near
        columns = slice(side * self.half, (side + 1) * self.half)
        if value is None:
            value = self.part[near - 1, :, columns].astype(F32)
        self.early(3 - near).wait_recv()
        self.part[near - 1, :, columns] = (value + self.via[side].astype(F32)).astype(BF16)
        self.direct(near, side).start()

    def total(self, value):
        for step in self.steps:
            for side in range(2 if self.square else 1):
                self.direct(step, side).wait_recv()
            value += self.landed[step - 1].astype(F32)
        return value

    def finish(self):
        for step in self.steps:
            for side in range(2 if self.square else 1):
                self.direct(step, side).wait_send()
            if self.square:
                self.early(step).wait_send()


def passing(count, rows, model):
    slots = 2 if count == 4 else count - 1
    return [
        ((count - 1, rows, model), BF16),
        ((slots, rows, model), BF16),
        ((2, rows, model // 2), BF16),
    ]


class Chain:
    def __init__(self, rep, chips, parts, own, sems, kind, scratch, total):
        self.parts, self.own, self.sems, self.kind = parts, own, sems, kind
        self.up, self.cross, self.held = scratch
        self.total = total
        core, chip = rep % 2, rep // 2
        side = chip // (chips // 2)
        self.core, self.last = core, chips // 2 - 1
        self.depth = side * (chips - 1 - chip) + (1 - side) * chip
        ahead = 1 - 2 * side
        self.inner = {"rep": (chip + ahead) * 2 + core}
        self.outer = {"rep": (chip - ahead) * 2 + core}
        self.mate = {"rep": rep + 1 - 2 * core}

    def copy(self, which, part):
        where = (self.inner, self.inner, self.outer, self.mate)[which]
        final = self.total(self.core, part)
        source = self.held.at[part] if which < 2 else final
        target = (self.up.at[part], self.cross.at[part], final, final)[which]
        return post(source, target, self.sems, self.kind + which, part, where)

    def reduce(self, part):
        depth, last = self.depth, self.last
        value = self.own(part)

        @pl.when(depth == 0)
        def _():
            self.held[part] = value.astype(BF16)

        if last > 0:

            @pl.when(depth > 0)
            def _():
                self.copy(0, part).wait_recv()
                self.held[part] = (value + self.up[part].astype(F32)).astype(BF16)

            @pl.when(depth < last)
            def _():
                self.copy(0, part).start()

        @pl.when(depth == last)
        def _():
            self.copy(1, part).start()

    def result(self, part):
        depth, last = self.depth, self.last

        @pl.when(depth == last)
        def _():
            self.copy(1, part).wait_recv()
            both = self.held[part].astype(F32) + self.cross[part].astype(F32)
            self.total(self.core, part)[...] = both.astype(BF16)

        if last > 0:

            @pl.when(depth < last)
            def _():
                self.copy(2, part).wait_recv()

            @pl.when(depth > 0)
            def _():
                self.copy(2, part).start()

        self.copy(3, part).start()

    def within(self, part, act):
        @pl.when((part >= 0) & (part < self.parts))
        def _():
            act(part)

    def step(self, turn):
        self.within(turn - HOP * self.depth, self.reduce)
        self.within(turn - HOP * (2 * self.last + 1 - self.depth), self.result)

    def turns(self):
        return self.parts + HOP * (2 * self.last + 1)

    def finish(self):
        def closing(part, carry):
            if self.last > 0:

                @pl.when(self.depth < self.last)
                def _():
                    self.copy(0, part).wait_send()

                @pl.when(self.depth > 0)
                def _():
                    self.copy(2, part).wait_send()

            @pl.when(self.depth == self.last)
            def _():
                self.copy(1, part).wait_send()

            final = self.total(1 - self.core, part)
            self.copy(3, part).wait_send()
            post(final, final, self.sems, self.kind + 3, part, self.mate).wait_recv()
            return carry

        lax.fori_loop(0, self.parts, closing, 0)


def loop(count, act):
    def body(part, carry):
        act(part)
        return carry

    lax.fori_loop(0, count, body, 0)


def lead(chain):
    @pl.when(chain.depth == 0)
    def _():
        loop(chain.parts, chain.reduce)


def follow(chain, lag=2):
    @pl.when(chain.depth == 0)
    def _():
        loop(chain.parts, chain.result)

    if chain.last > 0:

        @pl.when(chain.depth > 0)
        def _():
            def both(part):
                chain.within(part, chain.reduce)
                chain.within(part - lag, chain.result)

            loop(chain.parts + lag, both)


def live_keys(local_len, rows, total):
    place = lax.broadcasted_iota(jnp.int32, (1, total), 1)
    inner = place % rows
    return (inner < local_len) & ((place // rows) * local_len + inner < LEN)


def early_kernel(
    count,
    size,
    local_len,
    move,
    raw_ref,
    raw_up,
    live_ref,
    pk_ref,
    wqkv_ref,
    wo_ref,
    w1_ref,
    bias_ref,
    w2_ref,
    fc1_bias,
    tok_ref,
    up_ref,
    first_all,
    wq,
    project,
    mixed,
    stat,
    attn,
    pk_all,
    middle_out,
    middle_grad,
    branch,
    pair_w1,
    pair_w2,
    grad_bias,
    sums,
    fc2_all,
    w1c,
    part,
    landed,
    via,
    grad_w1,
    grad_w2,
    other_w1,
    other_w2,
    second_all,
    pre_in,
    act,
    part_two,
    landed_two,
    via_two,
    own,
    send_sem,
    recv_sem,
):
    sems = (send_sem, recv_sem)
    me, rep = lax.axis_index("shard"), lax.axis_index("rep")
    core = rep % 2
    mate = rep + 1 - 2 * core
    rows, model = tok_ref.shape
    owned = pk_ref.shape[1]
    units = w1c.shape[1]
    half = owned // 2
    greet(me, count, (mate,))

    own_cols = pl.ds(pl.multiple_of(me * owned, 128), owned)
    own_rows = pl.ds(pl.multiple_of(me * owned, 16), owned)
    mine = spot(me, rows)
    ours = pl.ds(pl.multiple_of(core * half, 16), half)
    pk_all[:, own_cols] = pk_ref[...]
    PK, FIRST, FC2, W1, WQ, FQ, F1, SUM = 0, 1, 3, 5, 6, 9, 10, 11
    gather_first = Gather(first_all, rows, me, count, sems, FIRST)
    gather_fc2 = Gather(fc2_all, rows, me, count, sems, FC2)
    scatter = Scatter(part, landed, via, me, count, sems, SUM)
    sent = []

    def block(source):
        return pl.ds(pl.multiple_of(source * owned + core * half, 16), half)

    def push(source, target, kind, step):
        copy = post(source, target, sems, kind, step, {"shard": partner(me, step, count)})
        copy.start()
        sent.append(copy)

    def hand(target, kind, step):
        copy = post(target, target, sems, kind, step, {"rep": mate})
        copy.start()
        sent.append(copy)
        return copy

    for step in range(1, count):
        push(pk_ref, pk_all.at[:, own_cols], PK, step)
    for step in range(1, count):
        other = partner(me, step, count)
        for third in range(3):
            push(
                wqkv_ref.at[ours, pl.ds(pl.multiple_of(third * model + other * owned, 128), owned)],
                wq.at[block(me), third * owned : (third + 1) * owned],
                WQ + third,
                step,
            )
    own[...] = jnp.zeros_like(own)
    own[0:local_len, :] = raw_ref[...].astype(F32)
    tok_ref[...] = own[...].astype(BF16)
    hidden = tok_ref[...].astype(F32)
    normed, _ = norm_parts(hidden)
    for step in range(1, count):
        other = pl.ds(pl.multiple_of(partner(me, step, count) * owned, 128), owned)
        post(pk_ref, pk_all.at[:, other], sems, PK, step, {"rep": mate}).wait_recv()
    first_all[mine, :] = (normed * pk_all[0:1] + pk_all[2:3]).astype(BF16)
    gather_first.start()
    for third in range(3):
        columns = pl.ds(pl.multiple_of(third * model + me * owned, 128), owned)
        wq[own_rows, third * owned : (third + 1) * owned] = wqkv_ref[:, columns]
    move.need(6)
    w1c[own_rows, :] = w1_ref[:, pl.ds(pl.multiple_of(me * units, 128), units)]
    own[0:local_len, :] = raw_up[...].astype(F32)
    place = lax.broadcasted_iota(jnp.int32, (rows, 1), 0)
    valid = (place < local_len) & (me * local_len + place < LEN) & (live_ref[0:1, 0:1] > 0.5)
    up_ref[...] = jnp.where(valid, own[...], 0.0).astype(BF16)
    fc2_all[mine, :] = (up_ref[...].astype(F32) * pk_all[5:6]).astype(BF16)

    handed = []
    for step in range(1, count):
        other = partner(me, step, count)
        for third in range(3):
            columns = slice(third * owned, (third + 1) * owned)
            post(
                wq.at[block(other), columns],
                wq.at[block(other), columns],
                sems,
                WQ + third,
                step,
                {"rep": mate},
            ).wait_recv()
        handed.append(hand(wq.at[block(other)], FQ, step))
    for copy in handed:
        copy.wait_recv()

    def shifting(step):
        other = partner(me, step, count)
        columns = pl.ds(pl.multiple_of(other * units, 128), units)
        where = {"shard": other}
        return post(w1_ref.at[ours, columns], w1c.at[block(me)], sems, W1, step, where)

    def projecting(step, carry):
        there = spot(partner(me, step, count), rows)

        gather_first.arrive(step)

        @pl.when(step == min(1, count - 1))
        def _():
            for other in range(1, count):
                shifting(other).start()

        project[there, :] = (plain_dot(first_all[there, :], wq[...]) + bias_ref[...]).astype(BF16)
        return carry

    lax.fori_loop(0, count, projecting, 0)
    move.need(5)
    move.leave(2, 3, 4)
    gather_fc2.start()
    live = live_keys(local_len, rows, project.shape[0])

    def attending(turn, carry):
        step = count - 1 - turn
        there = spot(partner(me, step, count), rows)

        if count == 4:

            @pl.when(turn == count - 2)
            def _():
                gather_fc2.arrive(1)

        attend_rows(size, there, live, project, mixed, stat)
        result = plain_dot(mixed[there, :], wo_ref[...])

        @pl.when(step > 0)
        def _():
            scatter.send(step, result)

        @pl.when(step == 0)
        def _():
            attn[...] = result

        return carry

    lax.fori_loop(0, count, attending, 0)
    move.leave(5, 6)
    for step in range(1, count):
        other = block(partner(me, step, count))
        post(w1c.at[other], w1c.at[other], sems, W1, step, {"rep": mate}).wait_recv()
        handed.append(hand(w1c.at[other], F1, step))
    attn[...] = scatter.total(attn[...] + pk_all[6:7])
    move.leave(7)
    tile = min(256, units)
    SECOND, SUM, PAIR = 14, 16, 19
    gather = Gather(second_all, rows, me, count, sems, SECOND)
    scatter_two = Scatter(part_two, landed_two, via_two, me, count, sems, SUM)
    middle = tok_ref[...].astype(F32) + pk_all[4:5] * attn[...]
    middle_out[...] = middle
    normed, _ = norm_parts(middle)
    second_all[mine, :] = (normed * pk_all[1:2] + pk_all[3:4]).astype(BF16)
    gather.start()
    grad_bias[...] = jnp.zeros_like(grad_bias)
    for copy in handed[count - 1 :]:
        copy.wait_recv()

    def feeding(step, carry):
        there = spot(partner(me, step, count), rows)

        gather.arrive(step)
        if count == 4:

            @pl.when(step > 1)
            def _():
                gather_fc2.arrive(step)

        else:
            gather_fc2.arrive(step)

        def tiles(number, inner):
            columns = pl.ds(pl.multiple_of(number * tile, 128), tile)
            pre = plain_dot(second_all[there, :], w1c[:, columns]) + fc1_bias[:, columns]
            value, slope = gelu_pair(pre)
            act[there, columns] = value.astype(BF16)
            back = back_dot(
                fc2_all[there, :], w2_ref[pl.ds(pl.multiple_of(number * tile, 16), tile), :]
            )
            back = back * slope
            grad_bias[:, columns] += column_sum(back)
            pre_in[there, columns] = back.astype(BF16)
            return inner

        lax.fori_loop(0, units // tile, tiles, 0)
        result = back_dot(pre_in[there, :], w1c[...])

        @pl.when(step > 0)
        def _():
            scatter_two.send(step, result, False)

        @pl.when(step == 0)
        def _():
            own[...] = result

        return carry

    move.need(8)
    move.leave(9)
    lax.fori_loop(0, count, feeding, 0)

    def branching(step, carry):
        there = spot(partner(me, step, count), rows)
        branch[step] = plain_dot(act[there, :], w2_ref[...]).astype(BF16)
        return carry

    lax.fori_loop(0, count, branching, 0)
    move.leave(11)
    if count == 4:
        for near in (1, 2):
            scatter_two.combine(near)

    def weighing_two(number, carry):
        columns = pl.ds(pl.multiple_of(number * tile, 128), tile)
        here = pl.ds(pl.multiple_of(lax.rem(number, halves) * tile, 16), tile)
        grad_w2[number // halves, here, :] = row_dot(act[:, columns], fc2_all[...]).astype(BF16)
        return carry

    halves = units // tile // 2
    lax.fori_loop(0, units // tile, weighing_two, 0)
    copies = [post(grad_w2.at[1 - core], other_w2, sems, PAIR, 0, {"rep": mate})]
    copies[0].start()

    def weighing_one(number, carry):
        columns = pl.ds(pl.multiple_of(number * owned, 128), owned)
        product = row_dot(second_all[:, columns], pre_in[...]).astype(BF16)
        grad_w1[0, number] = product[:half]
        grad_w1[1, number] = product[half:]
        return carry

    lax.fori_loop(0, count, weighing_one, 0)
    copies.append(post(grad_w1.at[1 - core], other_w1, sems, PAIR, 1, {"rep": mate}))
    copies[1].start()
    for copy in copies:
        copy.wait()
    pair_w2[...] = (grad_w2[core].astype(F32) + other_w2[...].astype(F32)).astype(BF16)
    pair_w1[...] = (grad_w1[core].astype(F32) + other_w1[...].astype(F32)).astype(BF16)

    result = scatter_two.total(own[...])
    normed, inverse = norm_parts(middle_out[...])
    sums[0:1, :] = column_sum(result * normed)
    sums[1:2, :] = column_sum(result)
    middle_grad[...] = up_ref[...].astype(F32) + norm_backward(
        result, normed, inverse, pk_all[1:2]
    )
    for done in (gather_first, gather_fc2, gather, scatter, scatter_two):
        done.finish()
    for step in range(1, count):
        shifting(step).wait_send()
    for copy in sent:
        copy.wait_send()


def last_kernel(
    count,
    size,
    local_len,
    move,
    tok_ref,
    up_ref,
    attn_ref,
    pk_ref,
    middle_ref,
    middle_grad,
    branch,
    sums_in,
    first_all,
    project,
    mixed,
    stat,
    wo_ref,
    wq,
    pair_w1,
    pair_w2,
    bias_rows,
    output,
    outgoing,
    total_w1,
    total_w2,
    total_wq,
    total_wo,
    flat,
    attn_all,
    joined,
    dk,
    dv,
    part,
    landed,
    via,
    part_two,
    landed_two,
    via_two,
    own,
    swapped_w1,
    up_w1,
    cross_w1,
    held_w1,
    up_w2,
    cross_w2,
    held_w2,
    swapped_wq,
    up_wq,
    cross_wq,
    held_wq,
    up_wo,
    cross_wo,
    held_wo,
    grad_wq,
    grad_wo,
    other_wq,
    other_wo,
    sums,
    sums_by,
    flat_by,
    send_sem,
    recv_sem,
):
    sems = (send_sem, recv_sem)
    me = lax.axis_index("shard")
    rows, model = tok_ref.shape
    total, owned = mixed.shape
    mine = spot(me, rows)
    GRAD, BRANCH, SUM, SWAP1, SWAPQ, PAIR, SMALL, FLAT = 0, 2, 5, 8, 9, 10, 11, 12
    gather = Gather(attn_all, rows, me, count, sems, GRAD)
    scatter = Scatter(part, landed, via, me, count, sems, SUM)
    scatter_two = Scatter(part_two, landed_two, via_two, me, count, sems, BRANCH)
    rep, reps = lax.axis_index("rep"), lax.axis_size("rep")
    core = rep % 2
    mate = rep + 1 - 2 * core
    half = owned // 2
    heads = owned // size
    greet(me, count, [lax.rem(rep + other, reps) for other in range(1, reps)])

    def summed_w2(number):
        return pair_w2[number].astype(F32)

    def summed_w1(part):
        number = part // 2
        step = partner(me, number, count)

        @pl.when((step > 0) & (lax.rem(part, 2) == 0))
        def _():
            post(
                swapped_w1.at[number], swapped_w1.at[number], sems, SWAP1, step, {"shard": me}
            ).wait_recv()

        return swapped_w1[number, spot(lax.rem(part, 2), half // 2)].astype(F32)

    def summed_wq(number):
        source, third = number // 3, lax.rem(number, 3)
        step = partner(me, source, count)

        @pl.when((step > 0) & (third == 0))
        def _():
            post(
                swapped_wq.at[source], swapped_wq.at[source], sems, SWAPQ, step, {"shard": me}
            ).wait_recv()

        columns = pl.ds(pl.multiple_of(third * owned, 128), owned)
        return swapped_wq[source, :, columns].astype(F32)

    def summed_wo(number):
        return grad_wo[core, number].astype(F32) + other_wo[number].astype(F32)

    def place_w1(part, number):
        rows_here = spot(part * 2 + lax.rem(number, 2), half // 2)
        return total_w1.at[rows_here, pl.ds(pl.multiple_of((number // 2) * units, 128), units)]

    def place_w2(part, number):
        return total_w2.at[spot(part * 2 * count + number, pair_w2.shape[1])]

    def place_wq(part, number):
        column = lax.rem(number, 3) * model + (number // 3) * owned
        rows_here = pl.ds(pl.multiple_of(part * half, 16), half)
        return total_wq.at[rows_here, pl.ds(pl.multiple_of(column, 128), owned)]

    def place_wo(part, number):
        return total_wo.at[spot(part * count + number, half // count)]

    units = pair_w1.shape[2]
    line = functools.partial(Chain, rep, reps // 2)
    chain_w2 = line(2 * count, summed_w2, sems, 13, (up_w2, cross_w2, held_w2), place_w2)
    chain_w1 = line(2 * count, summed_w1, sems, 17, (up_w1, cross_w1, held_w1), place_w1)
    chain_wo = line(count, summed_wo, sems, 21, (up_wo, cross_wo, held_wo), place_wo)
    chain_wq = line(3 * count, summed_wq, sems, 25, (up_wq, cross_wq, held_wq), place_wq)

    def feed_turn(turn):
        chain_w2.step(turn)

    attn_grad = middle_grad[...] * pk_ref[4:5]
    attn_all[mine, :] = attn_grad.astype(BF16)
    gather.start()
    sent = []
    def swapping(step):
        other = partner(me, step, count)
        return post(pair_w1.at[other], swapped_w1.at[me], sems, SWAP1, step, {"shard": other})

    sums[1:2, :] = sums_in[0:1, :]
    sums[3:4, :] = sums_in[1:2, :]
    sums[4:5, :] = column_sum(middle_grad[...] * attn_ref[...])
    sums[6:7, :] = column_sum(attn_grad)
    sums[7:8, :] = column_sum(up_ref[...].astype(F32) * pk_ref[5:6])
    dk[...] = jnp.zeros_like(dk)
    dv[...] = jnp.zeros_like(dv)
    live = live_keys(local_len, rows, total)

    def attending(step, carry):
        there = spot(partner(me, step, count), rows)

        gather.arrive(step)

        @pl.when(step == min(1, count - 1))
        def _():
            for other in range(1, count):
                swapping(other).start()

        @pl.when(step == min(2, count - 1))
        def _():
            for other in range(count - 1, 0, -1):
                scatter_two.send(other, branch[other].astype(F32), False)

        grad = back_dot(attn_all[there, :], wo_ref[...]).astype(BF16)
        attend_rows_back(
            size,
            there,
            live,
            project,
            mixed,
            stat,
            grad,
            joined,
            dk,
            dv,
            lambda head: feed_turn(step * heads + head),
        )
        return carry

    move.need(6, 9, 10, 11, 12, 14, 15)
    swapped_w1[me] = pair_w1[me]
    lax.fori_loop(0, count, attending, 0)
    move.need(4, 8, 13)
    lead(chain_w1)
    turned = jnp.transpose(dv[...])
    joined[:, owned : 2 * owned] = jnp.transpose(dk[...]).astype(BF16)
    joined[:, 2 * owned :] = turned.astype(BF16)
    flat[8:9, :] = column_sum(joined[:, 0:owned].astype(F32))
    flat[9:10, :] = column_sum(turned)

    product = row_dot(mixed[...], attn_all[...]).astype(BF16)
    grad_wo[0] = product[:half].reshape(grad_wo.shape[1:])
    grad_wo[1] = product[half:].reshape(grad_wo.shape[1:])
    pair_wo = post(grad_wo.at[1 - core], other_wo, sems, PAIR, 0, {"rep": mate})
    pair_wo.start()

    def weighing(number, carry):
        columns = pl.ds(pl.multiple_of(number * owned, 128), owned)
        product = row_dot(first_all[:, columns], joined[...]).astype(BF16)
        grad_wq[0, number] = product[:half]
        grad_wq[1, number] = product[half:]
        return carry

    lax.fori_loop(0, count, weighing, 0)
    pair_wq = post(grad_wq.at[1 - core], other_wq, sems, PAIR, 1, {"rep": mate})
    pair_wq.start()
    def returning(turn, carry):
        step = count - 1 - turn
        there = spot(partner(me, step, count), rows)
        result = back_dot(joined[there, :], wq[...])

        @pl.when(step > 0)
        def _():
            scatter.send(step, result, False)

        @pl.when(step == 0)
        def _():
            own[...] = result

        return carry

    lax.fori_loop(0, count, returning, 0)
    pair_wo.wait()
    pair_wq.wait()
    grad_wq[core] = (grad_wq[core].astype(F32) + other_wq[...].astype(F32)).astype(BF16)
    for step in range(1, count):
        other = partner(me, step, count)
        copy = post(
            grad_wq.at[core, other], swapped_wq.at[me], sems, SWAPQ, step, {"shard": other}
        )
        copy.start()
        sent.append(copy)
    swapped_wq[me] = grad_wq[core, me]
    lax.fori_loop(count * heads, chain_w2.turns(), lambda turn, carry: (feed_turn(turn), carry)[1], 0)
    lead(chain_wo)
    follow(chain_w1)
    if count == 4:
        for near in (1, 2):
            scatter.combine(near)
            scatter_two.combine(near)
    lead(chain_wq)
    follow(chain_wo)
    for step in range(1, count):
        swapping(step).wait_send()
    result = scatter.total(own[...])
    normed, inverse = norm_parts(tok_ref[...].astype(F32))
    sums[0:1, :] = column_sum(result * normed)
    sums[2:3, :] = column_sum(result)
    own[...] = middle_grad[...] + norm_backward(result, normed, inverse, pk_ref[0:1])
    outgoing[...] = own[0:local_len, :]
    result = branch[0].astype(F32) + pk_ref[7:8]
    result = scatter_two.total(result)
    output[...] = (middle_ref[...] + pk_ref[5:6] * result).astype(BF16)
    sums[5:6, :] = column_sum(up_ref[...].astype(F32) * result)

    own_cols = pl.ds(pl.multiple_of(me * owned, 128), owned)
    for step in range(1, count):
        other = partner(me, step, count)
        copy = post(
            sums.at[:, pl.ds(pl.multiple_of(other * owned, 128), owned)],
            sums_by.at[me],
            sems,
            SMALL,
            step,
            {"shard": other},
        )
        copy.start()
        sent.append(copy)
    sums_by[me] = sums[:, own_cols]

    for done in (chain_w2, chain_w1):
        done.finish()
    move.leave(2, 3)
    follow(chain_wq)
    for step in range(1, count):
        other = partner(me, step, count)
        post(sums_by.at[other], sums_by.at[other], sems, SMALL, step, {"shard": me}).wait_recv()
    flat[0:8, :] = functools.reduce(lambda left, right: left + right, [sums_by[i] for i in range(count)])
    flat[10:, :] = jnp.zeros((flat.shape[0] - 10, owned), F32)
    for number in range(bias_rows.shape[1] // owned):
        flat[10 + number : 11 + number, :] = bias_rows[:, number * owned : (number + 1) * owned]
    flat_by[rep] = flat[...]
    for step in range(1, reps):
        copy = post(
            flat, flat_by.at[rep], sems, FLAT, step, {"rep": lax.rem(rep + step, reps)}
        )
        copy.start()
        sent.append(copy)
    for copy in sent:
        copy.wait_send()
    for step in range(1, reps):
        source = lax.rem(rep + reps - step, reps)
        post(flat_by.at[source], flat_by.at[source], sems, FLAT, step, {"shard": me}).wait_recv()
    flat[...] = functools.reduce(lambda left, right: left + right, [flat_by[i] for i in range(reps)])
    for done in (gather, scatter, scatter_two, chain_wo, chain_wq):
        done.finish()


class Mover:
    def __init__(self, fetches, stores, sem):
        self.fetches, self.stores, self.sem, self.left = fetches, stores, sem, []
        self.order = {key: place for place, key in enumerate([*fetches, *stores])}
        for key in fetches:
            self.copy(key).start()

    def copy(self, key):
        pair = self.fetches[key] if key in self.fetches else self.stores[key]
        return pltpu.make_async_copy(*pair, self.sem.at[self.order[key]])

    def need(self, *numbers):
        for number in numbers:
            self.copy(("in", number)).wait()

    def leave(self, *numbers):
        for number in numbers:
            self.copy(("out", number)).start()
            self.left.append(("out", number))

    def finish(self):
        for key in self.left:
            self.copy(key).wait()


def moving(body, ins, outs, late, early, *refs):
    refs = list(refs)
    extra = len(late) + len(early) + 1
    held = refs[len(refs) - extra :]
    fetches, stores = {}, {}
    for number, buffer in zip(late, held):
        fetches["in", number] = (refs[number], buffer)
        refs[number] = buffer
    for number, buffer in zip(early, held[len(late) :]):
        stores["out", number] = (buffer, refs[ins + number])
        refs[ins + number] = buffer
    move = Mover(fetches, stores, held[-1])
    body(move, *refs[: len(refs) - extra])
    move.finish()


def call(body, number, name, operands, outs, scratch, kinds, flops, late, early):
    far = pl.BlockSpec(memory_space=pl.ANY)
    buffers = [(operands[i].shape, operands[i].dtype) for i in late] + [outs[i] for i in early]
    return pl.pallas_call(
        functools.partial(moving, body, len(operands), len(outs), late, early),
        in_specs=[far if i in late else VMEM for i in range(len(operands))],
        out_specs=[far if i in early else VMEM for i in range(len(outs))],
        out_shape=[jax.ShapeDtypeStruct(*out) for out in outs],
        scratch_shapes=[pltpu.VMEM(*item) for item in scratch]
        + [pltpu.SemaphoreType.DMA(kinds), pltpu.SemaphoreType.DMA(kinds)]
        + [pltpu.VMEM(*item) for item in buffers]
        + [pltpu.SemaphoreType.DMA((len(buffers),))],
        compiler_params=pltpu.CompilerParams(
            collective_id=number, has_side_effects=True, vmem_limit_bytes=60 * 1024 * 1024
        ),
        cost_estimate=pl.CostEstimate(flops=flops, bytes_accessed=2**24, transcendentals=2**22),
        name=name,
    )(*operands)


def local(
    tokens,
    cotangent,
    slot_live,
    w_qkv,
    w_out,
    w_fc1,
    w_fc2,
    norm_gain,
    norm_bias,
    layer_scale,
    qv_bias,
    proj_bias,
    fc1_bias,
):
    count = lax.axis_size("shard")
    me = lax.axis_index("shard")
    _, local_len, model = tokens.shape
    owned = model // count
    units = w_fc2.shape[1]
    hidden_units = w_fc1.shape[2]
    size = model // HEADS
    rows = -(-local_len // 16) * 16
    extra = rows - local_len
    total = rows * count

    alive = jnp.broadcast_to((slot_live > 0).astype(F32)[:, None], (1, 128))
    packed = jnp.concatenate([norm_gain[0], norm_bias[0], layer_scale[0], proj_bias[0]], axis=0)
    packed = packed.astype(F32)
    qv = qv_bias[0].astype(F32)
    bias_row = jnp.concatenate([qv[0], jnp.zeros_like(qv[0]), qv[1]])[None]

    big = (total, model)
    small = (rows, model)
    half = owned // 2
    wide_one = (count, half, units)
    wide_two = (2 * count, units // 4 // count, model)
    wide_half = (2 * count, half // 2, units)
    wide_q = (count, half, 3 * owned)
    wide_o = (count, half // count, model)
    (
        tok,
        up,
        first_all,
        wq,
        project,
        mixed,
        stat,
        attn,
        pk_all,
        middle,
        middle_grad,
        branch,
        pair_w1,
        pair_w2,
        grad_b1,
        sums,
    ) = call(
        functools.partial(early_kernel, count, size, local_len),
        0,
        "forward_and_feed",
        (
            tokens[0],
            cotangent[0],
            alive,
            packed,
            w_qkv[0],
            w_out[0],
            w_fc1[0],
            bias_row,
            w_fc2[0],
            fc1_bias.astype(F32),
        ),
        (
            (small, BF16),
            (small, BF16),
            (big, BF16),
            ((model, 3 * owned), BF16),
            ((total, 3 * owned), BF16),
            ((total, owned), BF16),
            ((total, 128), F32),
            (small, F32),
            ((8, model), F32),
            (small, F32),
            (small, F32),
            ((count, *small), BF16),
            (wide_one, BF16),
            ((units // 2, model), BF16),
            ((1, units), F32),
            ((8, model), F32),
        ),
        (
            (big, BF16),
            ((model, units), BF16),
            *passing(count, *small),
            ((2, *wide_one), BF16),
            ((2, units // 2, model), BF16),
            (wide_one, BF16),
            ((units // 2, model), BF16),
            (big, BF16),
            ((total, units), BF16),
            ((total, units), BF16),
            *passing(count, *small),
            (small, F32),
        ),
        (20, count),
        2 * 10**10,
        (5, 6, 8),
        (2, 3, 4, 5, 6, 7, 9, 11),
    )
    reps = lax.axis_size("rep")
    extra_rows = units // owned
    flat_rows = -(-(10 + extra_rows) // 8) * 8
    output, outgoing, total_w1, total_w2, total_wq, total_wo, flat = call(
        functools.partial(last_kernel, count, size, local_len),
        2,
        "attend_backward",
        (
            tok,
            up,
            attn,
            pk_all,
            middle,
            middle_grad,
            branch,
            sums,
            first_all,
            project,
            mixed,
            stat,
            w_out[0],
            wq,
            pair_w1,
            pair_w2.reshape(wide_two),
            grad_b1,
        ),
        (
            (small, BF16),
            ((local_len, model), F32),
            ((owned, hidden_units), BF16),
            ((units, model), BF16),
            ((owned, 3 * model), BF16),
            ((owned, model), BF16),
            ((flat_rows, owned), F32),
        ),
        (
            (big, BF16),
            ((total, 3 * owned), BF16),
            ((owned, total), F32),
            ((owned, total), F32),
            *passing(count, *small),
            *passing(count, *small),
            (small, F32),
            (wide_one, BF16),
            *([(wide_half, BF16)] * 3),
            *([(wide_two, BF16)] * 3),
            (wide_q, BF16),
            *([((3 * count, half, owned), BF16)] * 3),
            *([(wide_o, BF16)] * 3),
            ((2, *wide_q), BF16),
            ((2, *wide_o), BF16),
            (wide_q, BF16),
            (wide_o, BF16),
            ((8, model), F32),
            ((count, 8, owned), F32),
            ((reps, flat_rows, owned), F32),
        ),
        (29, max(3 * count, reps)),
        10**10,
        (4, 6, 8, 9, 10, 11, 12, 13, 14, 15),
        (2, 3),
    )
    return (
        output[:local_len][None],
        outgoing[None],
        total_wq.astype(F32)[None],
        total_wo.astype(F32)[None],
        total_w1.astype(F32)[None],
        total_w2.astype(F32)[None],
        flat[0:2][None],
        flat[2:4][None],
        flat[4:6][None],
        flat[8:10][None],
        flat[6:8][None],
        flat[10 : 10 + extra_rows].reshape(1, -1),
    )


def solution(mesh):
    rows = P("rep", "shard", None)
    matrix = P(None, "shard", None)
    vector = P(None, None, "shard")
    return jax.shard_map(
        local,
        mesh=mesh,
        in_specs=(rows, rows, P("rep"), *([matrix] * 4), *([vector] * 5), P(None, "shard")),
        out_specs=(rows, rows, *([matrix] * 4), *([vector] * 5), P(None, "shard")),
        check_vma=False,
    )
```

```python
import functools
import math

import jax
import jax.numpy as jnp
from jax import lax
from jax.experimental import pallas as pl
from jax.experimental.pallas import tpu as pltpu
from jax.sharding import PartitionSpec as P

HEADS = 16
LEN = 1025
EPSILON = 1e-06
F32 = jnp.float32
BF16 = jnp.bfloat16
MESH = pl.DeviceIdType.MESH
HOP = 2
VMEM = pl.BlockSpec(memory_space=pltpu.VMEM)


def norm_parts(hidden):
    center = hidden - jnp.mean(hidden, axis=-1, keepdims=True)
    inverse = lax.rsqrt(jnp.mean(center * center, axis=-1, keepdims=True) + EPSILON)
    return (center * inverse, inverse)


def norm_backward(incoming, normed, inverse, gain):
    scaled = incoming * gain
    return inverse * (
        scaled
        - jnp.mean(scaled, axis=-1, keepdims=True)
        - normed * jnp.mean(scaled * normed, axis=-1, keepdims=True)
    )


def gelu_pair(values):
    cumulative = 0.5 * (1.0 + lax.erf(values * 0.7071067811865476))
    slope = cumulative + values * jnp.exp(-0.5 * values * values) * 0.3989422804014327
    return (values * cumulative, slope)


def plain_dot(left, right):
    return jnp.dot(left, right, preferred_element_type=F32)


def row_dot(left, right):
    return lax.dot_general(left, right, (((0,), (0,)), ((), ())), preferred_element_type=F32)


def back_dot(left, right):
    return lax.dot_general(left, right, (((1,), (1,)), ((), ())), preferred_element_type=F32)


def head_parts(size, width):
    lane = lax.broadcasted_iota(jnp.int32, (1, width), 1)
    return [
        ((lane >= size * number) & (lane < size * (number + 1))) for number in range(width // size)
    ]


def column_sum(values):
    return jnp.sum(values, axis=0, keepdims=True)


def partner(me, step, count):
    other, bit = me, 1
    while bit < count:
        other = other + ((step // bit) % 2) * (1 - 2 * ((me // bit) % 2)) * bit
        bit *= 2
    return other


def spot(index, rows):
    return pl.ds(pl.multiple_of(index * rows, math.gcd(rows, 1024)), rows)


def greet(me, count, others=()):
    barrier = pltpu.get_barrier_semaphore()
    for step in range(1, count):
        pl.semaphore_signal(
            barrier, 1, device_id={"shard": partner(me, step, count)}, device_id_type=MESH
        )
    for other in others:
        pl.semaphore_signal(barrier, 1, device_id={"rep": other}, device_id_type=MESH)
    pl.semaphore_wait(barrier, count - 1 + len(others))


def post(source, target, sems, kind, step, where):
    return pltpu.make_async_remote_copy(
        source,
        target,
        sems[0].at[kind, step],
        sems[1].at[kind, step],
        device_id=where,
        device_id_type=MESH,
    )


def score(queries, keys, live):
    return jnp.where(live, back_dot(queries, keys), -1e30)


def attend_rows(size, here, live, project, mixed, stat):
    owned = mixed.shape[1]
    width = min(max(128, size), owned)
    factor = 1.0 / math.sqrt(size)
    for pair in range(owned // width):
        columns = slice(pair * width, (pair + 1) * width)
        queries = project[here, columns]
        keys = project[:, owned + pair * width : owned + (pair + 1) * width]
        values = project[:, 2 * owned + pair * width : 2 * owned + (pair + 1) * width]
        out = jnp.zeros(queries.shape, F32)
        for number, part in enumerate(head_parts(size, width)):
            own = (jnp.where(part, queries, 0) * factor).astype(BF16)
            scores = score(own, keys, live)
            top = jnp.max(scores, axis=-1, keepdims=True)
            power = jnp.exp(scores - top)
            total = jnp.sum(power, axis=-1, keepdims=True)
            product = plain_dot(power.astype(BF16), values) * (1.0 / total)
            out = jnp.where(part, product, out)
            place = pair * (width // size) + number
            stat[here, place : place + 1] = top + jnp.log(total)
        mixed[here, columns] = out.astype(BF16)


def attend_rows_back(size, here, live, project, mixed, stat, grad, joined, dk, dv, between):
    owned = mixed.shape[1]
    width = min(max(128, size), owned)
    factor = 1.0 / math.sqrt(size)
    for pair in range(owned // width):
        columns = slice(pair * width, (pair + 1) * width)
        queries = project[here, columns]
        keys = project[:, owned + pair * width : owned + (pair + 1) * width]
        values = project[:, 2 * owned + pair * width : 2 * owned + (pair + 1) * width]
        grads = grad[:, columns]
        overlap = grads.astype(F32) * mixed[here, columns].astype(F32)
        turned_q = jnp.transpose(queries.astype(F32) * factor).astype(BF16)
        turned_g = jnp.transpose(grads.astype(F32)).astype(BF16)
        dq = jnp.zeros(queries.shape, F32)
        for number, part in enumerate(head_parts(size, width)):
            place = pair * (width // size) + number
            own_q = (jnp.where(part, queries, 0) * factor).astype(BF16)
            own_g = jnp.where(part, grads, 0).astype(BF16)
            weights = jnp.exp(score(own_q, keys, live) - stat[here, place : place + 1])
            delta = jnp.sum(jnp.where(part, overlap, 0), axis=-1, keepdims=True)
            slope = (weights * (back_dot(own_g, values) - delta)).astype(BF16)
            span = slice(place * size, (place + 1) * size)
            inner = slice(number * size, (number + 1) * size)
            dk[span, :] += plain_dot(turned_q[inner], slope)
            dv[span, :] += plain_dot(turned_g[inner], weights.astype(BF16))
            dq = jnp.where(part, plain_dot(slope, keys), dq)
            between(place)
        joined[here, columns] = (dq * factor).astype(BF16)


class Gather:
    def __init__(self, array, rows, me, count, sems, kind):
        self.array, self.rows, self.me, self.count = array, rows, me, count
        self.sems, self.kind, self.square = sems, kind, count == 4
        self.steps = (1, 2) if self.square else tuple(range(1, count))
        self.half = array.shape[1] // 2

    def direct(self, owner, step):
        block = self.array.at[spot(owner, self.rows)]
        where = {"shard": partner(self.me, step, self.count)}
        return post(block, block, self.sems, self.kind, step, where)

    def relay(self, owner, step):
        columns = pl.ds((step - 1) * self.half, self.half)
        block = self.array.at[spot(owner, self.rows), columns]
        where = {"shard": partner(self.me, 3 - step, self.count)}
        return post(block, block, self.sems, self.kind + 1, step, where)

    def start(self):
        for step in self.steps:
            self.direct(self.me, step).start()

    def arrive(self, step):
        if not self.square:

            @pl.when(step > 0)
            def _():
                self.direct(partner(self.me, step, self.count), step).wait_recv()

            return

        @pl.when(step == 1)
        def _():
            for near in (1, 2):
                owner = partner(self.me, near, 4)
                self.direct(owner, near).wait_recv()
                self.relay(owner, near).start()

        @pl.when(step == 3)
        def _():
            for near in (1, 2):
                self.relay(partner(self.me, 3, 4), near).wait_recv()

    def finish(self):
        for step in self.steps:
            self.direct(self.me, step).wait_send()
            if self.square:
                self.relay(partner(self.me, step, 4), step).wait_send()


class Scatter:
    def __init__(self, part, landed, via, me, count, sems, kind):
        self.part, self.landed, self.via, self.me, self.count = part, landed, via, me, count
        self.sems, self.kind, self.square = sems, kind, count == 4
        self.steps = (1, 2) if self.square else tuple(range(1, count))
        self.half = part.shape[2] // 2

    def direct(self, step, side=0):
        source, target = self.part.at[step - 1], self.landed.at[step - 1]
        if self.square:
            columns = pl.ds(side * self.half, self.half)
            source, target = source.at[:, columns], target.at[:, columns]
        where = {"shard": partner(self.me, step, self.count)}
        return post(source, target, self.sems, self.kind + 2 * side, step, where)

    def early(self, near):
        return post(
            self.part.at[2, :, pl.ds((near - 1) * self.half, self.half)],
            self.via.at[near - 1],
            self.sems,
            self.kind + 1,
            near,
            {"shard": partner(self.me, near, 4)},
        )

    def send(self, step, value, ready=True):
        if not self.square:
            self.part[step - 1] = value.astype(BF16)
            self.direct(step).start()
            return
        self.part[step - 1] = value.astype(BF16)

        @pl.when(step == 3)
        def _():
            for near in (1, 2):
                self.early(near).start()

        for near in (1, 2):

            @pl.when(step == near)
            def _():
                self.direct(near, near - 1).start()
                if ready:
                    side = 2 - near
                    self.combine(near, value[:, side * self.half : (side + 1) * self.half])

    def combine(self, near, value=None):
        side = 2 - near
        columns = slice(side * self.half, (side + 1) * self.half)
        if value is None:
            value = self.part[near - 1, :, columns].astype(F32)
        self.early(3 - near).wait_recv()
        self.part[near - 1, :, columns] = (value + self.via[side].astype(F32)).astype(BF16)
        self.direct(near, side).start()

    def total(self, value):
        for step in self.steps:
            for side in range(2 if self.square else 1):
                self.direct(step, side).wait_recv()
            value += self.landed[step - 1].astype(F32)
        return value

    def finish(self):
        for step in self.steps:
            for side in range(2 if self.square else 1):
                self.direct(step, side).wait_send()
            if self.square:
                self.early(step).wait_send()


def passing(count, rows, model):
    slots = 2 if count == 4 else count - 1
    return [
        ((count - 1, rows, model), BF16),
        ((slots, rows, model), BF16),
        ((2, rows, model // 2), BF16),
    ]


class Chain:
    def __init__(self, rep, chips, parts, own, sems, kind, scratch, total):
        self.parts, self.own, self.sems, self.kind = parts, own, sems, kind
        self.up, self.cross, self.held = scratch
        self.total = total
        core, chip = rep % 2, rep // 2
        side = chip // (chips // 2)
        self.core, self.last = core, chips // 2 - 1
        self.depth = side * (chips - 1 - chip) + (1 - side) * chip
        ahead = 1 - 2 * side
        self.inner = {"rep": (chip + ahead) * 2 + core}
        self.outer = {"rep": (chip - ahead) * 2 + core}
        self.mate = {"rep": rep + 1 - 2 * core}

    def copy(self, which, part):
        where = (self.inner, self.inner, self.outer, self.mate)[which]
        final = self.total(self.core, part)
        source = self.held.at[part] if which < 2 else final
        target = (self.up.at[part], self.cross.at[part], final, final)[which]
        return post(source, target, self.sems, self.kind + which, part, where)

    def reduce(self, part):
        depth, last = self.depth, self.last
        value = self.own(part)

        @pl.when(depth == 0)
        def _():
            self.held[part] = value.astype(BF16)

        if last > 0:

            @pl.when(depth > 0)
            def _():
                self.copy(0, part).wait_recv()
                self.held[part] = (value + self.up[part].astype(F32)).astype(BF16)

            @pl.when(depth < last)
            def _():
                self.copy(0, part).start()

        @pl.when(depth == last)
        def _():
            self.copy(1, part).start()

    def result(self, part):
        depth, last = self.depth, self.last

        @pl.when(depth == last)
        def _():
            self.copy(1, part).wait_recv()
            both = self.held[part].astype(F32) + self.cross[part].astype(F32)
            self.total(self.core, part)[...] = both.astype(BF16)

        if last > 0:

            @pl.when(depth < last)
            def _():
                self.copy(2, part).wait_recv()

            @pl.when(depth > 0)
            def _():
                self.copy(2, part).start()

        self.copy(3, part).start()

    def within(self, part, act):
        @pl.when((part >= 0) & (part < self.parts))
        def _():
            act(part)

    def step(self, turn):
        self.within(turn - HOP * self.depth, self.reduce)
        self.within(turn - HOP * (2 * self.last + 1 - self.depth), self.result)

    def turns(self):
        return self.parts + HOP * (2 * self.last + 1)

    def finish(self):
        def closing(part, carry):
            if self.last > 0:

                @pl.when(self.depth < self.last)
                def _():
                    self.copy(0, part).wait_send()

                @pl.when(self.depth > 0)
                def _():
                    self.copy(2, part).wait_send()

            @pl.when(self.depth == self.last)
            def _():
                self.copy(1, part).wait_send()

            final = self.total(1 - self.core, part)
            self.copy(3, part).wait_send()
            post(final, final, self.sems, self.kind + 3, part, self.mate).wait_recv()
            return carry

        lax.fori_loop(0, self.parts, closing, 0)


def loop(count, act):
    def body(part, carry):
        act(part)
        return carry

    lax.fori_loop(0, count, body, 0)


def lead(chain):
    @pl.when(chain.depth == 0)
    def _():
        loop(chain.parts, chain.reduce)


def follow(chain, lag=2):
    @pl.when(chain.depth == 0)
    def _():
        loop(chain.parts, chain.result)

    if chain.last > 0:

        @pl.when(chain.depth > 0)
        def _():
            def both(part):
                chain.within(part, chain.reduce)
                chain.within(part - lag, chain.result)

            loop(chain.parts + lag, both)


def live_keys(local_len, rows, total):
    place = lax.broadcasted_iota(jnp.int32, (1, total), 1)
    inner = place % rows
    return (inner < local_len) & ((place // rows) * local_len + inner < LEN)


def early_kernel(
    count,
    size,
    local_len,
    move,
    raw_ref,
    raw_up,
    live_ref,
    rows_ref,
    wqkv_ref,
    wo_ref,
    w1_ref,
    w2_ref,
    tok_ref,
    up_ref,
    first_all,
    wq,
    project,
    mixed,
    stat,
    attn,
    pk_all,
    middle_out,
    middle_grad,
    branch,
    pair_w1,
    pair_w2,
    grad_bias,
    sums,
    fc2_all,
    w1c,
    part,
    landed,
    via,
    grad_w1,
    grad_w2,
    other_w1,
    other_w2,
    second_all,
    pre_in,
    act,
    part_two,
    landed_two,
    via_two,
    own,
    bias_ref,
    fc1_bias,
    send_sem,
    recv_sem,
):
    sems = (send_sem, recv_sem)
    me, rep = lax.axis_index("shard"), lax.axis_index("rep")
    core = rep % 2
    mate = rep + 1 - 2 * core
    rows, model = tok_ref.shape
    owned = rows_ref.shape[1]
    pk_ref = rows_ref.at[0:8]
    units = w1c.shape[1]
    half = owned // 2
    greet(me, count, (mate,))

    own_cols = pl.ds(pl.multiple_of(me * owned, 128), owned)
    own_rows = pl.ds(pl.multiple_of(me * owned, 16), owned)
    mine = spot(me, rows)
    ours = pl.ds(pl.multiple_of(core * half, 16), half)
    pk_all[:, own_cols] = pk_ref[...]
    PK, FIRST, FC2, W1, WQ, FQ, F1, SUM = 0, 1, 3, 5, 6, 9, 10, 11
    gather_first = Gather(first_all, rows, me, count, sems, FIRST)
    gather_fc2 = Gather(fc2_all, rows, me, count, sems, FC2)
    scatter = Scatter(part, landed, via, me, count, sems, SUM)
    sent = []

    def block(source):
        return pl.ds(pl.multiple_of(source * owned + core * half, 16), half)

    def push(source, target, kind, step):
        copy = post(source, target, sems, kind, step, {"shard": partner(me, step, count)})
        copy.start()
        sent.append(copy)

    def hand(target, kind, step):
        copy = post(target, target, sems, kind, step, {"rep": mate})
        copy.start()
        sent.append(copy)
        return copy

    for step in range(1, count):
        push(pk_ref, pk_all.at[:, own_cols], PK, step)
    for step in range(1, count):
        other = partner(me, step, count)
        for third in range(3):
            push(
                wqkv_ref.at[ours, pl.ds(pl.multiple_of(third * model + other * owned, 128), owned)],
                wq.at[block(me), third * owned : (third + 1) * owned],
                WQ + third,
                step,
            )
    own[...] = jnp.zeros_like(own)
    own[0:local_len, :] = raw_ref[...].astype(F32)
    tok_ref[...] = own[...].astype(BF16)
    hidden = tok_ref[...].astype(F32)
    normed, _ = norm_parts(hidden)
    for step in range(1, count):
        other = pl.ds(pl.multiple_of(partner(me, step, count) * owned, 128), owned)
        post(pk_ref, pk_all.at[:, other], sems, PK, step, {"rep": mate}).wait_recv()
    first_all[mine, :] = (normed * pk_all[0:1] + pk_all[2:3]).astype(BF16)
    gather_first.start()
    for third in range(3):
        columns = pl.ds(pl.multiple_of(third * model + me * owned, 128), owned)
        wq[own_rows, third * owned : (third + 1) * owned] = wqkv_ref[:, columns]
    bias_ref[...] = jnp.zeros_like(bias_ref)
    bias_ref[:, 0:owned] = rows_ref[8:9, :]
    bias_ref[:, 2 * owned :] = rows_ref[9:10, :]
    for number in range(units // owned):
        fc1_bias[:, number * owned : (number + 1) * owned] = rows_ref[10 + number : 11 + number, :]
    move.need(6)
    w1c[own_rows, :] = w1_ref[:, pl.ds(pl.multiple_of(me * units, 128), units)]
    own[0:local_len, :] = raw_up[...].astype(F32)
    place = lax.broadcasted_iota(jnp.int32, (rows, 1), 0)
    valid = (place < local_len) & (me * local_len + place < LEN) & (live_ref[0:1, 0:1] > 0.5)
    up_ref[...] = jnp.where(valid, own[...], 0.0).astype(BF16)
    fc2_all[mine, :] = (up_ref[...].astype(F32) * pk_all[5:6]).astype(BF16)

    handed = []
    for step in range(1, count):
        other = partner(me, step, count)
        for third in range(3):
            columns = slice(third * owned, (third + 1) * owned)
            post(
                wq.at[block(other), columns],
                wq.at[block(other), columns],
                sems,
                WQ + third,
                step,
                {"rep": mate},
            ).wait_recv()
        handed.append(hand(wq.at[block(other)], FQ, step))
    for copy in handed:
        copy.wait_recv()

    def shifting(step):
        other = partner(me, step, count)
        columns = pl.ds(pl.multiple_of(other * units, 128), units)
        where = {"shard": other}
        return post(w1_ref.at[ours, columns], w1c.at[block(me)], sems, W1, step, where)

    def projecting(step, carry):
        there = spot(partner(me, step, count), rows)

        gather_first.arrive(step)

        @pl.when(step == min(1, count - 1))
        def _():
            for other in range(1, count):
                shifting(other).start()

        project[there, :] = (plain_dot(first_all[there, :], wq[...]) + bias_ref[...]).astype(BF16)
        return carry

    lax.fori_loop(0, count, projecting, 0)
    move.need(5)
    move.leave(2, 3, 4)
    gather_fc2.start()
    live = live_keys(local_len, rows, project.shape[0])

    def attending(turn, carry):
        step = count - 1 - turn
        there = spot(partner(me, step, count), rows)

        if count == 4:

            @pl.when(turn == count - 2)
            def _():
                gather_fc2.arrive(1)

        attend_rows(size, there, live, project, mixed, stat)
        result = plain_dot(mixed[there, :], wo_ref[...])

        @pl.when(step > 0)
        def _():
            scatter.send(step, result)

        @pl.when(step == 0)
        def _():
            attn[...] = result

        return carry

    lax.fori_loop(0, count, attending, 0)
    move.leave(5, 6)
    for step in range(1, count):
        other = block(partner(me, step, count))
        post(w1c.at[other], w1c.at[other], sems, W1, step, {"rep": mate}).wait_recv()
        handed.append(hand(w1c.at[other], F1, step))
    attn[...] = scatter.total(attn[...] + pk_all[6:7])
    move.leave(7)
    tile = min(256, units)
    SECOND, SUM, PAIR = 14, 16, 19
    gather = Gather(second_all, rows, me, count, sems, SECOND)
    scatter_two = Scatter(part_two, landed_two, via_two, me, count, sems, SUM)
    middle = tok_ref[...].astype(F32) + pk_all[4:5] * attn[...]
    middle_out[...] = middle
    normed, _ = norm_parts(middle)
    second_all[mine, :] = (normed * pk_all[1:2] + pk_all[3:4]).astype(BF16)
    gather.start()
    grad_bias[...] = jnp.zeros_like(grad_bias)
    for copy in handed[count - 1 :]:
        copy.wait_recv()

    def feeding(step, carry):
        there = spot(partner(me, step, count), rows)

        gather.arrive(step)
        if count == 4:

            @pl.when(step > 1)
            def _():
                gather_fc2.arrive(step)

        else:
            gather_fc2.arrive(step)

        def tiles(number, inner):
            columns = pl.ds(pl.multiple_of(number * tile, 128), tile)
            pre = plain_dot(second_all[there, :], w1c[:, columns]) + fc1_bias[:, columns]
            value, slope = gelu_pair(pre)
            act[there, columns] = value.astype(BF16)
            back = back_dot(
                fc2_all[there, :], w2_ref[pl.ds(pl.multiple_of(number * tile, 16), tile), :]
            )
            back = back * slope
            grad_bias[:, columns] += column_sum(back)
            pre_in[there, columns] = back.astype(BF16)
            return inner

        lax.fori_loop(0, units // tile, tiles, 0)
        result = back_dot(pre_in[there, :], w1c[...])

        @pl.when(step > 0)
        def _():
            scatter_two.send(step, result, False)

        @pl.when(step == 0)
        def _():
            own[...] = result

        return carry

    move.need(7)
    move.leave(9)
    lax.fori_loop(0, count, feeding, 0)

    def branching(step, carry):
        there = spot(partner(me, step, count), rows)
        branch[step] = plain_dot(act[there, :], w2_ref[...]).astype(BF16)
        return carry

    lax.fori_loop(0, count, branching, 0)
    move.leave(11)
    if count == 4:
        for near in (1, 2):
            scatter_two.combine(near)

    def weighing_two(number, carry):
        columns = pl.ds(pl.multiple_of(number * tile, 128), tile)
        here = pl.ds(pl.multiple_of(lax.rem(number, halves) * tile, 16), tile)
        grad_w2[number // halves, here, :] = row_dot(act[:, columns], fc2_all[...]).astype(BF16)
        return carry

    halves = units // tile // 2
    lax.fori_loop(0, units // tile, weighing_two, 0)
    copies = [post(grad_w2.at[1 - core], other_w2, sems, PAIR, 0, {"rep": mate})]
    copies[0].start()

    def weighing_one(number, carry):
        columns = pl.ds(pl.multiple_of(number * owned, 128), owned)
        product = row_dot(second_all[:, columns], pre_in[...]).astype(BF16)
        grad_w1[0, number] = product[:half]
        grad_w1[1, number] = product[half:]
        return carry

    lax.fori_loop(0, count, weighing_one, 0)
    copies.append(post(grad_w1.at[1 - core], other_w1, sems, PAIR, 1, {"rep": mate}))
    copies[1].start()
    for copy in copies:
        copy.wait()
    pair_w2[...] = (grad_w2[core].astype(F32) + other_w2[...].astype(F32)).astype(BF16)
    pair_w1[...] = (grad_w1[core].astype(F32) + other_w1[...].astype(F32)).astype(BF16)

    move.leave(0, 1, 12, 13)
    result = scatter_two.total(own[...])
    normed, inverse = norm_parts(middle_out[...])
    sums[0:1, :] = column_sum(result * normed)
    sums[1:2, :] = column_sum(result)
    middle_grad[...] = up_ref[...].astype(F32) + norm_backward(
        result, normed, inverse, pk_all[1:2]
    )
    for done in (gather_first, gather_fc2, gather, scatter, scatter_two):
        done.finish()
    for step in range(1, count):
        shifting(step).wait_send()
    for copy in sent:
        copy.wait_send()


def last_kernel(
    count,
    size,
    local_len,
    move,
    tok_ref,
    up_ref,
    attn_ref,
    pk_ref,
    middle_ref,
    middle_grad,
    branch,
    sums_in,
    first_all,
    project,
    mixed,
    stat,
    wo_ref,
    wq,
    pair_w1,
    pair_w2,
    bias_rows,
    output,
    outgoing,
    total_w1,
    total_w2,
    total_wq,
    total_wo,
    flat,
    attn_all,
    joined,
    dk,
    dv,
    part,
    landed,
    via,
    part_two,
    landed_two,
    via_two,
    own,
    swapped_w1,
    up_w1,
    cross_w1,
    held_w1,
    up_w2,
    cross_w2,
    held_w2,
    swapped_wq,
    up_wq,
    cross_wq,
    held_wq,
    up_wo,
    cross_wo,
    held_wo,
    grad_wq,
    grad_wo,
    other_wq,
    other_wo,
    sums,
    sums_by,
    flat_by,
    send_sem,
    recv_sem,
):
    sems = (send_sem, recv_sem)
    me = lax.axis_index("shard")
    rows, model = tok_ref.shape
    total, owned = mixed.shape
    mine = spot(me, rows)
    GRAD, BRANCH, SUM, SWAP1, SWAPQ, PAIR, SMALL, FLAT = 0, 2, 5, 8, 9, 10, 11, 12
    gather = Gather(attn_all, rows, me, count, sems, GRAD)
    scatter = Scatter(part, landed, via, me, count, sems, SUM)
    scatter_two = Scatter(part_two, landed_two, via_two, me, count, sems, BRANCH)
    rep, reps = lax.axis_index("rep"), lax.axis_size("rep")
    core = rep % 2
    mate = rep + 1 - 2 * core
    half = owned // 2
    heads = owned // size
    greet(me, count, [lax.rem(rep + other, reps) for other in range(1, reps)])

    def summed_w2(number):
        return pair_w2[number].astype(F32)

    def summed_w1(part):
        number = part // 2
        step = partner(me, number, count)

        @pl.when((step > 0) & (lax.rem(part, 2) == 0))
        def _():
            post(
                swapped_w1.at[number], swapped_w1.at[number], sems, SWAP1, step, {"shard": me}
            ).wait_recv()

        return swapped_w1[number, spot(lax.rem(part, 2), half // 2)].astype(F32)

    def summed_wq(number):
        source, third = number // 3, lax.rem(number, 3)
        step = partner(me, source, count)

        @pl.when((step > 0) & (third == 0))
        def _():
            post(
                swapped_wq.at[source], swapped_wq.at[source], sems, SWAPQ, step, {"shard": me}
            ).wait_recv()

        columns = pl.ds(pl.multiple_of(third * owned, 128), owned)
        return swapped_wq[source, :, columns].astype(F32)

    def summed_wo(number):
        return grad_wo[core, number].astype(F32) + other_wo[number].astype(F32)

    def place_w1(part, number):
        rows_here = spot(part * 2 + lax.rem(number, 2), half // 2)
        return total_w1.at[rows_here, pl.ds(pl.multiple_of((number // 2) * units, 128), units)]

    def place_w2(part, number):
        return total_w2.at[spot(part * 2 * count + number, pair_w2.shape[1])]

    def place_wq(part, number):
        column = lax.rem(number, 3) * model + (number // 3) * owned
        rows_here = pl.ds(pl.multiple_of(part * half, 16), half)
        return total_wq.at[rows_here, pl.ds(pl.multiple_of(column, 128), owned)]

    def place_wo(part, number):
        return total_wo.at[spot(part * count + number, half // count)]

    units = pair_w1.shape[2]
    line = functools.partial(Chain, rep, reps // 2)
    chain_w2 = line(2 * count, summed_w2, sems, 13, (up_w2, cross_w2, held_w2), place_w2)
    chain_w1 = line(2 * count, summed_w1, sems, 17, (up_w1, cross_w1, held_w1), place_w1)
    chain_wo = line(count, summed_wo, sems, 21, (up_wo, cross_wo, held_wo), place_wo)
    chain_wq = line(3 * count, summed_wq, sems, 25, (up_wq, cross_wq, held_wq), place_wq)

    def feed_turn(turn):
        chain_w2.step(turn)

    attn_grad = middle_grad[...] * pk_ref[4:5]
    attn_all[mine, :] = attn_grad.astype(BF16)
    gather.start()
    sent = []
    def swapping(step):
        other = partner(me, step, count)
        return post(pair_w1.at[other], swapped_w1.at[me], sems, SWAP1, step, {"shard": other})

    sums[1:2, :] = sums_in[0:1, :]
    sums[3:4, :] = sums_in[1:2, :]
    dk[...] = jnp.zeros_like(dk)
    dv[...] = jnp.zeros_like(dv)
    live = live_keys(local_len, rows, total)

    def attending(step, carry):
        there = spot(partner(me, step, count), rows)

        gather.arrive(step)

        @pl.when(step == min(1, count - 1))
        def _():
            for other in range(1, count):
                swapping(other).start()

        @pl.when(step == min(2, count - 1))
        def _():
            for other in range(count - 1, 0, -1):
                scatter_two.send(other, branch[other].astype(F32), False)

        grad = back_dot(attn_all[there, :], wo_ref[...]).astype(BF16)
        attend_rows_back(
            size,
            there,
            live,
            project,
            mixed,
            stat,
            grad,
            joined,
            dk,
            dv,
            lambda head: feed_turn(step * heads + head),
        )
        return carry

    move.need(6, 9, 10, 11, 12, 14, 15)
    swapped_w1[me] = pair_w1[me]
    lax.fori_loop(0, count, attending, 0)
    move.need(0, 1, 2, 4, 8, 13)
    lead(chain_w1)
    turned = jnp.transpose(dv[...])
    joined[:, owned : 2 * owned] = jnp.transpose(dk[...]).astype(BF16)
    joined[:, 2 * owned :] = turned.astype(BF16)
    flat[8:9, :] = column_sum(joined[:, 0:owned].astype(F32))
    flat[9:10, :] = column_sum(turned)

    product = row_dot(mixed[...], attn_all[...]).astype(BF16)
    grad_wo[0] = product[:half].reshape(grad_wo.shape[1:])
    grad_wo[1] = product[half:].reshape(grad_wo.shape[1:])
    pair_wo = post(grad_wo.at[1 - core], other_wo, sems, PAIR, 0, {"rep": mate})
    pair_wo.start()

    def weighing(number, carry):
        columns = pl.ds(pl.multiple_of(number * owned, 128), owned)
        product = row_dot(first_all[:, columns], joined[...]).astype(BF16)
        grad_wq[0, number] = product[:half]
        grad_wq[1, number] = product[half:]
        return carry

    lax.fori_loop(0, count, weighing, 0)
    pair_wq = post(grad_wq.at[1 - core], other_wq, sems, PAIR, 1, {"rep": mate})
    pair_wq.start()
    def returning(turn, carry):
        step = count - 1 - turn
        there = spot(partner(me, step, count), rows)
        result = back_dot(joined[there, :], wq[...])

        @pl.when(step > 0)
        def _():
            scatter.send(step, result, False)

        @pl.when(step == 0)
        def _():
            own[...] = result

        return carry

    lax.fori_loop(0, count, returning, 0)
    pair_wo.wait()
    pair_wq.wait()
    grad_wq[core] = (grad_wq[core].astype(F32) + other_wq[...].astype(F32)).astype(BF16)
    for step in range(1, count):
        other = partner(me, step, count)
        copy = post(
            grad_wq.at[core, other], swapped_wq.at[me], sems, SWAPQ, step, {"shard": other}
        )
        copy.start()
        sent.append(copy)
    swapped_wq[me] = grad_wq[core, me]
    lax.fori_loop(count * heads, chain_w2.turns(), lambda turn, carry: (feed_turn(turn), carry)[1], 0)
    lead(chain_wo)
    follow(chain_w1)
    if count == 4:
        for near in (1, 2):
            scatter.combine(near)
            scatter_two.combine(near)
    lead(chain_wq)
    follow(chain_wo)
    for step in range(1, count):
        swapping(step).wait_send()
    sums[4:5, :] = column_sum(middle_grad[...] * attn_ref[...])
    sums[6:7, :] = column_sum(middle_grad[...] * pk_ref[4:5])
    sums[7:8, :] = column_sum(up_ref[...].astype(F32) * pk_ref[5:6])
    result = scatter.total(own[...])
    normed, inverse = norm_parts(tok_ref[...].astype(F32))
    sums[0:1, :] = column_sum(result * normed)
    sums[2:3, :] = column_sum(result)
    own[...] = middle_grad[...] + norm_backward(result, normed, inverse, pk_ref[0:1])
    outgoing[...] = own[0:local_len, :]
    result = branch[0].astype(F32) + pk_ref[7:8]
    result = scatter_two.total(result)
    output[...] = (middle_ref[...] + pk_ref[5:6] * result).astype(BF16)
    sums[5:6, :] = column_sum(up_ref[...].astype(F32) * result)

    own_cols = pl.ds(pl.multiple_of(me * owned, 128), owned)
    for step in range(1, count):
        other = partner(me, step, count)
        copy = post(
            sums.at[:, pl.ds(pl.multiple_of(other * owned, 128), owned)],
            sums_by.at[me],
            sems,
            SMALL,
            step,
            {"shard": other},
        )
        copy.start()
        sent.append(copy)
    sums_by[me] = sums[:, own_cols]

    for done in (chain_w2, chain_w1):
        done.finish()
    move.leave(2, 3)
    follow(chain_wq)
    for step in range(1, count):
        other = partner(me, step, count)
        post(sums_by.at[other], sums_by.at[other], sems, SMALL, step, {"shard": me}).wait_recv()
    flat[0:8, :] = functools.reduce(lambda left, right: left + right, [sums_by[i] for i in range(count)])
    flat[10:, :] = jnp.zeros((flat.shape[0] - 10, owned), F32)
    for number in range(bias_rows.shape[1] // owned):
        flat[10 + number : 11 + number, :] = bias_rows[:, number * owned : (number + 1) * owned]
    flat_by[rep] = flat[...]
    for step in range(1, reps):
        copy = post(
            flat, flat_by.at[rep], sems, FLAT, step, {"rep": lax.rem(rep + step, reps)}
        )
        copy.start()
        sent.append(copy)
    for copy in sent:
        copy.wait_send()
    for step in range(1, reps):
        source = lax.rem(rep + reps - step, reps)
        post(flat_by.at[source], flat_by.at[source], sems, FLAT, step, {"shard": me}).wait_recv()
    flat[...] = functools.reduce(lambda left, right: left + right, [flat_by[i] for i in range(reps)])
    for done in (gather, scatter, scatter_two, chain_wo, chain_wq):
        done.finish()


class Mover:
    def __init__(self, fetches, stores, sem):
        self.fetches, self.stores, self.sem, self.left = fetches, stores, sem, []
        self.order = {key: place for place, key in enumerate([*fetches, *stores])}
        for key in fetches:
            self.copy(key).start()

    def copy(self, key):
        pair = self.fetches[key] if key in self.fetches else self.stores[key]
        return pltpu.make_async_copy(*pair, self.sem.at[self.order[key]])

    def need(self, *numbers):
        for number in numbers:
            self.copy(("in", number)).wait()

    def leave(self, *numbers):
        for number in numbers:
            self.copy(("out", number)).start()
            self.left.append(("out", number))

    def finish(self):
        for key in self.left:
            self.copy(key).wait()


def moving(body, ins, outs, late, early, *refs):
    refs = list(refs)
    extra = len(late) + len(early) + 1
    held = refs[len(refs) - extra :]
    fetches, stores = {}, {}
    for number, buffer in zip(late, held):
        fetches["in", number] = (refs[number], buffer)
        refs[number] = buffer
    for number, buffer in zip(early, held[len(late) :]):
        stores["out", number] = (buffer, refs[ins + number])
        refs[ins + number] = buffer
    move = Mover(fetches, stores, held[-1])
    body(move, *refs[: len(refs) - extra])
    move.finish()


def call(body, number, name, operands, outs, scratch, kinds, flops, late, early):
    far = pl.BlockSpec(memory_space=pl.ANY)
    buffers = [(operands[i].shape, operands[i].dtype) for i in late] + [outs[i] for i in early]
    return pl.pallas_call(
        functools.partial(moving, body, len(operands), len(outs), late, early),
        in_specs=[far if i in late else VMEM for i in range(len(operands))],
        out_specs=[far if i in early else VMEM for i in range(len(outs))],
        out_shape=[jax.ShapeDtypeStruct(*out) for out in outs],
        scratch_shapes=[pltpu.VMEM(*item) for item in scratch]
        + [pltpu.SemaphoreType.DMA(kinds), pltpu.SemaphoreType.DMA(kinds)]
        + [pltpu.VMEM(*item) for item in buffers]
        + [pltpu.SemaphoreType.DMA((len(buffers),))],
        compiler_params=pltpu.CompilerParams(
            collective_id=number, has_side_effects=True, vmem_limit_bytes=60 * 1024 * 1024
        ),
        cost_estimate=pl.CostEstimate(flops=flops, bytes_accessed=2**24, transcendentals=2**22),
        name=name,
    )(*operands)


def local(
    tokens,
    cotangent,
    slot_live,
    w_qkv,
    w_out,
    w_fc1,
    w_fc2,
    norm_gain,
    norm_bias,
    layer_scale,
    qv_bias,
    proj_bias,
    fc1_bias,
):
    count = lax.axis_size("shard")
    me = lax.axis_index("shard")
    _, local_len, model = tokens.shape
    owned = model // count
    units = w_fc2.shape[1]
    hidden_units = w_fc1.shape[2]
    size = model // HEADS
    rows = -(-local_len // 16) * 16
    extra = rows - local_len
    total = rows * count

    alive = jnp.broadcast_to((slot_live > 0).astype(F32)[:, None], (1, 128))
    extra_rows = units // owned
    flat_rows = -(-(10 + extra_rows) // 8) * 8
    lines = [norm_gain[0], norm_bias[0], layer_scale[0], proj_bias[0], qv_bias[0]]
    lines.append(fc1_bias.reshape(extra_rows, owned))
    lines.append(jnp.zeros((flat_rows - 10 - extra_rows, owned), BF16))
    packed = jnp.concatenate(lines, axis=0).astype(F32)

    big = (total, model)
    small = (rows, model)
    half = owned // 2
    wide_one = (count, half, units)
    wide_two = (2 * count, units // 4 // count, model)
    wide_half = (2 * count, half // 2, units)
    wide_q = (count, half, 3 * owned)
    wide_o = (count, half // count, model)
    (
        tok,
        up,
        first_all,
        wq,
        project,
        mixed,
        stat,
        attn,
        pk_all,
        middle,
        middle_grad,
        branch,
        pair_w1,
        pair_w2,
        grad_b1,
        sums,
    ) = call(
        functools.partial(early_kernel, count, size, local_len),
        0,
        "forward_and_feed",
        (
            tokens[0],
            cotangent[0],
            alive,
            packed,
            w_qkv[0],
            w_out[0],
            w_fc1[0],
            w_fc2[0],
        ),
        (
            (small, BF16),
            (small, BF16),
            (big, BF16),
            ((model, 3 * owned), BF16),
            ((total, 3 * owned), BF16),
            ((total, owned), BF16),
            ((total, 128), F32),
            (small, F32),
            ((8, model), F32),
            (small, F32),
            (small, F32),
            ((count, *small), BF16),
            (wide_one, BF16),
            ((units // 2, model), BF16),
            ((1, units), F32),
            ((8, model), F32),
        ),
        (
            (big, BF16),
            ((model, units), BF16),
            *passing(count, *small),
            ((2, *wide_one), BF16),
            ((2, units // 2, model), BF16),
            (wide_one, BF16),
            ((units // 2, model), BF16),
            (big, BF16),
            ((total, units), BF16),
            ((total, units), BF16),
            *passing(count, *small),
            (small, F32),
            ((1, 3 * owned), F32),
            ((1, units), F32),
        ),
        (20, count),
        2 * 10**10,
        (5, 6, 7),
        (0, 1, 2, 3, 4, 5, 6, 7, 9, 11, 12, 13),
    )
    reps = lax.axis_size("rep")
    output, outgoing, total_w1, total_w2, total_wq, total_wo, flat = call(
        functools.partial(last_kernel, count, size, local_len),
        2,
        "attend_backward",
        (
            tok,
            up,
            attn,
            pk_all,
            middle,
            middle_grad,
            branch,
            sums,
            first_all,
            project,
            mixed,
            stat,
            w_out[0],
            wq,
            pair_w1,
            pair_w2.reshape(wide_two),
            grad_b1,
        ),
        (
            (small, BF16),
            ((local_len, model), F32),
            ((owned, hidden_units), BF16),
            ((units, model), BF16),
            ((owned, 3 * model), BF16),
            ((owned, model), BF16),
            ((flat_rows, owned), F32),
        ),
        (
            (big, BF16),
            ((total, 3 * owned), BF16),
            ((owned, total), F32),
            ((owned, total), F32),
            *passing(count, *small),
            *passing(count, *small),
            (small, F32),
            (wide_one, BF16),
            *([(wide_half, BF16)] * 3),
            *([(wide_two, BF16)] * 3),
            (wide_q, BF16),
            *([((3 * count, half, owned), BF16)] * 3),
            *([(wide_o, BF16)] * 3),
            ((2, *wide_q), BF16),
            ((2, *wide_o), BF16),
            (wide_q, BF16),
            (wide_o, BF16),
            ((8, model), F32),
            ((count, 8, owned), F32),
            ((reps, flat_rows, owned), F32),
        ),
        (29, max(3 * count, reps)),
        10**10,
        (0, 1, 2, 4, 6, 8, 9, 10, 11, 12, 13, 14, 15),
        (2, 3),
    )
    return (
        output[:local_len][None],
        outgoing[None],
        total_wq.astype(F32)[None],
        total_wo.astype(F32)[None],
        total_w1.astype(F32)[None],
        total_w2.astype(F32)[None],
        flat[0:2][None],
        flat[2:4][None],
        flat[4:6][None],
        flat[8:10][None],
        flat[6:8][None],
        flat[10 : 10 + extra_rows].reshape(1, -1),
    )


def solution(mesh):
    rows = P("rep", "shard", None)
    matrix = P(None, "shard", None)
    vector = P(None, None, "shard")
    return jax.shard_map(
        local,
        mesh=mesh,
        in_specs=(rows, rows, P("rep"), *([matrix] * 4), *([vector] * 5), P(None, "shard")),
        out_specs=(rows, rows, *([matrix] * 4), *([vector] * 5), P(None, "shard")),
        check_vma=False,
    )
```
